32 devices in a mesh: wide: 8 (over z, y), narrow: 4 (over x, core).
Axes of the slice: x: 2, y: 2, z: 4, core: 2. Of those that a mesh axis runs over, the one named last changes fastest.
Arguments:
- latents: bfloat16 [8192, 128], P(('wide', 'narrow')), may hold values from -40 to 40
- targets: int32 [8192], P(('wide', 'narrow')), may hold values from 0 to 8191, as said below
- embed_weight: bfloat16 [128, 3072], replicated, may hold values from -4 to 4
- mod_shift: float32 [3072], replicated, may hold values from -3 to 3
- mod_scale: float32 [3072], replicated, may hold values from -0.5 to 0.5
- qkv_weight: bfloat16 [3, 3072, 2048], P(None, 'wide', 'narrow'), may hold values from -0.109375 to 0.109375
- out_weight: bfloat16 [3072, 2048], P('wide', 'narrow'), may hold values from -0.75 to 0.75
- mod_gate: float32 [3072], replicated, may hold values from 2 to 6
- block_list: int32 [64, 8], P('wide'), may hold values from 0 to 15, as said below
- block_count: int32 [64], P('wide'), may hold values from 1 to 8, as said below
Outputs:
- mixed: bfloat16 [8192, 3072], P(('wide', 'narrow'))
The draws below stay inside these ranges and needn't reach their ends.
Inputs may be any that keep to these rules, and one draw needn't show every extreme that they name: `targets`: A permutation of the positions. Raster row r goes to position p with p // 256 and r // 256 equal modulo 1024 // 256; of every aligned block of 256 raster rows exactly 32 go to each tile p // 1024. `block_list`: key block b holds tile positions b * 512 to b * 512 + 511. Slot 0 holds the block containing the query block; the slots below block_count hold distinct blocks whose tile b * 512 // 1024 is within two of the query block's tile; the later slots repeat slot 0. `block_count`: some row of every draw uses all 8 slots.
All inputs are finite; a program needn't handle non-finite values.
Results may differ from the reference program's by a relative error of at most 0.015.
Values may be sent and summed in bfloat16 or wider, within the bound.
No kernel may reach another device: no remote copies, remote signals or barrier semaphores. Data moves between devices by JAX's collectives and lax.ppermute only.
A program may use at most 192 MiB of HBM per device.

```python
import math
import jax
import jax.numpy as jnp
from jax import lax

D = 3072
PATCH = 128
HEADS = 32
HEAD = 64
NB = 8
KB = 512
QB = 128
TILE = 1024
TOK_DEV = 256
HD = 2048
HEAD_GROUPS = 4
TOKENS = 8192
QBLOCKS = 64


def draw_latents(key, part):
    first_key, second_key = jax.random.split(key)
    entries = jax.random.truncated_normal(first_key, -4.0, 4.0, (TOKENS, PATCH), jnp.float32)
    row_scale = jnp.exp(jax.random.uniform(second_key, (TOKENS, 1), jnp.float32, 0.0, math.log(10.0)))
    return (entries * row_scale).astype(jnp.bfloat16)


def draw_embed_weight(key, part):
    first_key, second_key = jax.random.split(key)
    entries = jax.random.truncated_normal(first_key, -4.0, 4.0, (PATCH, D), jnp.float32)
    column_scale = jnp.exp(jax.random.uniform(second_key, (1, D), jnp.float32, 0.0, math.log(10.0)))
    return (0.1 * entries * column_scale).astype(jnp.bfloat16)


def shuffled_rows(key, block_total, row_total):
    raw = jax.random.randint(key, (block_total, row_total), 0, 1 << 16) * row_total + jnp.arange(row_total)[None, :]
    return jnp.argsort(raw, axis=1).astype(jnp.int32)


def draw_targets(key, part):
    wide_count = TOKENS // TILE
    narrow_count = TILE // TOK_DEV
    per_peer = TOK_DEV // wide_count
    block_total = wide_count * narrow_count
    send_key, recv_key = jax.random.split(jax.random.fold_in(key, 3))
    send_perm = shuffled_rows(send_key, block_total, TOK_DEV)
    recv_perm = shuffled_rows(recv_key, block_total, TOK_DEV)
    block_ids = jnp.arange(block_total, dtype=jnp.int32)[:, None]
    source_wide = block_ids // narrow_count
    narrow_ids = block_ids % narrow_count
    dest_wide = send_perm // per_peer
    slot_ids = send_perm % per_peer
    receiver = dest_wide * narrow_count + narrow_ids
    local_pos = recv_perm[receiver, source_wide * per_peer + slot_ids]
    target_pos = dest_wide * TILE + narrow_ids * TOK_DEV + local_pos
    return target_pos.reshape(TOKENS).astype(jnp.int32)


def mask_tables(key):
    wide_count = TOKENS // TILE
    per_tile = TILE // QB
    keys_per_tile = TILE // KB
    cand_count = 5 * keys_per_tile
    score_key, count_key = jax.random.split(jax.random.fold_in(key, 7))
    query_ids = jnp.arange(QBLOCKS, dtype=jnp.int32)[:, None]
    tile_ids = query_ids // per_tile
    own_block = query_ids * QB // KB
    candidates = jnp.arange(cand_count, dtype=jnp.int32)[None, :]
    cand_tile = tile_ids - 2 + candidates // keys_per_tile
    cand_block = cand_tile * keys_per_tile + candidates % keys_per_tile
    valid = (cand_tile >= 0) & (cand_tile < wide_count) & (cand_block != own_block)
    raw = jax.random.randint(score_key, (QBLOCKS, cand_count), 0, 1 << 16) * cand_count + candidates
    ranked = jnp.where(valid, raw, -1 - candidates)
    top_values, top_index = lax.top_k(ranked, NB - 1)
    picked = jnp.take_along_axis(jnp.broadcast_to(cand_block, (QBLOCKS, cand_count)), top_index, axis=1)
    valid_count = jnp.sum(valid.astype(jnp.int32), axis=1)
    drawn = jax.random.randint(count_key, (QBLOCKS,), 1, NB + 1)
    counts = jnp.minimum(drawn, valid_count + 1)
    forced = wide_count // 2 * per_tile
    counts = jnp.where(jnp.arange(QBLOCKS) == forced, NB, counts)
    full_list = jnp.concatenate([own_block, picked], axis=1)
    slot_ids = jnp.arange(NB, dtype=jnp.int32)[None, :]
    full_list = jnp.where(slot_ids < counts[:, None], full_list, own_block)
    return (full_list.astype(jnp.int32), counts.astype(jnp.int32))


def draw_block_list(key, part):
    return mask_tables(key)[0]


def draw_block_count(key, part):
    return mask_tables(key)[1]


def block_scale(key, extent, pieces, low, high):
    gain = 1.0
    for position, blocks in pieces:
        draws = jax.random.uniform(jax.random.fold_in(jax.random.fold_in(key, 6), position), (blocks,), jnp.float32, low / len(pieces), high / len(pieces))
        gain = gain * jnp.repeat(jnp.exp(draws), extent[position] // blocks).reshape((-1,) + (1,) * (len(extent) - 1 - position))
    return gain


def noise(own_key, extent, spread, bound, cuts=(), held_as=jnp.bfloat16):
    result = jax.random.normal(own_key, extent, jnp.float32) * spread
    if len(cuts) > 0:
        result = block_scale(own_key, extent, cuts, -0.22, 0.18) * result
    return jnp.clip(result, min=-bound, max=bound).astype(held_as)


def setup_inputs(seed: int = 0) -> dict:
    keys = jax.random.split(jax.random.key(seed), 11)
    latents = draw_latents(jax.random.fold_in(keys[10], 71), 0)
    targets = draw_targets(jax.random.fold_in(keys[10], 71), 0)
    embed_weight = draw_embed_weight(jax.random.fold_in(keys[10], 71), 0)
    mod_shift = noise(keys[3], (D,), 0.5, 3.0, (), jnp.float32)
    mod_scale = jnp.clip(jax.random.uniform(keys[4], (D,), jnp.float32, -0.5, 0.5), -0.5, 0.5)
    qkv_weight = noise(keys[5], (3, D, HD), D ** -0.5, 0.109375, ((1, 8), (2, 4)))
    out_weight = noise(keys[6], (D, HD), HEAD ** -0.5, 0.75, ((0, 8), (1, 4)))
    mod_gate = jnp.clip(jax.random.uniform(keys[7], (D,), jnp.float32, 2.0, 6.0), 2.0, 6.0)
    block_list = draw_block_list(jax.random.fold_in(keys[10], 71), 0)
    block_count = draw_block_count(jax.random.fold_in(keys[10], 71), 0)
    return dict(latents=latents, targets=targets, embed_weight=embed_weight, mod_shift=mod_shift, mod_scale=mod_scale, qkv_weight=qkv_weight, out_weight=out_weight, mod_gate=mod_gate, block_list=block_list, block_count=block_count)


EPSILON = 1e-06

def layer_norm(inputs):
    row_mean = lax.optimization_barrier(jnp.mean(inputs, axis=-1, keepdims=True))
    centred = inputs - row_mean
    variance = lax.optimization_barrier(jnp.mean(centred * centred, axis=-1, keepdims=True))
    return centred * lax.rsqrt(variance + EPSILON)

def head_norm(inputs):
    shaped = inputs.reshape(inputs.shape[0], -1, HEAD)
    return layer_norm(shaped).reshape(inputs.shape)

def reference(latents, targets, embed_weight, mod_shift, mod_scale, qkv_weight, out_weight, mod_gate, block_list, block_count):
    tiled = jnp.zeros_like(latents).at[targets].set(latents)
    tiles_all = tiled.reshape(TOKENS // TILE, TILE, PATCH)
    weights_full = qkv_weight.astype(jnp.float32)

    def project(tile_patches):
        embedded = jnp.dot(tile_patches, embed_weight, preferred_element_type=jnp.float32)
        normed = (layer_norm(embedded) * (1.0 + mod_scale) + mod_shift).astype(jnp.bfloat16)
        projected = jnp.einsum('td,cdh->cth', normed.astype(jnp.float32), weights_full)
        queries = head_norm(projected[0]).astype(jnp.bfloat16)
        keys_tile = head_norm(projected[1]).astype(jnp.bfloat16)
        values_tile = projected[2].astype(jnp.bfloat16)
        return (queries, keys_tile, values_tile)
    queries, keys_all, values_all = lax.map(project, tiles_all)
    queries = queries.reshape(TOKENS, HD)
    keys_all = keys_all.reshape(TOKENS, HD)
    values_all = values_all.reshape(TOKENS, HD)
    out_groups = out_weight.astype(jnp.float32).reshape(D, HEAD_GROUPS, HD // HEAD_GROUPS)

    def attend(inputs):
        block_index, blocks, live_count = inputs
        query_rows = lax.dynamic_slice_in_dim(queries, block_index * QB, QB, 0).reshape(QB, HEADS, HEAD)
        starts = (blocks * KB).astype(jnp.int32)
        key_rows = jax.vmap(lambda start_row: lax.dynamic_slice_in_dim(keys_all, start_row, KB, 0))(starts)
        value_rows = jax.vmap(lambda start_row: lax.dynamic_slice_in_dim(values_all, start_row, KB, 0))(starts)
        key_rows = key_rows.reshape(NB * KB, HEADS, HEAD).astype(jnp.float32)
        value_rows = value_rows.reshape(NB * KB, HEADS, HEAD).astype(jnp.float32)
        scores = jnp.einsum('qhd,khd->hqk', query_rows.astype(jnp.float32), key_rows) * 0.125
        live_mask = (jnp.arange(NB * KB) // KB < live_count).astype(jnp.float32)
        weighted = jnp.exp(scores) * live_mask
        probs = (weighted / lax.optimization_barrier(jnp.sum(weighted, axis=-1, keepdims=True))).astype(jnp.bfloat16)
        attended = jnp.einsum('hqk,khd->qhd', probs.astype(jnp.float32), value_rows).astype(jnp.bfloat16)
        grouped = attended.reshape(QB, HEAD_GROUPS, HD // HEAD_GROUPS).astype(jnp.float32)
        partial_value = jnp.einsum('qgc,dgc->gqd', grouped, out_groups)
        partial_value = lax.optimization_barrier(partial_value.astype(jnp.bfloat16)).astype(jnp.float32)
        return (mod_gate * lax.optimization_barrier(jnp.sum(partial_value, axis=0))).astype(jnp.bfloat16)
    mixed = lax.map(attend, (jnp.arange(QBLOCKS, dtype=jnp.int32), block_list, block_count))
    return mixed.reshape(TOKENS, D)
```

```python
import functools

import jax
import jax.numpy as jnp
from jax import lax
from jax.experimental import pallas as pl
from jax.experimental.pallas import tpu as pltpu
from jax.sharding import PartitionSpec as P

HEAD = 64
NB = 8
KB = 512
QB = 128
REACH = 2
SPAN = 2 * REACH + 1
EPSILON = 1e-06

f32 = jnp.float32
bf16 = jnp.bfloat16
NT = (((1,), (1,)), ((), ()))
TN = (((0,), (0,)), ((), ()))


def ntdot(a, b):
    return lax.dot_general(a, b, NT, preferred_element_type=f32)


def whole_spec():
    return pl.BlockSpec(memory_space=pltpu.VMEM)


def split3(value):
    high = value.astype(bf16)
    rest = value - high.astype(f32)
    mid = rest.astype(bf16)
    low = (rest - mid.astype(f32)).astype(bf16)
    return high, mid, low


def gram_kernel(embed_ref, gram_ref):
    embed = embed_ref[...].astype(f32)
    width = embed.shape[1]
    centred = embed - jnp.mean(embed, axis=1, keepdims=True)
    gram = lax.dot_general(
        centred, centred, NT, preferred_element_type=f32, precision=lax.Precision.HIGHEST
    ) * (1.0 / width)
    for index, term in enumerate(split3(gram)):
        gram_ref[index] = term


def prep_kernel(
    wide_count,
    embed_ref,
    slice_ref,
    scale_ref,
    shift_ref,
    qkv_ref,
    latents_ref,
    row_ref,
    column_ref,
    weight_ref,
    bias_ref,
    rows_ref,
    place_ref,
):
    row_mean = jnp.mean(embed_ref[...].astype(f32), axis=1, keepdims=True)
    factor = (slice_ref[...].astype(f32) - row_mean) * (1.0 + scale_ref[...])
    high, mid, _ = split3(factor)
    shift_terms = split3(jnp.broadcast_to(shift_ref[...], (16, shift_ref.shape[1])))
    heads_width = qkv_ref.shape[2]
    for part in range(3):
        piece = qkv_ref[part]
        product = jnp.dot(high, piece, preferred_element_type=f32) + jnp.dot(
            mid, piece, preferred_element_type=f32
        )
        turned = product.T
        if part < 2:
            grouped = turned.reshape(heads_width // HEAD, HEAD, turned.shape[1])
            grouped = grouped - jnp.mean(grouped, axis=1, keepdims=True)
            turned = grouped.reshape(turned.shape)
        weight_ref[part * heads_width : (part + 1) * heads_width, :] = turned.astype(bf16)
        bias = (
            jnp.dot(shift_terms[0], piece, preferred_element_type=f32)
            + jnp.dot(shift_terms[1], piece, preferred_element_type=f32)
            + jnp.dot(shift_terms[2], piece, preferred_element_type=f32)
        )
        bias_ref[part : part + 1, :] = bias[0:1, :].astype(bf16)
    row_total = latents_ref.shape[0]
    share = row_total // wide_count
    across = row_ref[...]
    down = column_ref[...]
    slot_across = jnp.sum((down < across).astype(f32), axis=0, keepdims=True)
    slot_down = jnp.sum((across < down).astype(f32), axis=1, keepdims=True)
    local = (down % row_total).astype(f32)
    count = rows_ref.shape[1]
    latents = latents_ref[...]
    for receiver in range(wide_count):
        first = (receiver - REACH) * share
        wanted = lax.broadcasted_iota(jnp.int32, (count, row_total), 0)
        chosen = (slot_across == (wanted + first).astype(f32)) & (wanted < SPAN * share)
        rows_ref[receiver] = jnp.dot(
            chosen.astype(bf16), latents, preferred_element_type=f32
        ).astype(bf16)
        lane = lax.broadcasted_iota(jnp.int32, (row_total, 128), 1)
        mine = (slot_down == (lane + receiver * share).astype(f32)) & (lane < share)
        spots = jnp.sum(jnp.where(mine, local, 0.0), axis=0, keepdims=True)
        place_ref[receiver] = jnp.broadcast_to(spots, (16, 128)).astype(bf16)


def attend_kernel(
    row_total,
    tile_size,
    order_ref,
    starts_ref,
    counts_ref,
    patches_ref,
    spots_ref,
    weight_ref,
    bias_ref,
    value_bias_ref,
    gram_ref,
    out_ref,
    keys_ref,
    values_ref,
    queries_ref,
    twin_ref,
    total_ref,
):
    heads_width = out_ref.shape[1]
    local_heads = heads_width // HEAD
    pairs = heads_width // 128
    narrow_count = tile_size // row_total

    def doubled(part):
        weight = weight_ref[part * heads_width : (part + 1) * heads_width, :]
        return jnp.concatenate([weight, weight], axis=1)

    def centred_bias(part):
        bias = bias_ref[part * heads_width : (part + 1) * heads_width, :]
        grouped = bias.reshape(local_heads, HEAD, 1)
        grouped = grouped - jnp.mean(grouped, axis=1, keepdims=True)
        return grouped.reshape(heads_width, 1)

    def unit_heads(turned, bias):
        grouped = (turned + bias).reshape(local_heads, HEAD, turned.shape[1])
        square = jnp.mean(grouped * grouped, axis=1, keepdims=True)
        return (grouped * lax.rsqrt(square + EPSILON)).reshape(turned.shape)

    gram_top = jnp.concatenate([gram_ref[0], gram_ref[1]], axis=0)
    key_bias = centred_bias(1)

    def project(step, carry):
        tile = step // narrow_count
        block = step % narrow_count
        place = order_ref[block] * row_total
        rows = patches_ref[block, pl.ds(pl.multiple_of(tile * row_total, row_total), row_total), :]
        wide_rows = rows.astype(f32)
        image = jnp.dot(
            jnp.concatenate([rows, rows], axis=1), gram_top, preferred_element_type=f32
        ) + jnp.dot(rows, gram_ref[2], preferred_element_type=f32)
        variance = jnp.sum(image * wide_rows, axis=1, keepdims=True)
        scaled = wide_rows * lax.rsqrt(variance + EPSILON)
        high = scaled.astype(bf16)
        low = (scaled - high.astype(f32)).astype(bf16)
        both = jnp.concatenate([high, low], axis=1)
        at = pl.multiple_of(tile * tile_size + place, row_total)
        keys_ref[:, pl.ds(at, row_total)] = unit_heads(ntdot(doubled(1), both), key_bias).astype(bf16)
        values_ref[pl.ds(at, row_total), :] = (
            ntdot(both, doubled(2)) + value_bias_ref[...]
        ).astype(bf16)

        @pl.when(tile == REACH)
        def _():
            wanted = lax.broadcasted_iota(jnp.int32, (row_total, row_total), 0).astype(f32)
            chosen = (spots_ref[block].astype(f32) == wanted).astype(bf16)
            placed = jnp.dot(chosen, both, preferred_element_type=f32).astype(bf16)
            turned = unit_heads(ntdot(doubled(0), placed), centred_bias(0)).astype(bf16) * 0.125
            queries_ref[pl.ds(pl.multiple_of(place, row_total), row_total), :] = (
                turned.astype(f32).T.astype(bf16)
            )

        return carry

    lax.fori_loop(0, SPAN * narrow_count, project, 0)

    left = lax.broadcasted_iota(jnp.int32, (QB, 128), 1) < HEAD
    ones = jnp.ones((KB, 128), bf16)

    def attend(block, carry):
        at = pl.multiple_of(block * QB, QB)
        for pair in range(pairs):
            rows = queries_ref[pl.ds(at, QB), pair * 128 : (pair + 1) * 128]
            twin_ref[pair, 0:QB, :] = jnp.where(left, rows, jnp.zeros_like(rows))
            twin_ref[pair, QB : 2 * QB, :] = jnp.where(left, jnp.zeros_like(rows), rows)
            total_ref[pair] = jnp.zeros_like(total_ref[pair])

        def visit(slot, inner):
            start = pl.multiple_of(starts_ref[block * NB + slot], KB)
            for pair in range(pairs):
                columns = slice(pair * 128, (pair + 1) * 128)
                scores = jnp.dot(
                    twin_ref[pair],
                    keys_ref[columns, pl.ds(start, KB)],
                    preferred_element_type=f32,
                )
                weights = jnp.exp(scores).astype(bf16)
                side = jnp.concatenate([values_ref[pl.ds(start, KB), columns], ones], axis=1)
                total_ref[pair] += jnp.dot(weights, side, preferred_element_type=f32)
            return inner

        lax.fori_loop(0, counts_ref[block], visit, 0)
        for pair in range(pairs):
            both = total_ref[pair, :, 0:128] / total_ref[pair, :, 128:256]
            out_ref[pl.ds(at, QB), pair * 128 : (pair + 1) * 128] = jnp.where(
                left, both[0:QB], both[QB : 2 * QB]
            ).astype(bf16)
        return carry

    lax.fori_loop(0, tile_size // QB, attend, 0)


def output_kernel(narrow_count, attended_ref, weight_ref, gate_ref, out_ref):
    rows = weight_ref.shape[0] // narrow_count
    width = weight_ref.shape[1]
    total = None
    for index in range(narrow_count):
        term = ntdot(
            attended_ref[:, index * width : (index + 1) * width],
            weight_ref[index * rows : (index + 1) * rows, :],
        )
        total = term if total is None else total + term
    out_ref[...] = (total * gate_ref[...]).astype(bf16)


def flip(block, axis, bit):
    devices = range(lax.axis_size(axis))
    return lax.ppermute(block, axis, [(i, i ^ bit) for i in devices])


def per_device(
    latents,
    targets,
    embed_weight,
    mod_shift,
    mod_scale,
    qkv_weight,
    out_weight,
    mod_gate,
    block_list,
    block_count,
):
    row_total, patch = latents.shape
    width = embed_weight.shape[1]
    wide_count = lax.axis_size("wide")
    narrow_count = lax.axis_size("narrow")
    wide_index = lax.axis_index("wide")
    narrow_index = lax.axis_index("narrow")
    tile_size = row_total * narrow_count
    depth, heads_width = qkv_weight.shape[1:]
    share = row_total // wide_count
    count = -(-SPAN * share // 16) * 16
    piece = 3 * heads_width // wide_count

    out_all = lax.all_gather(out_weight, ("wide", "narrow"), axis=0, tiled=True)

    first = wide_index * depth
    weight_part, bias_part, rows, spots = pl.pallas_call(
        functools.partial(prep_kernel, wide_count),
        out_shape=(
            jax.ShapeDtypeStruct((3 * heads_width, patch), bf16),
            jax.ShapeDtypeStruct((3, heads_width), bf16),
            jax.ShapeDtypeStruct((wide_count, count, patch), bf16),
            jax.ShapeDtypeStruct((wide_count, 16, 128), bf16),
        ),
        in_specs=[whole_spec()] * 8,
        out_specs=(whole_spec(),) * 4,
        name="prep",
    )(
        embed_weight,
        lax.dynamic_slice_in_dim(embed_weight, first, depth, 1),
        lax.dynamic_slice_in_dim(mod_scale, first, depth, 0).reshape(1, depth),
        lax.dynamic_slice_in_dim(mod_shift, first, depth, 0).reshape(1, depth),
        qkv_weight,
        latents,
        targets.reshape(1, row_total),
        targets.reshape(row_total, 1),
    )
    gram = pl.pallas_call(
        gram_kernel,
        out_shape=jax.ShapeDtypeStruct((3, patch, patch), bf16),
        in_specs=[whole_spec()],
        out_specs=whole_spec(),
        name="gram",
    )(embed_weight)

    bias_rows = -(-piece // 128)
    bias_block = jnp.pad(bias_part.reshape(wide_count, piece), ((0, 0), (0, 16 * 128 - piece)))
    payload = jnp.concatenate(
        [weight_part.reshape(wide_count, piece, patch), bias_block.reshape(wide_count, 16, 128), rows, spots],
        axis=1,
    )
    arrived = lax.all_to_all(payload, "wide", split_axis=0, concat_axis=0, tiled=True)

    summed = jnp.sum(arrived[:, : piece + 16].astype(f32), axis=0).astype(bf16)
    spread = jnp.broadcast_to(summed[None], (wide_count,) + summed.shape)
    near = arrived[:, piece + 16 : piece + 16 + SPAN * share]
    near = near.reshape(wide_count, SPAN, share, patch).transpose(1, 0, 2, 3)
    near = near.reshape(SPAN * row_total, patch)
    mine = arrived[:, piece + 16 + count, :share].reshape(-1)
    mine = jnp.pad(mine, (0, 16 * 128 - row_total)).reshape(16, 128)
    group = jnp.concatenate([near, mine], axis=0)[None]
    order = [0]
    bits = [1 << k for k in range(1, narrow_count.bit_length() - 1)] + [1]
    for bit in bits:
        group = jnp.concatenate([group, flip(group, "narrow", bit)], axis=0)
        order = order + [index ^ bit for index in order]
    everything = lax.all_to_all(spread, "wide", split_axis=0, concat_axis=0, tiled=True)
    weight_all = everything[:, :piece].reshape(3 * heads_width, patch)
    bias_all = everything[:, piece:].reshape(wide_count, 16 * 128)[:, :piece].reshape(-1).astype(f32)

    order_ids = jnp.bitwise_xor(jnp.array(order, jnp.int32), narrow_index)
    starts = (block_list * KB - (wide_index - REACH) * tile_size).reshape(-1)
    spots_all = group[:, SPAN * row_total :].reshape(narrow_count, 1, 16 * 128)[:, :, :row_total]
    smem = pl.BlockSpec(memory_space=pltpu.SMEM)
    attended = pl.pallas_call(
        functools.partial(attend_kernel, row_total, tile_size),
        out_shape=jax.ShapeDtypeStruct((tile_size, heads_width), bf16),
        in_specs=[smem] * 3 + [whole_spec()] * 6,
        out_specs=whole_spec(),
        scratch_shapes=[
            pltpu.VMEM((heads_width, SPAN * tile_size), bf16),
            pltpu.VMEM((SPAN * tile_size, heads_width), bf16),
            pltpu.VMEM((tile_size, heads_width), bf16),
            pltpu.VMEM((heads_width // 128, 2 * QB, 128), bf16),
            pltpu.VMEM((heads_width // 128, 2 * QB, 256), f32),
        ],
        name="attend",
    )(
        order_ids,
        starts,
        block_count,
        group,
        spots_all,
        weight_all,
        bias_all.reshape(-1, 1),
        bias_all[2 * heads_width :].reshape(1, heads_width),
        gram,
    )

    merged = lax.all_to_all(attended, "narrow", split_axis=0, concat_axis=1, tiled=True)
    out_rows = out_weight.shape[0]
    gate = mod_gate.reshape(1, width)
    if out_rows % 128 == 0:
        return pl.pallas_call(
            functools.partial(output_kernel, narrow_count),
            grid=(wide_count,),
            out_shape=jax.ShapeDtypeStruct((row_total, width), bf16),
            in_specs=[
                pl.BlockSpec((row_total, narrow_count * heads_width), lambda i: (0, 0)),
                pl.BlockSpec((narrow_count * out_rows, heads_width), lambda i: (i, 0)),
                pl.BlockSpec((1, out_rows), lambda i: (0, i)),
            ],
            out_specs=pl.BlockSpec((row_total, out_rows), lambda i: (0, i)),
            name="output",
        )(merged, out_all, gate)
    weights = out_all.reshape(wide_count, narrow_count, out_rows, heads_width)
    product = jnp.einsum(
        "tnk,wnfk->twf",
        merged.reshape(row_total, narrow_count, heads_width),
        weights,
        preferred_element_type=f32,
    )
    return (gate * product.reshape(row_total, width)).astype(bf16)


def solution(mesh):
    in_specs = (
        P(("wide", "narrow"), None),
        P(("wide", "narrow")),
        P(),
        P(),
        P(),
        P(None, "wide", "narrow"),
        P("wide", "narrow"),
        P(),
        P("wide", None),
        P("wide"),
    )
    out_specs = P(("wide", "narrow"), None)
    return jax.shard_map(
        per_device, mesh=mesh, in_specs=in_specs, out_specs=out_specs, check_vma=False
    )
```

```python
import functools

import jax
import jax.numpy as jnp
from jax import lax
from jax.experimental import pallas as pl
from jax.experimental.pallas import tpu as pltpu
from jax.sharding import PartitionSpec as P

HEAD = 64
NB = 8
KB = 512
QB = 128
REACH = 2
SPAN = 2 * REACH + 1
EPSILON = 1e-06

f32 = jnp.float32
bf16 = jnp.bfloat16
NT = (((1,), (1,)), ((), ()))


def ntdot(a, b):
    return lax.dot_general(a, b, NT, preferred_element_type=f32)


def whole_spec():
    return pl.BlockSpec(memory_space=pltpu.VMEM)


def split3(value):
    high = value.astype(bf16)
    rest = value - high.astype(f32)
    mid = rest.astype(bf16)
    low = (rest - mid.astype(f32)).astype(bf16)
    return high, mid, low


def gram_kernel(embed_ref, gram_ref):
    embed = embed_ref[...].astype(f32)
    width = embed.shape[1]
    centred = embed - jnp.mean(embed, axis=1, keepdims=True)
    gram = lax.dot_general(
        centred, centred, NT, preferred_element_type=f32, precision=lax.Precision.HIGHEST
    ) * (1.0 / width)
    for index, term in enumerate(split3(gram)):
        gram_ref[index] = term


def prep_kernel(
    wide_count,
    sliced,
    at_ref,
    embed_ref,
    slice_ref,
    scale_ref,
    shift_ref,
    qkv_ref,
    latents_ref,
    targets_ref,
    *out_refs,
):
    depth, heads_width = qkv_ref.shape[1:]
    patch = embed_ref.shape[0]
    if sliced:
        own, scale, shift = slice_ref[...], scale_ref[...], shift_ref[...]
    else:
        columns = pl.ds(pl.multiple_of(at_ref[0], 128), depth)
        own, scale, shift = embed_ref[:, columns], scale_ref[:, columns], shift_ref[:, columns]
    piece = 3 * heads_width // wide_count
    row_mean = jnp.mean(embed_ref[...].astype(f32), axis=1, keepdims=True)
    factor = (own.astype(f32) - row_mean) * (1.0 + scale)
    stacked = jnp.concatenate([factor, jnp.broadcast_to(shift, (16, depth))], axis=0)
    high, mid, _ = split3(stacked)
    bias_rows = []
    for part in range(3):
        weights = qkv_ref[part]
        product = jnp.dot(high, weights, preferred_element_type=f32) + jnp.dot(
            mid, weights, preferred_element_type=f32
        )
        for chunk in range(heads_width // 128):
            bias_rows.append(product[patch : patch + 1, chunk * 128 : (chunk + 1) * 128])
        turned = product[0:patch].T
        if part < 2:
            grouped = turned.reshape(heads_width // HEAD, HEAD, patch)
            grouped = grouped - jnp.mean(grouped, axis=1, keepdims=True)
            turned = grouped.reshape(turned.shape)
        turned = turned.astype(bf16)
        top = part * heads_width
        if sliced:
            out_refs[0][top : top + heads_width, :] = turned
            continue
        for receiver in range(wide_count):
            low = max(receiver * piece, top)
            end = min((receiver + 1) * piece, top + heads_width)
            if low < end:
                base = receiver * piece
                out_refs[0][receiver, low - base : end - base, :] = turned[low - top : end - top]
    bias_rows.append(jnp.zeros((16 - len(bias_rows), 128), f32))
    bias = jnp.concatenate(bias_rows, axis=0).astype(bf16)
    row_total = latents_ref.shape[0]
    share = row_total // wide_count
    across = targets_ref[...]
    same = lax.broadcasted_iota(jnp.int32, (row_total, row_total), 0) == lax.broadcasted_iota(
        jnp.int32, (row_total, row_total), 1
    )
    down = jnp.sum(jnp.where(same, across.astype(f32), 0.0), axis=1, keepdims=True)
    across = across.astype(f32)
    slot_across = jnp.sum((down < across).astype(f32), axis=0, keepdims=True)
    slot_down = jnp.sum((across < down).astype(f32), axis=1, keepdims=True)
    local = (down.astype(jnp.int32) % row_total).astype(f32)
    count = -(-SPAN * share // 16) * 16
    latents = latents_ref[...]
    wanted = lax.broadcasted_iota(jnp.int32, (count, row_total), 0)
    lane = lax.broadcasted_iota(jnp.int32, (row_total, 128), 1)
    for receiver in range(wide_count):
        first = (receiver - REACH) * share
        chosen = (slot_across == (wanted + first).astype(f32)) & (wanted < SPAN * share)
        rows = jnp.dot(chosen.astype(bf16), latents, preferred_element_type=f32).astype(bf16)
        mine = (slot_down == (lane + receiver * share).astype(f32)) & (lane < share)
        spots = jnp.sum(jnp.where(mine, local, 0.0), axis=0, keepdims=True)
        spots = jnp.broadcast_to(spots, (16, 128)).astype(bf16)
        if sliced:
            out_refs[1][receiver, 0:16, :] = bias
            out_refs[1][receiver, 16 : 16 + count, :] = rows
            out_refs[1][receiver, 16 + count :, :] = spots
        else:
            out_refs[0][receiver, piece : piece + 16, :] = bias
            out_refs[0][receiver, piece + 16 : piece + 16 + count, :] = rows
            out_refs[0][receiver, piece + 16 + count :, :] = spots


def attend_kernel(
    row_total,
    tile_size,
    order_ref,
    starts_ref,
    counts_ref,
    patches_ref,
    weight_ref,
    bias_ref,
    gram_ref,
    out_ref,
    both_ref,
    keys_ref,
    values_ref,
    twin_ref,
    total_ref,
    even_ref,
    odd_ref,
    block_ref,
    first_ref,
):
    heads_width = out_ref.shape[1]
    local_heads = heads_width // HEAD
    pairs = heads_width // 128
    narrow_count = tile_size // row_total
    block_total = tile_size // QB
    chunks = heads_width // 128

    def doubled(part):
        weight = weight_ref[part * heads_width : (part + 1) * heads_width, :]
        return jnp.concatenate([weight, weight], axis=1)

    def centred_bias(part):
        same = lax.broadcasted_iota(jnp.int32, (128, 128), 0) == lax.broadcasted_iota(
            jnp.int32, (128, 128), 1
        )
        pieces = []
        for chunk in range(chunks):
            row = bias_ref[part * chunks + chunk : part * chunks + chunk + 1, :]
            pieces.append(jnp.sum(jnp.where(same, row, 0.0), axis=1, keepdims=True))
        grouped = jnp.concatenate(pieces, axis=0).reshape(local_heads, HEAD, 1)
        grouped = grouped - jnp.mean(grouped, axis=1, keepdims=True)
        return grouped.reshape(heads_width, 1)

    def unit_heads(turned, bias):
        grouped = (turned + bias).reshape(local_heads, HEAD, turned.shape[1])
        square = jnp.mean(grouped * grouped, axis=1, keepdims=True)
        return (grouped * lax.rsqrt(square + EPSILON)).reshape(turned.shape)

    gram_top = jnp.concatenate([gram_ref[0], gram_ref[1]], axis=0)
    gram_low = gram_ref[2]

    def scale(step, carry):
        block = step // SPAN
        tile = step % SPAN
        rows = patches_ref[block, pl.ds(pl.multiple_of(tile * row_total, row_total), row_total), :]
        wide_rows = rows.astype(f32)
        image = jnp.dot(
            jnp.concatenate([rows, rows], axis=1), gram_top, preferred_element_type=f32
        ) + jnp.dot(rows, gram_low, preferred_element_type=f32)
        variance = jnp.sum(image * wide_rows, axis=1, keepdims=True)
        scaled = wide_rows * lax.rsqrt(jnp.maximum(variance, 0.0) + EPSILON)
        high = scaled.astype(bf16)
        at = pl.multiple_of(tile * tile_size + order_ref[block] * row_total, row_total)
        both_ref[pl.ds(at, row_total), 0:128] = high
        both_ref[pl.ds(at, row_total), 128:256] = (scaled - high.astype(f32)).astype(bf16)
        return carry

    lax.fori_loop(0, SPAN * narrow_count, scale, 0, unroll=SPAN)

    key_bias = centred_bias(1)
    key_weight = doubled(1)
    value_weight = doubled(2).astype(f32).T.astype(bf16)
    value_bias = jnp.concatenate(
        [bias_ref[2 * chunks + chunk : 2 * chunks + chunk + 1, :] for chunk in range(chunks)], axis=1
    )

    def project(step, carry):
        at = pl.multiple_of(step * 256, 256)
        both = both_ref[pl.ds(at, 256), :]
        keys_ref[:, pl.ds(at, 256)] = unit_heads(ntdot(key_weight, both), key_bias).astype(bf16)
        values_ref[pl.ds(at, 256), :] = (
            jnp.dot(both, value_weight, preferred_element_type=f32) + value_bias
        ).astype(bf16)
        return carry

    lax.fori_loop(0, SPAN * tile_size // 256, project, 0, unroll=2)

    query_bias = centred_bias(0)
    query_weight = doubled(0)
    left = lax.broadcasted_iota(jnp.int32, (QB, 128), 1) < HEAD
    spot_rows = row_total // 128

    def ask(block, carry):
        place = order_ref[block] * row_total
        spots = jnp.concatenate(
            [
                patches_ref[block, SPAN * row_total + row : SPAN * row_total + row + 1, :]
                for row in range(spot_rows)
            ],
            axis=1,
        )
        wanted = lax.broadcasted_iota(jnp.int32, (row_total, row_total), 0).astype(f32)
        chosen = (spots.astype(f32) == wanted).astype(bf16)
        both = both_ref[pl.ds(pl.multiple_of(REACH * tile_size + place, row_total), row_total), :]
        placed = jnp.dot(chosen, both, preferred_element_type=f32).astype(bf16)
        turned = unit_heads(ntdot(query_weight, placed), query_bias).astype(bf16).astype(f32) * 0.125
        rows = turned.T.astype(bf16)
        for part in range(row_total // QB):
            query = order_ref[block] * (row_total // QB) + part
            for pair in range(pairs):
                piece = rows[part * QB : (part + 1) * QB, pair * 128 : (pair + 1) * 128]
                twin_ref[query, pair, 0:QB, :] = jnp.where(left, piece, jnp.zeros_like(piece))
                twin_ref[query, pair, QB : 2 * QB, :] = jnp.where(left, jnp.zeros_like(piece), piece)
        return carry

    lax.fori_loop(0, narrow_count, ask, 0)

    def listed(block, count):
        total_ref[block] = jnp.zeros_like(total_ref[block])

        def note(slot, inner):
            block_ref[count + slot] = block
            first_ref[count + slot] = starts_ref[block * NB + slot]
            return inner

        lax.fori_loop(0, counts_ref[block], note, 0)
        return count + counts_ref[block]

    steps = lax.fori_loop(0, block_total, listed, 0)
    for extra in range(2):
        block_ref[steps + extra] = block_total
        first_ref[steps + extra] = first_ref[0]

    ones = jnp.ones((KB, 128), bf16)

    def weigh(step, weights_ref):
        start = pl.multiple_of(first_ref[step], KB)
        query = jnp.minimum(block_ref[step], block_total - 1)
        for pair in range(pairs):
            scores = jnp.dot(
                twin_ref[query, pair],
                keys_ref[pair * 128 : (pair + 1) * 128, pl.ds(start, KB)],
                preferred_element_type=f32,
            )
            weights_ref[pair] = jnp.exp(scores).astype(bf16)

    def gather(step, weights_ref):
        start = pl.multiple_of(first_ref[step], KB)
        block = block_ref[step]
        for pair in range(pairs):
            side = jnp.concatenate(
                [values_ref[pl.ds(start, KB), pair * 128 : (pair + 1) * 128], ones], axis=1
            )
            total_ref[block, pair] += jnp.dot(weights_ref[pair], side, preferred_element_type=f32)

    weigh(0, even_ref)

    def visit(twice, carry):
        step = twice * 2
        weigh(step + 1, odd_ref)
        gather(step, even_ref)
        weigh(step + 2, even_ref)
        gather(step + 1, odd_ref)
        return carry

    lax.fori_loop(0, (steps + 1) // 2, visit, 0)

    def finish(block, carry):
        for pair in range(pairs):
            both = total_ref[block, pair, :, 0:128] / total_ref[block, pair, :, 128:256]
            out_ref[pl.ds(pl.multiple_of(block * QB, QB), QB), pair * 128 : (pair + 1) * 128] = (
                jnp.where(left, both[0:QB], both[QB : 2 * QB]).astype(bf16)
            )
        return carry

    lax.fori_loop(0, block_total, finish, 0)


def attend_scratch(row_total, tile_size, heads_width):
    pairs = heads_width // 128
    blocks = tile_size // QB
    return [
        pltpu.VMEM((SPAN * tile_size, 256), bf16),
        pltpu.VMEM((heads_width, SPAN * tile_size), bf16),
        pltpu.VMEM((SPAN * tile_size, heads_width), bf16),
        pltpu.VMEM((blocks, pairs, 2 * QB, 128), bf16),
        pltpu.VMEM((blocks + 1, pairs, 2 * QB, 256), f32),
        pltpu.VMEM((pairs, 2 * QB, KB), bf16),
        pltpu.VMEM((pairs, 2 * QB, KB), bf16),
        pltpu.SMEM((blocks * NB + 2,), jnp.int32),
        pltpu.SMEM((blocks * NB + 2,), jnp.int32),
    ]


def output_kernel(narrow_count, attended_ref, weight_ref, gate_ref, out_ref):
    rows = weight_ref.shape[0] // narrow_count
    width = weight_ref.shape[1]
    total = None
    for index in range(narrow_count):
        term = ntdot(
            attended_ref[:, index * width : (index + 1) * width],
            weight_ref[index * rows : (index + 1) * rows, :],
        )
        total = term if total is None else total + term
    out_ref[...] = (total * gate_ref[...]).astype(bf16)


def flip(block, axis, bit):
    devices = range(lax.axis_size(axis))
    return lax.ppermute(block, axis, [(i, i ^ bit) for i in devices])


def per_device(
    latents,
    targets,
    embed_weight,
    mod_shift,
    mod_scale,
    qkv_weight,
    out_weight,
    mod_gate,
    block_list,
    block_count,
):
    row_total, patch = latents.shape
    width = embed_weight.shape[1]
    wide_count = lax.axis_size("wide")
    narrow_count = lax.axis_size("narrow")
    wide_index = lax.axis_index("wide")
    narrow_index = lax.axis_index("narrow")
    tile_size = row_total * narrow_count
    depth, heads_width = qkv_weight.shape[1:]
    share = row_total // wide_count
    count = -(-SPAN * share // 16) * 16
    piece = 3 * heads_width // wide_count

    out_all = lax.all_gather(out_weight, ("wide", "narrow"), axis=0, tiled=True)

    first = wide_index * depth
    extra = 16 + count + 16
    sliced = depth % 128 != 0 or piece % 16 != 0
    scale = mod_scale.reshape(1, width)
    shift = mod_shift.reshape(1, width)
    own = embed_weight
    if sliced:
        own, scale, shift = (
            lax.dynamic_slice_in_dim(array, first, depth, 1) for array in (own, scale, shift)
        )
        prep_shapes = (
            jax.ShapeDtypeStruct((3 * heads_width, patch), bf16),
            jax.ShapeDtypeStruct((wide_count, extra, patch), bf16),
        )
    else:
        prep_shapes = (jax.ShapeDtypeStruct((wide_count, piece + extra, patch), bf16),)
    smem = pl.BlockSpec(memory_space=pltpu.SMEM)
    prepared = pl.pallas_call(
        functools.partial(prep_kernel, wide_count, sliced),
        out_shape=prep_shapes,
        in_specs=[smem] + [whole_spec()] * 7,
        out_specs=tuple(whole_spec() for _ in prep_shapes),
        name="prep",
    )(
        first.astype(jnp.int32).reshape(1),
        embed_weight,
        own,
        scale,
        shift,
        qkv_weight,
        latents,
        targets.reshape(1, row_total),
    )
    payload = prepared[0]
    if sliced:
        payload = jnp.concatenate(
            [payload.reshape(wide_count, piece, patch), prepared[1]], axis=1
        )
    gram = pl.pallas_call(
        gram_kernel,
        out_shape=jax.ShapeDtypeStruct((3, patch, patch), bf16),
        in_specs=[whole_spec()],
        out_specs=whole_spec(),
        name="gram",
    )(embed_weight)
    arrived = lax.all_to_all(payload, "wide", split_axis=0, concat_axis=0, tiled=True)

    summed = jnp.sum(arrived[:, :piece].astype(f32), axis=0).astype(bf16)
    bias = jnp.sum(arrived[:, piece : piece + 16].astype(f32), axis=0)
    spread = jnp.broadcast_to(summed[None], (wide_count,) + summed.shape)
    near = arrived[:, piece + 16 : piece + 16 + SPAN * share]
    near = near.reshape(wide_count, SPAN, share, patch).transpose(1, 0, 2, 3)
    near = near.reshape(SPAN * row_total, patch)
    mine = arrived[:, piece + 16 + count, :share].reshape(-1)
    mine = jnp.pad(mine, (0, 16 * 128 - row_total)).reshape(16, 128)
    group = jnp.concatenate([near, mine], axis=0)[None]
    order = [0]
    bits = [1 << k for k in range(1, narrow_count.bit_length() - 1)] + [1]
    for bit in bits:
        group = jnp.concatenate([group, flip(group, "narrow", bit)], axis=0)
        order = order + [index ^ bit for index in order]
    everything = lax.all_to_all(spread, "wide", split_axis=0, concat_axis=0, tiled=True)
    weight_all = everything.reshape(3 * heads_width, patch)

    order_ids = jnp.bitwise_xor(jnp.array(order, jnp.int32), narrow_index)
    starts = (block_list * KB - (wide_index - REACH) * tile_size).reshape(-1)
    attended = pl.pallas_call(
        functools.partial(attend_kernel, row_total, tile_size),
        out_shape=jax.ShapeDtypeStruct((tile_size, heads_width), bf16),
        in_specs=[smem] * 3 + [whole_spec()] * 4,
        out_specs=whole_spec(),
        scratch_shapes=attend_scratch(row_total, tile_size, heads_width),
        name="attend",
    )(order_ids, starts, block_count, group, weight_all, bias, gram)

    merged = lax.all_to_all(attended, "narrow", split_axis=0, concat_axis=1, tiled=True)
    out_rows = out_weight.shape[0]
    gate = mod_gate.reshape(1, width)
    if out_rows % 128 == 0:
        return pl.pallas_call(
            functools.partial(output_kernel, narrow_count),
            grid=(wide_count,),
            out_shape=jax.ShapeDtypeStruct((row_total, width), bf16),
            in_specs=[
                pl.BlockSpec((row_total, narrow_count * heads_width), lambda i: (0, 0)),
                pl.BlockSpec((narrow_count * out_rows, heads_width), lambda i: (i, 0)),
                pl.BlockSpec((1, out_rows), lambda i: (0, i)),
            ],
            out_specs=pl.BlockSpec((row_total, out_rows), lambda i: (0, i)),
            name="output",
        )(merged, out_all, gate)
    weights = out_all.reshape(wide_count, narrow_count, out_rows, heads_width)
    product = jnp.einsum(
        "tnk,wnfk->twf",
        merged.reshape(row_total, narrow_count, heads_width),
        weights,
        preferred_element_type=f32,
    )
    return (gate * product.reshape(row_total, width)).astype(bf16)


def solution(mesh):
    in_specs = (
        P(("wide", "narrow"), None),
        P(("wide", "narrow")),
        P(),
        P(),
        P(),
        P(None, "wide", "narrow"),
        P("wide", "narrow"),
        P(),
        P("wide", None),
        P("wide"),
    )
    out_specs = P(("wide", "narrow"), None)
    return jax.shard_map(
        per_device, mesh=mesh, in_specs=in_specs, out_specs=out_specs, check_vma=False
    )
```

```python
import functools

import jax
import jax.numpy as jnp
from jax import lax
from jax.experimental import pallas as pl
from jax.experimental.pallas import tpu as pltpu
from jax.sharding import PartitionSpec as P

HEAD = 64
NB = 8
KB = 512
QB = 128
REACH = 2
SPAN = 2 * REACH + 1
EPSILON = 1e-06
PROJECT_VMEM = 32 << 20
ATTEND_VMEM = 32 << 20
OUTPUT_VMEM = 53 << 20

f32 = jnp.float32
bf16 = jnp.bfloat16
NT = (((1,), (1,)), ((), ()))


def ntdot(a, b):
    return lax.dot_general(a, b, NT, preferred_element_type=f32)


def whole_spec():
    return pl.BlockSpec(memory_space=pltpu.VMEM)


def split3(value):
    high = value.astype(bf16)
    rest = value - high.astype(f32)
    mid = rest.astype(bf16)
    low = (rest - mid.astype(f32)).astype(bf16)
    return high, mid, low


def gram_kernel(embed_ref, gram_ref):
    embed = embed_ref[...].astype(f32)
    width = embed.shape[1]
    centred = embed - jnp.mean(embed, axis=1, keepdims=True)
    gram = lax.dot_general(
        centred, centred, NT, preferred_element_type=f32, precision=lax.Precision.HIGHEST
    ) * (1.0 / width)
    for index, term in enumerate(split3(gram)):
        gram_ref[index] = term


def prep_kernel(
    wide_count,
    sliced,
    at_ref,
    embed_ref,
    slice_ref,
    scale_ref,
    shift_ref,
    qkv_ref,
    latents_ref,
    targets_ref,
    *out_refs,
):
    depth, heads_width = qkv_ref.shape[1:]
    patch = embed_ref.shape[0]
    if sliced:
        own, scale, shift = slice_ref[...], scale_ref[...], shift_ref[...]
    else:
        columns = pl.ds(pl.multiple_of(at_ref[0], 128), depth)
        own, scale, shift = embed_ref[:, columns], scale_ref[:, columns], shift_ref[:, columns]
    piece = 3 * heads_width // wide_count
    row_mean = jnp.mean(embed_ref[...].astype(f32), axis=1, keepdims=True)
    factor = (own.astype(f32) - row_mean) * (1.0 + scale)
    stacked = jnp.concatenate([factor, jnp.broadcast_to(shift, (16, depth))], axis=0)
    high, mid, _ = split3(stacked)
    bias_rows = []
    for part in range(3):
        weights = qkv_ref[part]
        product = jnp.dot(high, weights, preferred_element_type=f32) + jnp.dot(
            mid, weights, preferred_element_type=f32
        )
        for chunk in range(heads_width // 128):
            bias_rows.append(product[patch : patch + 1, chunk * 128 : (chunk + 1) * 128])
        turned = product[0:patch].T
        if part < 2:
            grouped = turned.reshape(heads_width // HEAD, HEAD, patch)
            grouped = grouped - jnp.mean(grouped, axis=1, keepdims=True)
            turned = grouped.reshape(turned.shape)
        turned = turned.astype(bf16)
        top = part * heads_width
        if sliced:
            out_refs[0][top : top + heads_width, :] = turned
            continue
        for receiver in range(wide_count):
            low = max(receiver * piece, top)
            end = min((receiver + 1) * piece, top + heads_width)
            if low < end:
                base = receiver * piece
                out_refs[0][receiver, low - base : end - base, :] = turned[low - top : end - top]
    bias_rows.append(jnp.zeros((16 - len(bias_rows), 128), f32))
    bias = jnp.concatenate(bias_rows, axis=0).astype(bf16)
    row_total = latents_ref.shape[0]
    share = row_total // wide_count
    across = targets_ref[...]
    same = lax.broadcasted_iota(jnp.int32, (row_total, row_total), 0) == lax.broadcasted_iota(
        jnp.int32, (row_total, row_total), 1
    )
    down = jnp.sum(jnp.where(same, across.astype(f32), 0.0), axis=1, keepdims=True)
    across = across.astype(f32)
    slot_across = jnp.sum((down < across).astype(f32), axis=0, keepdims=True)
    slot_down = jnp.sum((across < down).astype(f32), axis=1, keepdims=True)
    local = (down.astype(jnp.int32) % row_total).astype(f32)
    count = -(-SPAN * share // 16) * 16
    latents = latents_ref[...]
    wanted = lax.broadcasted_iota(jnp.int32, (count, row_total), 0)
    lane = lax.broadcasted_iota(jnp.int32, (row_total, 128), 1)
    for receiver in range(wide_count):
        first = (receiver - REACH) * share
        chosen = (slot_across == (wanted + first).astype(f32)) & (wanted < SPAN * share)
        rows = jnp.dot(chosen.astype(bf16), latents, preferred_element_type=f32).astype(bf16)
        mine = (slot_down == (lane + receiver * share).astype(f32)) & (lane < share)
        spots = jnp.sum(jnp.where(mine, local, 0.0), axis=0, keepdims=True)
        spots = jnp.broadcast_to(spots, (16, 128)).astype(bf16)
        if sliced:
            out_refs[1][receiver, 0:16, :] = bias
            out_refs[1][receiver, 16 : 16 + count, :] = rows
            out_refs[1][receiver, 16 + count :, :] = spots
        else:
            out_refs[0][receiver, piece : piece + 16, :] = bias
            out_refs[0][receiver, piece + 16 : piece + 16 + count, :] = rows
            out_refs[0][receiver, piece + 16 + count :, :] = spots


def project_kernel(
    row_total,
    tile_size,
    order_ref,
    patches_ref,
    weight_ref,
    bias_ref,
    gram_ref,
    keys_ref,
    values_ref,
    twin_ref,
    both_ref,
):
    heads_width = keys_ref.shape[0]
    local_heads = heads_width // HEAD
    pairs = heads_width // 128
    narrow_count = tile_size // row_total
    chunks = heads_width // 128

    def doubled(part):
        weight = weight_ref[part * heads_width : (part + 1) * heads_width, :]
        return jnp.concatenate([weight, weight], axis=1)

    def centred_bias(part):
        same = lax.broadcasted_iota(jnp.int32, (128, 128), 0) == lax.broadcasted_iota(
            jnp.int32, (128, 128), 1
        )
        pieces = []
        for chunk in range(chunks):
            row = bias_ref[part * chunks + chunk : part * chunks + chunk + 1, :]
            pieces.append(jnp.sum(jnp.where(same, row, 0.0), axis=1, keepdims=True))
        grouped = jnp.concatenate(pieces, axis=0).reshape(local_heads, HEAD, 1)
        grouped = grouped - jnp.mean(grouped, axis=1, keepdims=True)
        return grouped.reshape(heads_width, 1)

    def unit_heads(turned, bias):
        grouped = (turned + bias).reshape(local_heads, HEAD, turned.shape[1])
        square = jnp.mean(grouped * grouped, axis=1, keepdims=True)
        return (grouped * lax.rsqrt(square + EPSILON)).reshape(turned.shape)

    gram_top = jnp.concatenate([gram_ref[0], gram_ref[1]], axis=0)
    gram_low = gram_ref[2]

    def scale(step, carry):
        block = step // SPAN
        tile = step % SPAN
        rows = patches_ref[block, pl.ds(pl.multiple_of(tile * row_total, row_total), row_total), :]
        wide_rows = rows.astype(f32)
        image = jnp.dot(
            jnp.concatenate([rows, rows], axis=1), gram_top, preferred_element_type=f32
        ) + jnp.dot(rows, gram_low, preferred_element_type=f32)
        variance = jnp.sum(image * wide_rows, axis=1, keepdims=True)
        scaled = wide_rows * lax.rsqrt(jnp.maximum(variance, 0.0) + EPSILON)
        high = scaled.astype(bf16)
        at = pl.multiple_of(tile * tile_size + order_ref[block] * row_total, row_total)
        both_ref[pl.ds(at, row_total), 0:128] = high
        both_ref[pl.ds(at, row_total), 128:256] = (scaled - high.astype(f32)).astype(bf16)
        return carry

    lax.fori_loop(0, SPAN * narrow_count, scale, 0, unroll=SPAN)

    key_bias = centred_bias(1)
    key_weight = doubled(1)
    value_weight = doubled(2).astype(f32).T.astype(bf16)
    value_bias = jnp.concatenate(
        [bias_ref[2 * chunks + chunk : 2 * chunks + chunk + 1, :] for chunk in range(chunks)], axis=1
    )

    def project(step, carry):
        at = pl.multiple_of(step * 256, 256)
        both = both_ref[pl.ds(at, 256), :]
        keys_ref[:, pl.ds(at, 256)] = unit_heads(ntdot(key_weight, both), key_bias).astype(bf16)
        values_ref[pl.ds(at, 256), :] = (
            jnp.dot(both, value_weight, preferred_element_type=f32) + value_bias
        ).astype(bf16)
        return carry

    lax.fori_loop(0, SPAN * tile_size // 256, project, 0, unroll=2)

    query_bias = centred_bias(0)
    query_weight = doubled(0)
    left = lax.broadcasted_iota(jnp.int32, (QB, 128), 1) < HEAD
    spot_rows = row_total // 128

    def ask(block, carry):
        place = order_ref[block] * row_total
        spots = jnp.concatenate(
            [
                patches_ref[block, SPAN * row_total + row : SPAN * row_total + row + 1, :]
                for row in range(spot_rows)
            ],
            axis=1,
        )
        wanted = lax.broadcasted_iota(jnp.int32, (row_total, row_total), 0).astype(f32)
        chosen = (spots.astype(f32) == wanted).astype(bf16)
        both = both_ref[pl.ds(pl.multiple_of(REACH * tile_size + place, row_total), row_total), :]
        placed = jnp.dot(chosen, both, preferred_element_type=f32).astype(bf16)
        turned = unit_heads(ntdot(query_weight, placed), query_bias).astype(bf16).astype(f32) * 0.125
        rows = turned.T.astype(bf16)
        for part in range(row_total // QB):
            query = order_ref[block] * (row_total // QB) + part
            for pair in range(pairs):
                piece = rows[part * QB : (part + 1) * QB, pair * 128 : (pair + 1) * 128]
                twin_ref[query, pair, 0:QB, :] = jnp.where(left, piece, jnp.zeros_like(piece))
                twin_ref[query, pair, QB : 2 * QB, :] = jnp.where(left, jnp.zeros_like(piece), piece)
        return carry

    lax.fori_loop(0, narrow_count, ask, 0)


def attend_kernel(
    parts, chunk, order_ref, starts_ref, counts_ref, keys_ref, values_ref, twin_ref, *rest
):
    out_refs = rest[:-5]
    total_ref, even_ref, odd_ref, block_ref, first_ref = rest[-5:]
    receivers = len(out_refs)
    pairs = twin_ref.shape[1]
    left = lax.broadcasted_iota(jnp.int32, (QB, 128), 1) < HEAD

    def listed(index, count):
        total_ref[index] = jnp.zeros_like(total_ref[index])
        block = index * parts + chunk

        def note(slot, inner):
            block_ref[count + slot] = index
            first_ref[count + slot] = starts_ref[block * NB + slot]
            return inner

        lax.fori_loop(0, counts_ref[block], note, 0)
        return count + counts_ref[block]

    steps = lax.fori_loop(0, receivers, listed, 0)
    for extra in range(2):
        block_ref[steps + extra] = receivers
        first_ref[steps + extra] = first_ref[0]

    ones = jnp.ones((KB, 128), bf16)

    def weigh(step, weights_ref):
        start = pl.multiple_of(first_ref[step], KB)
        query = jnp.minimum(block_ref[step], receivers - 1) * parts + chunk
        for pair in range(pairs):
            scores = jnp.dot(
                twin_ref[query, pair],
                keys_ref[pair * 128 : (pair + 1) * 128, pl.ds(start, KB)],
                preferred_element_type=f32,
            )
            weights_ref[pair] = jnp.exp(scores).astype(bf16)

    def gather(step, weights_ref):
        start = pl.multiple_of(first_ref[step], KB)
        block = block_ref[step]
        for pair in range(pairs):
            side = jnp.concatenate(
                [values_ref[pl.ds(start, KB), pair * 128 : (pair + 1) * 128], ones], axis=1
            )
            total_ref[block, pair] += jnp.dot(weights_ref[pair], side, preferred_element_type=f32)

    weigh(0, even_ref)

    def visit(twice, carry):
        step = twice * 2
        weigh(step + 1, odd_ref)
        gather(step, even_ref)
        weigh(step + 2, even_ref)
        gather(step + 1, odd_ref)
        return carry

    lax.fori_loop(0, (steps + 1) // 2, visit, 0)

    for away in range(receivers):
        block = order_ref[0] ^ away
        for pair in range(pairs):
            both = total_ref[block, pair, :, 0:128] / total_ref[block, pair, :, 128:256]
            out_refs[away][:, pair * 128 : (pair + 1) * 128] = jnp.where(
                left, both[0:QB], both[QB : 2 * QB]
            ).astype(bf16)


def attend_scratch(receivers, heads_width):
    pairs = heads_width // 128
    return [
        pltpu.VMEM((receivers + 1, pairs, 2 * QB, 256), f32),
        pltpu.VMEM((pairs, 2 * QB, KB), bf16),
        pltpu.VMEM((pairs, 2 * QB, KB), bf16),
        pltpu.SMEM((receivers * NB + 2,), jnp.int32),
        pltpu.SMEM((receivers * NB + 2,), jnp.int32),
    ]


def output_kernel(parts, narrow_count, together, order_ref, *refs):
    attended_refs = refs[: parts * narrow_count]
    weight_ref, gate_ref, out_ref = refs[parts * narrow_count :]
    rows = out_ref.shape[1] // together
    totals = [None] * together
    for away in range(narrow_count):
        attended = jnp.concatenate(
            [attended_refs[chunk * narrow_count + away][...] for chunk in range(parts)], axis=0
        )
        for index in range(together):
            at = pl.multiple_of((index * narrow_count + (order_ref[0] ^ away)) * rows, 16)
            term = ntdot(attended, weight_ref[pl.ds(at, rows), :])
            totals[index] = term if away == 0 else totals[index] + term
    for index, total in enumerate(totals):
        columns = slice(index * rows, (index + 1) * rows)
        out_ref[:, columns] = (total * gate_ref[:, columns]).astype(bf16)


def flip(block, axis, bit):
    devices = range(lax.axis_size(axis))
    return lax.ppermute(block, axis, [(i, i ^ bit) for i in devices])


def cost(flops, moved):
    return pl.CostEstimate(flops=flops, bytes_accessed=moved, transcendentals=0)


def block(
    latents,
    targets,
    embed_weight,
    mod_shift,
    mod_scale,
    qkv_weight,
    out_weight,
    mod_gate,
    block_list,
    block_count,
):
    row_total, patch = latents.shape
    width = embed_weight.shape[1]
    wide_count = lax.axis_size("wide")
    narrow_count = lax.axis_size("narrow")
    wide_index = lax.axis_index("wide")
    narrow_index = lax.axis_index("narrow")
    tile_size = row_total * narrow_count
    depth, heads_width = qkv_weight.shape[1:]
    share = row_total // wide_count
    count = -(-SPAN * share // 16) * 16
    piece = 3 * heads_width // wide_count

    out_all = lax.all_gather(out_weight, ("wide", "narrow"), axis=0, tiled=True)

    first = wide_index * depth
    extra = 16 + count + 16
    sliced = depth % 128 != 0 or piece % 16 != 0
    scale = mod_scale.reshape(1, width)
    shift = mod_shift.reshape(1, width)
    own = embed_weight
    if sliced:
        own, scale, shift = (
            lax.dynamic_slice_in_dim(array, first, depth, 1) for array in (own, scale, shift)
        )
        prep_shapes = (
            jax.ShapeDtypeStruct((3 * heads_width, patch), bf16),
            jax.ShapeDtypeStruct((wide_count, extra, patch), bf16),
        )
    else:
        prep_shapes = (jax.ShapeDtypeStruct((wide_count, piece + extra, patch), bf16),)
    smem = pl.BlockSpec(memory_space=pltpu.SMEM)
    prepared = pl.pallas_call(
        functools.partial(prep_kernel, wide_count, sliced),
        out_shape=prep_shapes,
        in_specs=[smem] + [whole_spec()] * 7,
        out_specs=tuple(whole_spec() for _ in prep_shapes),
        name="prep",
    )(
        first.astype(jnp.int32).reshape(1),
        embed_weight,
        own,
        scale,
        shift,
        qkv_weight,
        latents,
        targets.reshape(1, row_total),
    )
    payload = prepared[0]
    if sliced:
        payload = jnp.concatenate(
            [payload.reshape(wide_count, piece, patch), prepared[1]], axis=1
        )
    gram = pl.pallas_call(
        gram_kernel,
        out_shape=jax.ShapeDtypeStruct((3, patch, patch), bf16),
        in_specs=[whole_spec()],
        out_specs=whole_spec(),
        name="gram",
    )(embed_weight)
    arrived = lax.all_to_all(payload, "wide", split_axis=0, concat_axis=0, tiled=True)

    summed = jnp.sum(arrived[:, :piece].astype(f32), axis=0).astype(bf16)
    bias = jnp.sum(arrived[:, piece : piece + 16].astype(f32), axis=0)
    spread = jnp.broadcast_to(summed[None], (wide_count,) + summed.shape)
    near = arrived[:, piece + 16 : piece + 16 + SPAN * share]
    near = near.reshape(wide_count, SPAN, share, patch).transpose(1, 0, 2, 3)
    near = near.reshape(SPAN * row_total, patch)
    mine = arrived[:, piece + 16 + count, :share].reshape(-1)
    mine = jnp.pad(mine, (0, 16 * 128 - row_total)).reshape(16, 128)
    group = jnp.concatenate([near, mine], axis=0)[None]
    order = [0]
    bits = [1 << k for k in range(1, narrow_count.bit_length() - 1)] + [1]
    for bit in bits:
        other = flip(group, "narrow", bit)
        group = jnp.concatenate([group, other], axis=0)
        order = order + [index ^ bit for index in order]
    everything = lax.all_to_all(spread, "wide", split_axis=0, concat_axis=0, tiled=True)
    weight_all = everything.reshape(3 * heads_width, patch)

    order_ids = jnp.bitwise_xor(jnp.array(order, jnp.int32), narrow_index)
    starts = (block_list * KB - (wide_index - REACH) * tile_size).reshape(-1)
    parts = row_total // QB
    pairs = heads_width // 128
    keys, values, twin = pl.pallas_call(
        functools.partial(project_kernel, row_total, tile_size),
        out_shape=(
            pltpu.VMEM((heads_width, SPAN * tile_size), bf16),
            pltpu.VMEM((SPAN * tile_size, heads_width), bf16),
            pltpu.VMEM((tile_size // QB, pairs, 2 * QB, 128), bf16),
        ),
        in_specs=[smem] + [whole_spec()] * 4,
        out_specs=(whole_spec(),) * 3,
        scratch_shapes=[pltpu.VMEM((SPAN * tile_size, 256), bf16)],
        compiler_params=pltpu.CompilerParams(vmem_limit_bytes=PROJECT_VMEM),
        cost_estimate=cost(10 * SPAN * tile_size * patch * heads_width, 16 << 20),
        name="project",
    )(order_ids, group, weight_all, bias, gram)

    pieces = []
    for chunk in range(parts):
        mine = pl.pallas_call(
            functools.partial(attend_kernel, parts, chunk),
            out_shape=(jax.ShapeDtypeStruct((QB, heads_width), bf16),) * narrow_count,
            in_specs=[smem] * 3 + [whole_spec()] * 3,
            out_specs=(whole_spec(),) * narrow_count,
            scratch_shapes=attend_scratch(narrow_count, heads_width),
            compiler_params=pltpu.CompilerParams(vmem_limit_bytes=ATTEND_VMEM),
            cost_estimate=cost(4 * tile_size // parts * NB * KB * heads_width, 16 << 20),
        )(order_ids, starts, block_count, keys, values, twin)
        pieces.append(mine[0])
        for away in range(1, narrow_count):
            pieces.append(flip(mine[away], "narrow", away))

    out_rows = out_weight.shape[0]
    gate = mod_gate.reshape(1, width)
    if out_rows % 128 == 0:
        together = 2 if wide_count % 2 == 0 else 1
        span = together * out_rows
        return pl.pallas_call(
            functools.partial(output_kernel, parts, narrow_count, together),
            grid=(wide_count // together,),
            out_shape=jax.ShapeDtypeStruct((row_total, width), bf16),
            in_specs=[smem]
            + [pl.BlockSpec((QB, heads_width), lambda i: (0, 0))] * (parts * narrow_count)
            + [
                pl.BlockSpec((narrow_count * span, heads_width), lambda i: (i, 0)),
                pl.BlockSpec((1, span), lambda i: (0, i)),
            ],
            out_specs=pl.BlockSpec((row_total, span), lambda i: (0, i)),
            compiler_params=pltpu.CompilerParams(vmem_limit_bytes=OUTPUT_VMEM),
            name="output",
        )(order_ids, *pieces, out_all, gate)
    weights = out_all.reshape(wide_count, narrow_count, out_rows, heads_width)
    product = 0.0
    for away in range(narrow_count):
        attended = jnp.concatenate(pieces[away::narrow_count], axis=0)
        weight = lax.dynamic_index_in_dim(weights, narrow_index ^ away, 1, False)
        product = product + jnp.einsum(
            "tk,wfk->twf", attended, weight, preferred_element_type=f32
        )
    return (gate * product.reshape(row_total, width)).astype(bf16)


def solution(mesh):
    in_specs = (
        P(("wide", "narrow"), None),
        P(("wide", "narrow")),
        P(),
        P(),
        P(),
        P(None, "wide", "narrow"),
        P("wide", "narrow"),
        P(),
        P("wide", None),
        P("wide"),
    )
    out_specs = P(("wide", "narrow"), None)
    return jax.shard_map(block, mesh=mesh, in_specs=in_specs, out_specs=out_specs, check_vma=False)
```

```python
import functools

import jax
import jax.numpy as jnp
from jax import lax
from jax.experimental import pallas as pl
from jax.experimental.pallas import tpu as pltpu
from jax.sharding import PartitionSpec as P


HEAD = 64
NB = 8
KB = 512
QB = 128
REACH = 2
SPAN = 2 * REACH + 1
EPSILON = 1e-06
PROJECT_VMEM = 32 << 20
ATTEND_VMEM = 32 << 20
OUTPUT_VMEM = 53 << 20
PARTIAL_VMEM = 24 << 20

f32 = jnp.float32
bf16 = jnp.bfloat16
NT = (((1,), (1,)), ((), ()))


def ntdot(a, b):
    return lax.dot_general(a, b, NT, preferred_element_type=f32)


def whole_spec():
    return pl.BlockSpec(memory_space=pltpu.VMEM)


def split3(value):
    high = value.astype(bf16)
    rest = value - high.astype(f32)
    mid = rest.astype(bf16)
    low = (rest - mid.astype(f32)).astype(bf16)
    return high, mid, low


def gram_kernel(embed_ref, gram_ref):
    embed = embed_ref[...].astype(f32)
    width = embed.shape[1]
    centred = embed - jnp.mean(embed, axis=1, keepdims=True)
    gram = lax.dot_general(
        centred, centred, NT, preferred_element_type=f32, precision=lax.Precision.HIGHEST
    ) * (1.0 / width)
    for index, term in enumerate(split3(gram)):
        gram_ref[index] = term


def prep_kernel(
    wide_count,
    sliced,
    at_ref,
    embed_ref,
    slice_ref,
    scale_ref,
    shift_ref,
    qkv_ref,
    latents_ref,
    targets_ref,
    *out_refs,
):
    depth, heads_width = qkv_ref.shape[1:]
    patch = embed_ref.shape[0]
    if sliced:
        own, scale, shift = slice_ref[...], scale_ref[...], shift_ref[...]
    else:
        columns = pl.ds(pl.multiple_of(at_ref[0], 128), depth)
        own, scale, shift = embed_ref[:, columns], scale_ref[:, columns], shift_ref[:, columns]
    piece = 3 * heads_width // wide_count
    row_mean = jnp.mean(embed_ref[...].astype(f32), axis=1, keepdims=True)
    factor = (own.astype(f32) - row_mean) * (1.0 + scale)
    stacked = jnp.concatenate([factor, jnp.broadcast_to(shift, (16, depth))], axis=0)
    high, mid, _ = split3(stacked)
    bias_rows = []
    for part in range(3):
        weights = qkv_ref[part]
        product = jnp.dot(high, weights, preferred_element_type=f32) + jnp.dot(
            mid, weights, preferred_element_type=f32
        )
        for chunk in range(heads_width // 128):
            bias_rows.append(product[patch : patch + 1, chunk * 128 : (chunk + 1) * 128])
        turned = product[0:patch].T
        if part < 2:
            grouped = turned.reshape(heads_width // HEAD, HEAD, patch)
            grouped = grouped - jnp.mean(grouped, axis=1, keepdims=True)
            turned = grouped.reshape(turned.shape)
        turned = turned.astype(bf16)
        top = part * heads_width
        if sliced:
            out_refs[0][top : top + heads_width, :] = turned
            continue
        for receiver in range(wide_count):
            low = max(receiver * piece, top)
            end = min((receiver + 1) * piece, top + heads_width)
            if low < end:
                base = receiver * piece
                out_refs[0][receiver, low - base : end - base, :] = turned[low - top : end - top]
    bias_rows.append(jnp.zeros((16 - len(bias_rows), 128), f32))
    bias = jnp.concatenate(bias_rows, axis=0).astype(bf16)
    row_total = latents_ref.shape[0]
    share = row_total // wide_count
    across = targets_ref[...]
    same = lax.broadcasted_iota(jnp.int32, (row_total, row_total), 0) == lax.broadcasted_iota(
        jnp.int32, (row_total, row_total), 1
    )
    down = jnp.sum(jnp.where(same, across.astype(f32), 0.0), axis=1, keepdims=True)
    across = across.astype(f32)
    slot_across = jnp.sum((down < across).astype(f32), axis=0, keepdims=True)
    slot_down = jnp.sum((across < down).astype(f32), axis=1, keepdims=True)
    local = (down.astype(jnp.int32) % row_total).astype(f32)
    count = -(-SPAN * share // 16) * 16
    latents = latents_ref[...]
    wanted = lax.broadcasted_iota(jnp.int32, (count, row_total), 0)
    lane = lax.broadcasted_iota(jnp.int32, (row_total, 128), 1)
    for receiver in range(wide_count):
        first = (receiver - REACH) * share
        chosen = (slot_across == (wanted + first).astype(f32)) & (wanted < SPAN * share)
        rows = jnp.dot(chosen.astype(bf16), latents, preferred_element_type=f32).astype(bf16)
        mine = (slot_down == (lane + receiver * share).astype(f32)) & (lane < share)
        spots = jnp.sum(jnp.where(mine, local, 0.0), axis=0, keepdims=True)
        spots = jnp.broadcast_to(spots, (16, 128)).astype(bf16)
        if sliced:
            out_refs[1][receiver, 0:16, :] = bias
            out_refs[1][receiver, 16 : 16 + count, :] = rows
            out_refs[1][receiver, 16 + count :, :] = spots
        else:
            out_refs[0][receiver, piece : piece + 16, :] = bias
            out_refs[0][receiver, piece + 16 : piece + 16 + count, :] = rows
            out_refs[0][receiver, piece + 16 + count :, :] = spots


def project_kernel(
    row_total,
    tile_size,
    order_ref,
    patches_ref,
    weight_ref,
    bias_ref,
    gram_ref,
    keys_ref,
    values_ref,
    twin_ref,
    both_ref,
):
    heads_width = keys_ref.shape[0]
    local_heads = heads_width // HEAD
    pairs = heads_width // 128
    narrow_count = tile_size // row_total
    chunks = heads_width // 128

    def doubled(part):
        weight = weight_ref[part * heads_width : (part + 1) * heads_width, :]
        return jnp.concatenate([weight, weight], axis=1)

    def centred_bias(part):
        same = lax.broadcasted_iota(jnp.int32, (128, 128), 0) == lax.broadcasted_iota(
            jnp.int32, (128, 128), 1
        )
        pieces = []
        for chunk in range(chunks):
            row = bias_ref[part * chunks + chunk : part * chunks + chunk + 1, :]
            pieces.append(jnp.sum(jnp.where(same, row, 0.0), axis=1, keepdims=True))
        grouped = jnp.concatenate(pieces, axis=0).reshape(local_heads, HEAD, 1)
        grouped = grouped - jnp.mean(grouped, axis=1, keepdims=True)
        return grouped.reshape(heads_width, 1)

    def unit_heads(turned, bias):
        grouped = (turned + bias).reshape(local_heads, HEAD, turned.shape[1])
        square = jnp.mean(grouped * grouped, axis=1, keepdims=True)
        return (grouped * lax.rsqrt(square + EPSILON)).reshape(turned.shape)

    gram_top = jnp.concatenate([gram_ref[0], gram_ref[1]], axis=0)
    gram_low = gram_ref[2]

    def scale(step, carry):
        block = step // SPAN
        tile = step % SPAN
        rows = patches_ref[block, pl.ds(pl.multiple_of(tile * row_total, row_total), row_total), :]
        wide_rows = rows.astype(f32)
        image = jnp.dot(
            jnp.concatenate([rows, rows], axis=1), gram_top, preferred_element_type=f32
        ) + jnp.dot(rows, gram_low, preferred_element_type=f32)
        variance = jnp.sum(image * wide_rows, axis=1, keepdims=True)
        scaled = wide_rows * lax.rsqrt(jnp.maximum(variance, 0.0) + EPSILON)
        high = scaled.astype(bf16)
        at = pl.multiple_of(tile * tile_size + order_ref[block] * row_total, row_total)
        both_ref[pl.ds(at, row_total), 0:128] = high
        both_ref[pl.ds(at, row_total), 128:256] = (scaled - high.astype(f32)).astype(bf16)
        return carry

    lax.fori_loop(0, SPAN * narrow_count, scale, 0, unroll=SPAN)

    key_bias = centred_bias(1)
    key_weight = doubled(1)
    value_weight = doubled(2).astype(f32).T.astype(bf16)
    value_bias = jnp.concatenate(
        [bias_ref[2 * chunks + chunk : 2 * chunks + chunk + 1, :] for chunk in range(chunks)], axis=1
    )

    def project(step, carry):
        at = pl.multiple_of(step * 256, 256)
        both = both_ref[pl.ds(at, 256), :]
        keys_ref[:, pl.ds(at, 256)] = unit_heads(ntdot(key_weight, both), key_bias).astype(bf16)
        values_ref[pl.ds(at, 256), :] = (
            jnp.dot(both, value_weight, preferred_element_type=f32) + value_bias
        ).astype(bf16)
        return carry

    lax.fori_loop(0, SPAN * tile_size // 256, project, 0, unroll=2)

    query_bias = centred_bias(0)
    query_weight = doubled(0)
    left = lax.broadcasted_iota(jnp.int32, (QB, 128), 1) < HEAD
    spot_rows = row_total // 128

    def ask(block, carry):
        place = order_ref[block] * row_total
        spots = jnp.concatenate(
            [
                patches_ref[block, SPAN * row_total + row : SPAN * row_total + row + 1, :]
                for row in range(spot_rows)
            ],
            axis=1,
        )
        wanted = lax.broadcasted_iota(jnp.int32, (row_total, row_total), 0).astype(f32)
        chosen = (spots.astype(f32) == wanted).astype(bf16)
        both = both_ref[pl.ds(pl.multiple_of(REACH * tile_size + place, row_total), row_total), :]
        placed = jnp.dot(chosen, both, preferred_element_type=f32).astype(bf16)
        turned = unit_heads(ntdot(query_weight, placed), query_bias).astype(bf16).astype(f32) * 0.125
        rows = turned.T.astype(bf16)
        for part in range(row_total // QB):
            query = order_ref[block] * (row_total // QB) + part
            for pair in range(pairs):
                piece = rows[part * QB : (part + 1) * QB, pair * 128 : (pair + 1) * 128]
                twin_ref[query, pair, 0:QB, :] = jnp.where(left, piece, jnp.zeros_like(piece))
                twin_ref[query, pair, QB : 2 * QB, :] = jnp.where(left, jnp.zeros_like(piece), piece)
        return carry

    lax.fori_loop(0, narrow_count, ask, 0)


def attend_kernel(
    parts, entries, order_ref, starts_ref, counts_ref, keys_ref, values_ref, twin_ref, *rest
):
    out_refs = rest[:-6]
    total_ref, even_ref, odd_ref, block_ref, query_ref, first_ref = rest[-6:]
    pairs = twin_ref.shape[1]
    left = lax.broadcasted_iota(jnp.int32, (QB, 128), 1) < HEAD

    steps = jnp.int32(0)
    for index, (away, part) in enumerate(entries):
        total_ref[index] = jnp.zeros_like(total_ref[index])
        block = (order_ref[0] ^ away) * parts + part

        def note(slot, at, index=index, block=block):
            block_ref[at] = index
            query_ref[at] = block
            first_ref[at] = starts_ref[block * NB + slot]
            return at + 1

        steps = lax.fori_loop(0, counts_ref[block], note, steps)
    for extra in range(2):
        block_ref[steps + extra] = len(entries)
        query_ref[steps + extra] = query_ref[0]
        first_ref[steps + extra] = first_ref[0]

    ones = jnp.ones((KB, 128), bf16)

    def weigh(step, weights_ref):
        start = pl.multiple_of(first_ref[step], KB)
        query = query_ref[step]
        for pair in range(pairs):
            scores = jnp.dot(
                twin_ref[query, pair],
                keys_ref[pair * 128 : (pair + 1) * 128, pl.ds(start, KB)],
                preferred_element_type=f32,
            )
            weights_ref[pair] = jnp.exp(scores).astype(bf16)

    def gather(step, weights_ref):
        start = pl.multiple_of(first_ref[step], KB)
        block = block_ref[step]
        for pair in range(pairs):
            side = jnp.concatenate(
                [values_ref[pl.ds(start, KB), pair * 128 : (pair + 1) * 128], ones], axis=1
            )
            total_ref[block, pair] += jnp.dot(weights_ref[pair], side, preferred_element_type=f32)

    weigh(0, even_ref)

    def visit(twice, carry):
        step = twice * 2
        weigh(step + 1, odd_ref)
        gather(step, even_ref)
        weigh(step + 2, even_ref)
        gather(step + 1, odd_ref)
        return carry

    lax.fori_loop(0, (steps + 1) // 2, visit, 0)

    for index in range(len(entries)):
        for pair in range(pairs):
            both = total_ref[index, pair, :, 0:128] / total_ref[index, pair, :, 128:256]
            out_refs[index][:, pair * 128 : (pair + 1) * 128] = jnp.where(
                left, both[0:QB], both[QB : 2 * QB]
            ).astype(bf16)


def attend_scratch(entries, heads_width):
    pairs = heads_width // 128
    return [
        pltpu.VMEM((entries + 1, pairs, 2 * QB, 256), f32),
        pltpu.VMEM((pairs, 2 * QB, KB), bf16),
        pltpu.VMEM((pairs, 2 * QB, KB), bf16),
        pltpu.SMEM((entries * NB + 2,), jnp.int32),
        pltpu.SMEM((entries * NB + 2,), jnp.int32),
        pltpu.SMEM((entries * NB + 2,), jnp.int32),
    ]


def output_kernel(parts, narrow_count, together, order_ref, *refs):
    attended_refs = refs[: parts * narrow_count]
    weight_ref, gate_ref, out_ref = refs[parts * narrow_count :]
    rows = out_ref.shape[1] // together
    totals = [None] * together
    for away in range(narrow_count):
        attended = jnp.concatenate(
            [attended_refs[chunk * narrow_count + away][...] for chunk in range(parts)], axis=0
        )
        for index in range(together):
            at = pl.multiple_of((index * narrow_count + (order_ref[0] ^ away)) * rows, 16)
            term = ntdot(attended, weight_ref[pl.ds(at, rows), :])
            totals[index] = term if away == 0 else totals[index] + term
    for index, total in enumerate(totals):
        columns = slice(index * rows, (index + 1) * rows)
        out_ref[:, columns] = (total * gate_ref[:, columns]).astype(bf16)


def partial_kernel(kept, total, held_ref, *refs):
    attended_refs = refs[:total]
    weight_refs = refs[total:-2]
    keep_ref, send_ref = refs[-2:]
    rows = weight_refs[0].shape[0]
    keep = kept * QB
    for index, weight_ref in enumerate(weight_refs):

        @pl.when(held_ref[index] >= 0)
        def _():
            attended = jnp.concatenate([ref[...] for ref in attended_refs], axis=0)
            product = ntdot(attended, weight_ref[...])
            columns = pl.ds(pl.multiple_of(held_ref[index] * rows, 128), rows)
            keep_ref[:, columns] = product[0:keep]
            send_ref[:, columns] = product[keep:].astype(bf16)


def final_kernel(own_ref, first_ref, second_ref, third_ref, gate_ref, out_ref):
    far = jnp.concatenate([second_ref[...], third_ref[...]], axis=0).astype(f32)
    total = own_ref[...] + first_ref[...].astype(f32) + far
    out_ref[...] = (total * gate_ref[...]).astype(bf16)


def flip(block, axis, bit):
    devices = range(lax.axis_size(axis))
    return lax.ppermute(block, axis, [(i, i ^ bit) for i in devices])


def cost(flops, moved):
    return pl.CostEstimate(flops=flops, bytes_accessed=moved, transcendentals=0)


def gathered_rows(own):
    count = lax.axis_size("wide")
    index = lax.axis_index("wide")
    length = count // 2
    blocks, held = [own], [index]
    blocks.append(lax.ppermute(own, "wide", [(i, i ^ 1) for i in range(count)]))
    held.append(index ^ 1)
    for sign in (1, -1):
        current = own
        for step in range(1, length):
            move = 2 * sign
            route = [
                (i, i + move)
                for i in range(count)
                if 0 <= i + move < count and 0 <= i - move * (step - 1) < count
            ]
            current = lax.ppermute(current, "wide", route)
            source = index - move * step
            valid = (source >= 0) & (source < count)
            blocks.append(current)
            held.append(jnp.where(valid, source, -1))
            swap = [(i, i ^ 1) for i in range(count) if 0 <= i - move * step < count]
            blocks.append(lax.ppermute(current, "wide", swap))
            held.append(jnp.where(valid, source ^ 1, -1))
    return blocks, jnp.stack(held).astype(jnp.int32)


def block(
    latents,
    targets,
    embed_weight,
    mod_shift,
    mod_scale,
    qkv_weight,
    out_weight,
    mod_gate,
    block_list,
    block_count,
):
    row_total, patch = latents.shape
    width = embed_weight.shape[1]
    wide_count = lax.axis_size("wide")
    narrow_count = lax.axis_size("narrow")
    wide_index = lax.axis_index("wide")
    narrow_index = lax.axis_index("narrow")
    tile_size = row_total * narrow_count
    depth, heads_width = qkv_weight.shape[1:]
    share = row_total // wide_count
    count = -(-SPAN * share // 16) * 16
    piece = 3 * heads_width // wide_count

    chained = narrow_count == 4 and out_weight.shape[0] % 128 == 0 and row_total == 2 * QB
    if chained:
        blocks, held = gathered_rows(out_weight)
    else:
        out_all = lax.all_gather(out_weight, ("wide", "narrow"), axis=0, tiled=True)

    first = wide_index * depth
    extra = 16 + count + 16
    sliced = depth % 128 != 0 or piece % 16 != 0
    scale = mod_scale.reshape(1, width)
    shift = mod_shift.reshape(1, width)
    own = embed_weight
    if sliced:
        own, scale, shift = (
            lax.dynamic_slice_in_dim(array, first, depth, 1) for array in (own, scale, shift)
        )
        prep_shapes = (
            jax.ShapeDtypeStruct((3 * heads_width, patch), bf16),
            jax.ShapeDtypeStruct((wide_count, extra, patch), bf16),
        )
    else:
        prep_shapes = (jax.ShapeDtypeStruct((wide_count, piece + extra, patch), bf16),)
    smem = pl.BlockSpec(memory_space=pltpu.SMEM)
    prepare = pl.pallas_call(
        functools.partial(prep_kernel, wide_count, sliced),
        out_shape=prep_shapes,
        in_specs=[smem] + [whole_spec()] * 7,
        out_specs=tuple(whole_spec() for _ in prep_shapes),
        cost_estimate=cost(1 << 28, 4 << 20),
        name="prep",
    )
    prepared = prepare(
        first.astype(jnp.int32).reshape(1),
        embed_weight,
        own,
        scale,
        shift,
        qkv_weight,
        latents,
        targets.reshape(1, row_total),
    )
    payload = prepared[0]
    if sliced:
        payload = jnp.concatenate(
            [payload.reshape(wide_count, piece, patch), prepared[1]], axis=1
        )
    gram = pl.pallas_call(
        gram_kernel,
        out_shape=jax.ShapeDtypeStruct((3, patch, patch), bf16),
        in_specs=[whole_spec()],
        out_specs=whole_spec(),
        name="gram",
    )(embed_weight)
    arrived = lax.all_to_all(payload, "wide", split_axis=0, concat_axis=0, tiled=True)

    summed = jnp.sum(arrived[:, :piece].astype(f32), axis=0).astype(bf16)
    bias = jnp.sum(arrived[:, piece : piece + 16].astype(f32), axis=0)
    spread = jnp.broadcast_to(summed[None], (wide_count,) + summed.shape)
    near = arrived[:, piece + 16 : piece + 16 + SPAN * share]
    near = near.reshape(wide_count, SPAN, share, patch).transpose(1, 0, 2, 3)
    near = near.reshape(SPAN * row_total, patch)
    mine = arrived[:, piece + 16 + count, :share].reshape(-1)
    mine = jnp.pad(mine, (0, 16 * 128 - row_total)).reshape(16, 128)
    group = jnp.concatenate([near, mine], axis=0)[None]
    order = [0]
    bits = [1 << k for k in range(1, narrow_count.bit_length() - 1)] + [1]
    for bit in bits:
        other = flip(group, "narrow", bit)
        group = jnp.concatenate([group, other], axis=0)
        order = order + [index ^ bit for index in order]
    everything = lax.all_to_all(spread, "wide", split_axis=0, concat_axis=0, tiled=True)
    weight_all = everything.reshape(3 * heads_width, patch)

    order_ids = jnp.bitwise_xor(jnp.array(order, jnp.int32), narrow_index)
    starts = (block_list * KB - (wide_index - REACH) * tile_size).reshape(-1)
    parts = row_total // QB
    pairs = heads_width // 128
    keys, values, twin = pl.pallas_call(
        functools.partial(project_kernel, row_total, tile_size),
        out_shape=(
            pltpu.VMEM((heads_width, SPAN * tile_size), bf16),
            pltpu.VMEM((SPAN * tile_size, heads_width), bf16),
            pltpu.VMEM((tile_size // QB, pairs, 2 * QB, 128), bf16),
        ),
        in_specs=[smem] + [whole_spec()] * 4,
        out_specs=(whole_spec(),) * 3,
        scratch_shapes=[pltpu.VMEM((SPAN * tile_size, 256), bf16)],
        compiler_params=pltpu.CompilerParams(vmem_limit_bytes=PROJECT_VMEM),
        cost_estimate=cost(10 * SPAN * tile_size * patch * heads_width, 16 << 20),
        name="project",
    )(order_ids, group, weight_all, bias, gram)

    def attend(entries):
        return pl.pallas_call(
            functools.partial(attend_kernel, parts, entries),
            out_shape=(jax.ShapeDtypeStruct((QB, heads_width), bf16),) * len(entries),
            in_specs=[smem] * 3 + [whole_spec()] * 3,
            out_specs=(whole_spec(),) * len(entries),
            scratch_shapes=attend_scratch(len(entries), heads_width),
            compiler_params=pltpu.CompilerParams(vmem_limit_bytes=ATTEND_VMEM),
            cost_estimate=cost(4 * QB * len(entries) * NB * KB * heads_width, 16 << 20),
        )(order_ids, starts, block_count, keys, values, twin)

    if chained:
        gate = mod_gate.reshape(1, width)

        def multiply(attended, kept):
            rows = len(attended) * QB
            return pl.pallas_call(
                functools.partial(partial_kernel, kept, len(attended)),
                out_shape=(
                    jax.ShapeDtypeStruct((kept * QB, width), f32),
                    jax.ShapeDtypeStruct((rows - kept * QB, width), bf16),
                ),
                in_specs=[smem] + [whole_spec()] * (len(attended) + len(blocks)),
                out_specs=(whole_spec(),) * 2,
                compiler_params=pltpu.CompilerParams(vmem_limit_bytes=PARTIAL_VMEM),
                cost_estimate=cost(2 * rows * heads_width * width, 8 << 20),
            )(held, *attended, *blocks)

        far = []
        for part in range(parts):
            attended = attend(((2, part), (3, part)))
            keep, send = multiply(attended, 1)
            other = flip(send, "narrow", 1)
            joined = (keep + other.astype(f32)).astype(bf16)
            far.append(flip(joined, "narrow", 2))
        attended = attend(((0, 0), (0, 1), (1, 0), (1, 1)))
        own, send = multiply(attended, 2)
        other = flip(send, "narrow", 1)
        return pl.pallas_call(
            final_kernel,
            out_shape=jax.ShapeDtypeStruct((row_total, width), bf16),
            in_specs=[whole_spec()] * 5,
            out_specs=whole_spec(),
            name="final",
        )(own, other, *far, gate)

    pieces = []
    for chunk in range(parts):
        mine = attend(tuple((away, chunk) for away in range(narrow_count)))
        pieces.append(mine[0])
        for away in range(1, narrow_count):
            pieces.append(flip(mine[away], "narrow", away))

    out_rows = out_weight.shape[0]
    gate = mod_gate.reshape(1, width)
    if out_rows % 128 == 0:
        together = 2 if wide_count % 2 == 0 else 1
        span = together * out_rows
        return pl.pallas_call(
            functools.partial(output_kernel, parts, narrow_count, together),
            grid=(wide_count // together,),
            out_shape=jax.ShapeDtypeStruct((row_total, width), bf16),
            in_specs=[smem]
            + [pl.BlockSpec((QB, heads_width), lambda i: (0, 0))] * (parts * narrow_count)
            + [
                pl.BlockSpec((narrow_count * span, heads_width), lambda i: (i, 0)),
                pl.BlockSpec((1, span), lambda i: (0, i)),
            ],
            out_specs=pl.BlockSpec((row_total, span), lambda i: (0, i)),
            compiler_params=pltpu.CompilerParams(vmem_limit_bytes=OUTPUT_VMEM),
            name="output",
        )(order_ids, *pieces, out_all, gate)
    weights = out_all.reshape(wide_count, narrow_count, out_rows, heads_width)
    product = 0.0
    for away in range(narrow_count):
        attended = jnp.concatenate(pieces[away::narrow_count], axis=0)
        weight = lax.dynamic_index_in_dim(weights, narrow_index ^ away, 1, False)
        product = product + jnp.einsum(
            "tk,wfk->twf", attended, weight, preferred_element_type=f32
        )
    return (gate * product.reshape(row_total, width)).astype(bf16)


def solution(mesh):
    in_specs = (
        P(("wide", "narrow"), None),
        P(("wide", "narrow")),
        P(),
        P(),
        P(),
        P(None, "wide", "narrow"),
        P("wide", "narrow"),
        P(),
        P("wide", None),
        P("wide"),
    )
    out_specs = P(("wide", "narrow"), None)
    return jax.shard_map(block, mesh=mesh, in_specs=in_specs, out_specs=out_specs, check_vma=False)
```

```python
import functools

import jax
import jax.numpy as jnp
from jax import lax
from jax.experimental import pallas as pl
from jax.experimental.pallas import tpu as pltpu
from jax.sharding import PartitionSpec as P


HEAD = 64
NB = 8
KB = 512
QB = 128
REACH = 2
SPAN = 2 * REACH + 1
EPSILON = 1e-06
PROJECT_VMEM = 28 << 20
ATTEND_VMEM = 14 << 20
OUTPUT_VMEM = 53 << 20
SMALL_VMEM = 14 << 20

f32 = jnp.float32
bf16 = jnp.bfloat16
NT = (((1,), (1,)), ((), ()))


def ntdot(a, b):
    return lax.dot_general(a, b, NT, preferred_element_type=f32)


def whole_spec():
    return pl.BlockSpec(memory_space=pltpu.VMEM)


def split3(value):
    high = value.astype(bf16)
    rest = value - high.astype(f32)
    mid = rest.astype(bf16)
    low = (rest - mid.astype(f32)).astype(bf16)
    return high, mid, low


def gram_kernel(embed_ref, gram_ref):
    embed = embed_ref[...].astype(f32)
    width = embed.shape[1]
    centred = embed - jnp.mean(embed, axis=1, keepdims=True)
    gram = lax.dot_general(
        centred, centred, NT, preferred_element_type=f32, precision=lax.Precision.HIGHEST
    ) * (1.0 / width)
    for index, term in enumerate(split3(gram)):
        gram_ref[index] = term


def prep_kernel(
    wide_count,
    sliced,
    at_ref,
    embed_ref,
    slice_ref,
    scale_ref,
    shift_ref,
    qkv_ref,
    latents_ref,
    targets_ref,
    *out_refs,
):
    depth, heads_width = qkv_ref.shape[1:]
    patch = embed_ref.shape[0]
    if sliced:
        own, scale, shift = slice_ref[...], scale_ref[...], shift_ref[...]
    else:
        columns = pl.ds(pl.multiple_of(at_ref[0], 128), depth)
        own, scale, shift = embed_ref[:, columns], scale_ref[:, columns], shift_ref[:, columns]
    piece = 3 * heads_width // wide_count
    row_mean = jnp.mean(embed_ref[...].astype(f32), axis=1, keepdims=True)
    factor = (own.astype(f32) - row_mean) * (1.0 + scale)
    stacked = jnp.concatenate([factor, jnp.broadcast_to(shift, (16, depth))], axis=0)
    high, mid, _ = split3(stacked)
    bias_rows = []
    for part in range(3):
        weights = qkv_ref[part]
        product = jnp.dot(high, weights, preferred_element_type=f32) + jnp.dot(
            mid, weights, preferred_element_type=f32
        )
        for chunk in range(heads_width // 128):
            bias_rows.append(product[patch : patch + 1, chunk * 128 : (chunk + 1) * 128])
        turned = product[0:patch].T
        if part < 2:
            grouped = turned.reshape(heads_width // HEAD, HEAD, patch)
            grouped = grouped - jnp.mean(grouped, axis=1, keepdims=True)
            turned = grouped.reshape(turned.shape)
        turned = turned.astype(bf16)
        top = part * heads_width
        if sliced:
            out_refs[0][top : top + heads_width, :] = turned
            continue
        for receiver in range(wide_count):
            low = max(receiver * piece, top)
            end = min((receiver + 1) * piece, top + heads_width)
            if low < end:
                base = receiver * piece
                out_refs[0][receiver, low - base : end - base, :] = turned[low - top : end - top]
    bias_rows.append(jnp.zeros((16 - len(bias_rows), 128), f32))
    bias = jnp.concatenate(bias_rows, axis=0).astype(bf16)
    row_total = latents_ref.shape[0]
    share = row_total // wide_count
    across = targets_ref[...]
    same = lax.broadcasted_iota(jnp.int32, (row_total, row_total), 0) == lax.broadcasted_iota(
        jnp.int32, (row_total, row_total), 1
    )
    down = jnp.sum(jnp.where(same, across.astype(f32), 0.0), axis=1, keepdims=True)
    across = across.astype(f32)
    slot_across = jnp.sum((down < across).astype(f32), axis=0, keepdims=True)
    slot_down = jnp.sum((across < down).astype(f32), axis=1, keepdims=True)
    local = (down.astype(jnp.int32) % row_total).astype(f32)
    count = -(-SPAN * share // 16) * 16
    latents = latents_ref[...]
    wanted = lax.broadcasted_iota(jnp.int32, (count, row_total), 0)
    lane = lax.broadcasted_iota(jnp.int32, (row_total, 128), 1)
    for receiver in range(wide_count):
        first = (receiver - REACH) * share
        chosen = (slot_across == (wanted + first).astype(f32)) & (wanted < SPAN * share)
        rows = jnp.dot(chosen.astype(bf16), latents, preferred_element_type=f32).astype(bf16)
        mine = (slot_down == (lane + receiver * share).astype(f32)) & (lane < share)
        spots = jnp.sum(jnp.where(mine, local, 0.0), axis=0, keepdims=True)
        spots = jnp.broadcast_to(spots, (16, 128)).astype(bf16)
        if sliced:
            out_refs[1][receiver, 0:16, :] = bias
            out_refs[1][receiver, 16 : 16 + count, :] = rows
            out_refs[1][receiver, 16 + count :, :] = spots
        else:
            out_refs[0][receiver, piece : piece + 16, :] = bias
            out_refs[0][receiver, piece + 16 : piece + 16 + count, :] = rows
            out_refs[0][receiver, piece + 16 + count :, :] = spots


def project_kernel(
    row_total,
    tile_size,
    order_ref,
    patches_ref,
    weight_ref,
    bias_ref,
    gram_ref,
    keys_ref,
    values_ref,
    twin_ref,
    both_ref,
):
    heads_width = keys_ref.shape[0]
    local_heads = heads_width // HEAD
    pairs = heads_width // 128
    narrow_count = tile_size // row_total
    chunks = heads_width // 128

    def doubled(part):
        weight = weight_ref[part * heads_width : (part + 1) * heads_width, :]
        return jnp.concatenate([weight, weight], axis=1)

    def centred_bias(part):
        same = lax.broadcasted_iota(jnp.int32, (128, 128), 0) == lax.broadcasted_iota(
            jnp.int32, (128, 128), 1
        )
        pieces = []
        for chunk in range(chunks):
            row = bias_ref[part * chunks + chunk : part * chunks + chunk + 1, :]
            pieces.append(jnp.sum(jnp.where(same, row, 0.0), axis=1, keepdims=True))
        grouped = jnp.concatenate(pieces, axis=0).reshape(local_heads, HEAD, 1)
        grouped = grouped - jnp.mean(grouped, axis=1, keepdims=True)
        return grouped.reshape(heads_width, 1)

    def unit_heads(turned, bias):
        grouped = (turned + bias).reshape(local_heads, HEAD, turned.shape[1])
        square = jnp.mean(grouped * grouped, axis=1, keepdims=True)
        return (grouped * lax.rsqrt(square + EPSILON)).reshape(turned.shape)

    gram_top = jnp.concatenate([gram_ref[0], gram_ref[1]], axis=0)
    gram_low = gram_ref[2]

    def scale(step, carry):
        block = step // SPAN
        tile = step % SPAN
        rows = patches_ref[block, pl.ds(pl.multiple_of(tile * row_total, row_total), row_total), :]
        wide_rows = rows.astype(f32)
        image = jnp.dot(
            jnp.concatenate([rows, rows], axis=1), gram_top, preferred_element_type=f32
        ) + jnp.dot(rows, gram_low, preferred_element_type=f32)
        variance = jnp.sum(image * wide_rows, axis=1, keepdims=True)
        scaled = wide_rows * lax.rsqrt(jnp.maximum(variance, 0.0) + EPSILON)
        high = scaled.astype(bf16)
        at = pl.multiple_of(tile * tile_size + order_ref[block] * row_total, row_total)
        both_ref[pl.ds(at, row_total), 0:128] = high
        both_ref[pl.ds(at, row_total), 128:256] = (scaled - high.astype(f32)).astype(bf16)
        return carry

    lax.fori_loop(0, SPAN * narrow_count, scale, 0, unroll=SPAN)

    key_bias = centred_bias(1)
    key_weight = doubled(1)
    value_weight = doubled(2).astype(f32).T.astype(bf16)
    value_bias = jnp.concatenate(
        [bias_ref[2 * chunks + chunk : 2 * chunks + chunk + 1, :] for chunk in range(chunks)], axis=1
    )

    def project(step, carry):
        at = pl.multiple_of(step * 256, 256)
        both = both_ref[pl.ds(at, 256), :]
        keys_ref[:, pl.ds(at, 256)] = unit_heads(ntdot(key_weight, both), key_bias).astype(bf16)
        values_ref[pl.ds(at, 256), :] = (
            jnp.dot(both, value_weight, preferred_element_type=f32) + value_bias
        ).astype(bf16)
        return carry

    lax.fori_loop(0, SPAN * tile_size // 256, project, 0, unroll=2)

    query_bias = centred_bias(0)
    query_weight = doubled(0)
    left = lax.broadcasted_iota(jnp.int32, (QB, 128), 1) < HEAD
    spot_rows = row_total // 128

    def ask(block, carry):
        place = order_ref[block] * row_total
        spots = jnp.concatenate(
            [
                patches_ref[block, SPAN * row_total + row : SPAN * row_total + row + 1, :]
                for row in range(spot_rows)
            ],
            axis=1,
        )
        wanted = lax.broadcasted_iota(jnp.int32, (row_total, row_total), 0).astype(f32)
        chosen = (spots.astype(f32) == wanted).astype(bf16)
        both = both_ref[pl.ds(pl.multiple_of(REACH * tile_size + place, row_total), row_total), :]
        placed = jnp.dot(chosen, both, preferred_element_type=f32).astype(bf16)
        turned = unit_heads(ntdot(query_weight, placed), query_bias).astype(bf16).astype(f32) * 0.125
        rows = turned.T.astype(bf16)
        for part in range(row_total // QB):
            query = order_ref[block] * (row_total // QB) + part
            for pair in range(pairs):
                piece = rows[part * QB : (part + 1) * QB, pair * 128 : (pair + 1) * 128]
                twin_ref[query, pair, 0:QB, :] = jnp.where(left, piece, jnp.zeros_like(piece))
                twin_ref[query, pair, QB : 2 * QB, :] = jnp.where(left, jnp.zeros_like(piece), piece)
        return carry

    lax.fori_loop(0, narrow_count, ask, 0)


def attend_kernel(
    parts, entries, order_ref, starts_ref, counts_ref, keys_ref, values_ref, twin_ref, *rest
):
    out_refs = rest[:-6]
    total_ref, even_ref, odd_ref, block_ref, query_ref, first_ref = rest[-6:]
    pairs = twin_ref.shape[1]
    left = lax.broadcasted_iota(jnp.int32, (QB, 128), 1) < HEAD

    steps = jnp.int32(0)
    for index, (away, part) in enumerate(entries):
        total_ref[index] = jnp.zeros_like(total_ref[index])
        block = (order_ref[0] ^ away) * parts + part

        def note(slot, at, index=index, block=block):
            block_ref[at] = index
            query_ref[at] = block
            first_ref[at] = starts_ref[block * NB + slot]
            return at + 1

        steps = lax.fori_loop(0, counts_ref[block], note, steps)
    for extra in range(2):
        block_ref[steps + extra] = len(entries)
        query_ref[steps + extra] = query_ref[0]
        first_ref[steps + extra] = first_ref[0]

    ones = jnp.ones((KB, 128), bf16)

    def weigh(step, weights_ref):
        start = pl.multiple_of(first_ref[step], KB)
        query = query_ref[step]
        for pair in range(pairs):
            scores = jnp.dot(
                twin_ref[query, pair],
                keys_ref[pair * 128 : (pair + 1) * 128, pl.ds(start, KB)],
                preferred_element_type=f32,
            )
            weights_ref[pair] = jnp.exp(scores).astype(bf16)

    def gather(step, weights_ref):
        start = pl.multiple_of(first_ref[step], KB)
        block = block_ref[step]
        for pair in range(pairs):
            side = jnp.concatenate(
                [values_ref[pl.ds(start, KB), pair * 128 : (pair + 1) * 128], ones], axis=1
            )
            total_ref[block, pair] += jnp.dot(weights_ref[pair], side, preferred_element_type=f32)

    weigh(0, even_ref)

    def visit(twice, carry):
        step = twice * 2
        weigh(step + 1, odd_ref)
        gather(step, even_ref)
        weigh(step + 2, even_ref)
        gather(step + 1, odd_ref)
        return carry

    lax.fori_loop(0, (steps + 1) // 2, visit, 0)

    for index in range(len(entries)):
        for pair in range(pairs):
            both = total_ref[index, pair, :, 0:128] / total_ref[index, pair, :, 128:256]
            out_refs[index][:, pair * 128 : (pair + 1) * 128] = jnp.where(
                left, both[0:QB], both[QB : 2 * QB]
            ).astype(bf16)


def attend_scratch(entries, heads_width):
    pairs = heads_width // 128
    return [
        pltpu.VMEM((entries + 1, pairs, 2 * QB, 256), f32),
        pltpu.VMEM((pairs, 2 * QB, KB), bf16),
        pltpu.VMEM((pairs, 2 * QB, KB), bf16),
        pltpu.SMEM((entries * NB + 2,), jnp.int32),
        pltpu.SMEM((entries * NB + 2,), jnp.int32),
        pltpu.SMEM((entries * NB + 2,), jnp.int32),
    ]


def output_kernel(parts, narrow_count, together, order_ref, *refs):
    attended_refs = refs[: parts * narrow_count]
    weight_ref, gate_ref, out_ref = refs[parts * narrow_count :]
    rows = out_ref.shape[1] // together
    totals = [None] * together
    for away in range(narrow_count):
        attended = jnp.concatenate(
            [attended_refs[chunk * narrow_count + away][...] for chunk in range(parts)], axis=0
        )
        for index in range(together):
            at = pl.multiple_of((index * narrow_count + (order_ref[0] ^ away)) * rows, 16)
            term = ntdot(attended, weight_ref[pl.ds(at, rows), :])
            totals[index] = term if away == 0 else totals[index] + term
    for index, total in enumerate(totals):
        columns = slice(index * rows, (index + 1) * rows)
        out_ref[:, columns] = (total * gate_ref[:, columns]).astype(bf16)


def partial_kernel(kept, sent, held_ref, *refs):
    total = kept + sent
    outs = (kept > 0) + (sent > 0)
    attended_refs = refs[:total]
    weight_refs = refs[total:-outs]
    rows = weight_refs[0].shape[0] // 2
    for index, weight_ref in enumerate(weight_refs):
        first = held_ref[index]

        @pl.when(first >= 0)
        def _(first=first, weight_ref=weight_ref):
            attended = jnp.concatenate([ref[...] for ref in attended_refs], axis=0)
            product = ntdot(attended, weight_ref[...])
            for half in range(2):
                columns = pl.ds(pl.multiple_of((first ^ half) * rows, 128), rows)
                piece = product[:, half * rows : (half + 1) * rows]
                if kept:
                    refs[-outs][:, columns] = piece[: kept * QB]
                if sent:
                    refs[-1][:, columns] = piece[kept * QB :].astype(bf16)


def final_kernel(own_ref, first_ref, second_ref, third_ref, gate_ref, out_ref):
    far = jnp.concatenate([second_ref[...], third_ref[...]], axis=0).astype(f32)
    total = own_ref[...] + first_ref[...].astype(f32) + far
    out_ref[...] = (total * gate_ref[...]).astype(bf16)


def flip(block, axis, bit):
    devices = range(lax.axis_size(axis))
    return lax.ppermute(block, axis, [(i, i ^ bit) for i in devices])


def cost(flops, moved):
    return pl.CostEstimate(flops=flops, bytes_accessed=moved, transcendentals=0)


def gathered_rows(own):
    count = lax.axis_size("wide")
    index = lax.axis_index("wide")
    other = flip(own, "wide", 1)
    pair = jnp.concatenate([own, other], axis=0)
    blocks, held = [pair], [index]
    for sign in (1, -1):
        current = pair
        for step in range(1, count // 2):
            move = 2 * sign
            route = [
                (i, i + move)
                for i in range(count)
                if 0 <= i + move < count and 0 <= i - move * (step - 1) < count
            ]
            current = lax.ppermute(current, "wide", route)
            source = index - move * step
            blocks.append(current)
            held.append(jnp.where((source >= 0) & (source < count), source, -1))
    return blocks, jnp.stack(held).astype(jnp.int32)


def block(
    latents,
    targets,
    embed_weight,
    mod_shift,
    mod_scale,
    qkv_weight,
    out_weight,
    mod_gate,
    block_list,
    block_count,
):
    row_total, patch = latents.shape
    width = embed_weight.shape[1]
    wide_count = lax.axis_size("wide")
    narrow_count = lax.axis_size("narrow")
    wide_index = lax.axis_index("wide")
    narrow_index = lax.axis_index("narrow")
    tile_size = row_total * narrow_count
    depth, heads_width = qkv_weight.shape[1:]
    share = row_total // wide_count
    count = -(-SPAN * share // 16) * 16
    piece = 3 * heads_width // wide_count

    small = pltpu.CompilerParams(vmem_limit_bytes=SMALL_VMEM)
    chained = narrow_count == 4 and out_weight.shape[0] % 128 == 0 and row_total == 2 * QB
    if chained:
        blocks, held = gathered_rows(out_weight)
    else:
        out_all = lax.all_gather(out_weight, ("wide", "narrow"), axis=0, tiled=True)

    first = wide_index * depth
    extra = 16 + count + 16
    sliced = depth % 128 != 0 or piece % 16 != 0
    scale = mod_scale.reshape(1, width)
    shift = mod_shift.reshape(1, width)
    own = embed_weight
    if sliced:
        own, scale, shift = (
            lax.dynamic_slice_in_dim(array, first, depth, 1) for array in (own, scale, shift)
        )
        prep_shapes = (
            jax.ShapeDtypeStruct((3 * heads_width, patch), bf16),
            jax.ShapeDtypeStruct((wide_count, extra, patch), bf16),
        )
    else:
        prep_shapes = (jax.ShapeDtypeStruct((wide_count, piece + extra, patch), bf16),)
    smem = pl.BlockSpec(memory_space=pltpu.SMEM)
    prepare = pl.pallas_call(
        functools.partial(prep_kernel, wide_count, sliced),
        out_shape=prep_shapes,
        in_specs=[smem] + [whole_spec()] * 7,
        out_specs=tuple(whole_spec() for _ in prep_shapes),
        compiler_params=small,
        cost_estimate=cost(1 << 28, 4 << 20),
        name="prep",
    )
    prepared = prepare(
        first.astype(jnp.int32).reshape(1),
        embed_weight,
        own,
        scale,
        shift,
        qkv_weight,
        latents,
        targets.reshape(1, row_total),
    )
    payload = prepared[0]
    if sliced:
        payload = jnp.concatenate(
            [payload.reshape(wide_count, piece, patch), prepared[1]], axis=1
        )
    gram = pl.pallas_call(
        gram_kernel,
        out_shape=jax.ShapeDtypeStruct((3, patch, patch), bf16),
        in_specs=[whole_spec()],
        out_specs=whole_spec(),
        compiler_params=small,
        name="gram",
    )(embed_weight)
    arrived = lax.all_to_all(payload, "wide", split_axis=0, concat_axis=0, tiled=True)

    summed = jnp.sum(arrived[:, :piece].astype(f32), axis=0).astype(bf16)
    bias = jnp.sum(arrived[:, piece : piece + 16].astype(f32), axis=0)
    spread = jnp.broadcast_to(summed[None], (wide_count,) + summed.shape)
    near = arrived[:, piece + 16 : piece + 16 + SPAN * share]
    near = near.reshape(wide_count, SPAN, share, patch).transpose(1, 0, 2, 3)
    near = near.reshape(SPAN * row_total, patch)
    mine = arrived[:, piece + 16 + count, :share].reshape(-1)
    mine = jnp.pad(mine, (0, 16 * 128 - row_total)).reshape(16, 128)
    group = jnp.concatenate([near, mine], axis=0)[None]
    order = [0]
    bits = [1 << k for k in range(1, narrow_count.bit_length() - 1)] + [1]
    for bit in bits:
        other = flip(group, "narrow", bit)
        group = jnp.concatenate([group, other], axis=0)
        order = order + [index ^ bit for index in order]
    everything = lax.all_to_all(spread, "wide", split_axis=0, concat_axis=0, tiled=True)
    weight_all = everything.reshape(3 * heads_width, patch)

    order_ids = jnp.bitwise_xor(jnp.array(order, jnp.int32), narrow_index)
    starts = (block_list * KB - (wide_index - REACH) * tile_size).reshape(-1)
    parts = row_total // QB
    pairs = heads_width // 128
    keys, values, twin = pl.pallas_call(
        functools.partial(project_kernel, row_total, tile_size),
        out_shape=(
            pltpu.VMEM((heads_width, SPAN * tile_size), bf16),
            pltpu.VMEM((SPAN * tile_size, heads_width), bf16),
            pltpu.VMEM((tile_size // QB, pairs, 2 * QB, 128), bf16),
        ),
        in_specs=[smem] + [whole_spec()] * 4,
        out_specs=(whole_spec(),) * 3,
        scratch_shapes=[pltpu.VMEM((SPAN * tile_size, 256), bf16)],
        compiler_params=pltpu.CompilerParams(vmem_limit_bytes=PROJECT_VMEM),
        cost_estimate=cost(10 * SPAN * tile_size * patch * heads_width, 16 << 20),
        name="project",
    )(order_ids, group, weight_all, bias, gram)

    def attend(entries):
        return pl.pallas_call(
            functools.partial(attend_kernel, parts, entries),
            out_shape=(jax.ShapeDtypeStruct((QB, heads_width), bf16),) * len(entries),
            in_specs=[smem] * 3 + [whole_spec()] * 3,
            out_specs=(whole_spec(),) * len(entries),
            scratch_shapes=attend_scratch(len(entries), heads_width),
            compiler_params=pltpu.CompilerParams(vmem_limit_bytes=ATTEND_VMEM),
            cost_estimate=cost(4 * QB * len(entries) * NB * KB * heads_width, 16 << 20),
        )(order_ids, starts, block_count, keys, values, twin)

    if chained:
        gate = mod_gate.reshape(1, width)

        def multiply(attended, kept):
            sent = len(attended) - kept
            shapes = []
            if kept:
                shapes.append(jax.ShapeDtypeStruct((kept * QB, width), f32))
            if sent:
                shapes.append(jax.ShapeDtypeStruct((sent * QB, width), bf16))
            return pl.pallas_call(
                functools.partial(partial_kernel, kept, sent),
                out_shape=tuple(shapes),
                in_specs=[smem] + [whole_spec()] * (len(attended) + len(blocks)),
                out_specs=(whole_spec(),) * len(shapes),
                compiler_params=small,
                cost_estimate=cost(2 * len(attended) * QB * heads_width * width, 8 << 20),
            )(held, *attended, *blocks)

        far = []
        for part in range(parts):
            attended = attend(((2, part), (3, part)))
            keep, send = multiply(attended, 1)
            other = flip(send, "narrow", 1)
            joined = (keep + other.astype(f32)).astype(bf16)
            far.append(flip(joined, "narrow", 2))
        (send,) = multiply(attend(((1, 0), (1, 1))), 0)
        other = flip(send, "narrow", 1)
        (own,) = multiply(attend(((0, 0), (0, 1))), parts)
        return pl.pallas_call(
            final_kernel,
            out_shape=jax.ShapeDtypeStruct((row_total, width), bf16),
            in_specs=[whole_spec()] * 5,
            out_specs=whole_spec(),
            compiler_params=small,
            name="final",
        )(own, other, *far, gate)

    pieces = []
    for chunk in range(parts):
        mine = attend(tuple((away, chunk) for away in range(narrow_count)))
        pieces.append(mine[0])
        for away in range(1, narrow_count):
            pieces.append(flip(mine[away], "narrow", away))

    out_rows = out_weight.shape[0]
    gate = mod_gate.reshape(1, width)
    if out_rows % 128 == 0:
        together = 2 if wide_count % 2 == 0 else 1
        span = together * out_rows
        return pl.pallas_call(
            functools.partial(output_kernel, parts, narrow_count, together),
            grid=(wide_count // together,),
            out_shape=jax.ShapeDtypeStruct((row_total, width), bf16),
            in_specs=[smem]
            + [pl.BlockSpec((QB, heads_width), lambda i: (0, 0))] * (parts * narrow_count)
            + [
                pl.BlockSpec((narrow_count * span, heads_width), lambda i: (i, 0)),
                pl.BlockSpec((1, span), lambda i: (0, i)),
            ],
            out_specs=pl.BlockSpec((row_total, span), lambda i: (0, i)),
            compiler_params=pltpu.CompilerParams(vmem_limit_bytes=OUTPUT_VMEM),
            name="output",
        )(order_ids, *pieces, out_all, gate)
    weights = out_all.reshape(wide_count, narrow_count, out_rows, heads_width)
    product = 0.0
    for away in range(narrow_count):
        attended = jnp.concatenate(pieces[away::narrow_count], axis=0)
        weight = lax.dynamic_index_in_dim(weights, narrow_index ^ away, 1, False)
        product = product + jnp.einsum(
            "tk,wfk->twf", attended, weight, preferred_element_type=f32
        )
    return (gate * product.reshape(row_total, width)).astype(bf16)


def solution(mesh):
    in_specs = (
        P(("wide", "narrow"), None),
        P(("wide", "narrow")),
        P(),
        P(),
        P(),
        P(None, "wide", "narrow"),
        P("wide", "narrow"),
        P(),
        P("wide", None),
        P("wide"),
    )
    out_specs = P(("wide", "narrow"), None)
    return jax.shard_map(block, mesh=mesh, in_specs=in_specs, out_specs=out_specs, check_vma=False)
```

```python
import functools

import jax
import jax.numpy as jnp
from jax import lax
from jax.experimental import pallas as pl
from jax.experimental.pallas import tpu as pltpu
from jax.sharding import PartitionSpec as P


HEAD = 64
NB = 8
KB = 512
QB = 128
REACH = 2
SPAN = 2 * REACH + 1
EPSILON = 1e-06
PROJECT_VMEM = 19 << 20
ATTEND_VMEM = 11 << 20
OUTPUT_VMEM = 53 << 20
SMALL_VMEM = 11 << 20

f32 = jnp.float32
bf16 = jnp.bfloat16
NT = (((1,), (1,)), ((), ()))


def ntdot(a, b):
    return lax.dot_general(a, b, NT, preferred_element_type=f32)


def whole_spec():
    return pl.BlockSpec(memory_space=pltpu.VMEM)


def split3(value):
    high = value.astype(bf16)
    rest = value - high.astype(f32)
    mid = rest.astype(bf16)
    low = (rest - mid.astype(f32)).astype(bf16)
    return high, mid, low


def gram_kernel(embed_ref, gram_ref):
    embed = embed_ref[...].astype(f32)
    width = embed.shape[1]
    centred = embed - jnp.mean(embed, axis=1, keepdims=True)
    gram = lax.dot_general(
        centred, centred, NT, preferred_element_type=f32, precision=lax.Precision.HIGHEST
    ) * (1.0 / width)
    for index, term in enumerate(split3(gram)):
        gram_ref[index] = term


def prep_kernel(
    wide_count,
    sliced,
    at_ref,
    embed_ref,
    slice_ref,
    scale_ref,
    shift_ref,
    qkv_ref,
    latents_ref,
    targets_ref,
    *out_refs,
):
    depth, heads_width = qkv_ref.shape[1:]
    patch = embed_ref.shape[0]
    if sliced:
        own, scale, shift = slice_ref[...], scale_ref[...], shift_ref[...]
    else:
        columns = pl.ds(pl.multiple_of(at_ref[0], 128), depth)
        own, scale, shift = embed_ref[:, columns], scale_ref[:, columns], shift_ref[:, columns]
    piece = 3 * heads_width // wide_count
    row_mean = jnp.mean(embed_ref[...].astype(f32), axis=1, keepdims=True)
    factor = (own.astype(f32) - row_mean) * (1.0 + scale)
    stacked = jnp.concatenate([factor, jnp.broadcast_to(shift, (16, depth))], axis=0)
    high, mid, _ = split3(stacked)
    bias_rows = []
    for part in range(3):
        weights = qkv_ref[part]
        product = jnp.dot(high, weights, preferred_element_type=f32) + jnp.dot(
            mid, weights, preferred_element_type=f32
        )
        for chunk in range(heads_width // 128):
            bias_rows.append(product[patch : patch + 1, chunk * 128 : (chunk + 1) * 128])
        turned = product[0:patch].T
        if part < 2:
            grouped = turned.reshape(heads_width // HEAD, HEAD, patch)
            grouped = grouped - jnp.mean(grouped, axis=1, keepdims=True)
            turned = grouped.reshape(turned.shape)
        turned = turned.astype(bf16)
        top = part * heads_width
        if sliced:
            out_refs[0][top : top + heads_width, :] = turned
            continue
        for receiver in range(wide_count):
            low = max(receiver * piece, top)
            end = min((receiver + 1) * piece, top + heads_width)
            if low < end:
                base = receiver * piece
                out_refs[0][receiver, low - base : end - base, :] = turned[low - top : end - top]
    bias_rows.append(jnp.zeros((16 - len(bias_rows), 128), f32))
    bias = jnp.concatenate(bias_rows, axis=0).astype(bf16)
    row_total = latents_ref.shape[0]
    share = row_total // wide_count
    across = targets_ref[...]
    same = lax.broadcasted_iota(jnp.int32, (row_total, row_total), 0) == lax.broadcasted_iota(
        jnp.int32, (row_total, row_total), 1
    )
    down = jnp.sum(jnp.where(same, across.astype(f32), 0.0), axis=1, keepdims=True)
    across = across.astype(f32)
    slot_across = jnp.sum((down < across).astype(f32), axis=0, keepdims=True)
    slot_down = jnp.sum((across < down).astype(f32), axis=1, keepdims=True)
    local = (down.astype(jnp.int32) % row_total).astype(f32)
    count = -(-SPAN * share // 16) * 16
    latents = latents_ref[...]
    wanted = lax.broadcasted_iota(jnp.int32, (count, row_total), 0)
    lane = lax.broadcasted_iota(jnp.int32, (row_total, 128), 1)
    for receiver in range(wide_count):
        first = (receiver - REACH) * share
        chosen = (slot_across == (wanted + first).astype(f32)) & (wanted < SPAN * share)
        rows = jnp.dot(chosen.astype(bf16), latents, preferred_element_type=f32).astype(bf16)
        mine = (slot_down == (lane + receiver * share).astype(f32)) & (lane < share)
        spots = jnp.sum(jnp.where(mine, local, 0.0), axis=0, keepdims=True)
        spots = jnp.broadcast_to(spots, (16, 128)).astype(bf16)
        if sliced:
            out_refs[1][receiver, 0:16, :] = bias
            out_refs[1][receiver, 16 : 16 + count, :] = rows
            out_refs[1][receiver, 16 + count :, :] = spots
        else:
            out_refs[0][receiver, piece : piece + 16, :] = bias
            out_refs[0][receiver, piece + 16 : piece + 16 + count, :] = rows
            out_refs[0][receiver, piece + 16 + count :, :] = spots


def project_kernel(
    row_total,
    tile_size,
    order_ref,
    patches_ref,
    weight_ref,
    bias_ref,
    gram_ref,
    keys_ref,
    values_ref,
    twin_ref,
    both_ref,
):
    heads_width = keys_ref.shape[0]
    local_heads = heads_width // HEAD
    pairs = heads_width // 128
    narrow_count = tile_size // row_total
    chunks = heads_width // 128

    def doubled(part):
        weight = weight_ref[part * heads_width : (part + 1) * heads_width, :]
        return jnp.concatenate([weight, weight], axis=1)

    def centred_bias(part):
        same = lax.broadcasted_iota(jnp.int32, (128, 128), 0) == lax.broadcasted_iota(
            jnp.int32, (128, 128), 1
        )
        pieces = []
        for chunk in range(chunks):
            row = bias_ref[part * chunks + chunk : part * chunks + chunk + 1, :]
            pieces.append(jnp.sum(jnp.where(same, row, 0.0), axis=1, keepdims=True))
        grouped = jnp.concatenate(pieces, axis=0).reshape(local_heads, HEAD, 1)
        grouped = grouped - jnp.mean(grouped, axis=1, keepdims=True)
        return grouped.reshape(heads_width, 1)

    def unit_heads(turned, bias):
        grouped = (turned + bias).reshape(local_heads, HEAD, turned.shape[1])
        square = jnp.mean(grouped * grouped, axis=1, keepdims=True)
        return (grouped * lax.rsqrt(square + EPSILON)).reshape(turned.shape)

    gram_top = jnp.concatenate([gram_ref[0], gram_ref[1]], axis=0)
    gram_low = gram_ref[2]

    def scale(step, carry):
        block = step // SPAN
        tile = step % SPAN
        rows = patches_ref[block, pl.ds(pl.multiple_of(tile * row_total, row_total), row_total), :]
        wide_rows = rows.astype(f32)
        image = jnp.dot(
            jnp.concatenate([rows, rows], axis=1), gram_top, preferred_element_type=f32
        ) + jnp.dot(rows, gram_low, preferred_element_type=f32)
        variance = jnp.sum(image * wide_rows, axis=1, keepdims=True)
        scaled = wide_rows * lax.rsqrt(jnp.maximum(variance, 0.0) + EPSILON)
        high = scaled.astype(bf16)
        at = pl.multiple_of(tile * tile_size + order_ref[block] * row_total, row_total)
        both_ref[pl.ds(at, row_total), 0:128] = high
        both_ref[pl.ds(at, row_total), 128:256] = (scaled - high.astype(f32)).astype(bf16)
        return carry

    lax.fori_loop(0, SPAN * narrow_count, scale, 0, unroll=SPAN)

    key_bias = centred_bias(1)
    key_weight = doubled(1)
    value_weight = doubled(2).astype(f32).T.astype(bf16)
    value_bias = jnp.concatenate(
        [bias_ref[2 * chunks + chunk : 2 * chunks + chunk + 1, :] for chunk in range(chunks)], axis=1
    )

    def project(step, carry):
        at = pl.multiple_of(step * 256, 256)
        both = both_ref[pl.ds(at, 256), :]
        keys_ref[:, pl.ds(at, 256)] = unit_heads(ntdot(key_weight, both), key_bias).astype(bf16)
        values_ref[pl.ds(at, 256), :] = (
            jnp.dot(both, value_weight, preferred_element_type=f32) + value_bias
        ).astype(bf16)
        return carry

    lax.fori_loop(0, SPAN * tile_size // 256, project, 0, unroll=2)

    query_bias = centred_bias(0)
    query_weight = doubled(0)
    left = lax.broadcasted_iota(jnp.int32, (QB, 128), 1) < HEAD
    spot_rows = row_total // 128

    def ask(block, carry):
        place = order_ref[block] * row_total
        spots = jnp.concatenate(
            [
                patches_ref[block, SPAN * row_total + row : SPAN * row_total + row + 1, :]
                for row in range(spot_rows)
            ],
            axis=1,
        )
        wanted = lax.broadcasted_iota(jnp.int32, (row_total, row_total), 0).astype(f32)
        chosen = (spots.astype(f32) == wanted).astype(bf16)
        both = both_ref[pl.ds(pl.multiple_of(REACH * tile_size + place, row_total), row_total), :]
        placed = jnp.dot(chosen, both, preferred_element_type=f32).astype(bf16)
        turned = unit_heads(ntdot(query_weight, placed), query_bias).astype(bf16).astype(f32) * 0.125
        rows = turned.T.astype(bf16)
        for part in range(row_total // QB):
            query = order_ref[block] * (row_total // QB) + part
            for pair in range(pairs):
                piece = rows[part * QB : (part + 1) * QB, pair * 128 : (pair + 1) * 128]
                twin_ref[query, pair, 0:QB, :] = jnp.where(left, piece, jnp.zeros_like(piece))
                twin_ref[query, pair, QB : 2 * QB, :] = jnp.where(left, jnp.zeros_like(piece), piece)
        return carry

    lax.fori_loop(0, narrow_count, ask, 0)


def attend_kernel(
    parts, entries, order_ref, starts_ref, counts_ref, keys_ref, values_ref, twin_ref, *rest
):
    out_refs = rest[:-6]
    total_ref, even_ref, odd_ref, block_ref, query_ref, first_ref = rest[-6:]
    pairs = twin_ref.shape[1]
    left = lax.broadcasted_iota(jnp.int32, (QB, 128), 1) < HEAD

    steps = jnp.int32(0)
    for index, (away, part) in enumerate(entries):
        total_ref[index] = jnp.zeros_like(total_ref[index])
        block = (order_ref[0] ^ away) * parts + part

        def note(slot, at, index=index, block=block):
            block_ref[at] = index
            query_ref[at] = block
            first_ref[at] = starts_ref[block * NB + slot]
            return at + 1

        steps = lax.fori_loop(0, counts_ref[block], note, steps)
    for extra in range(2):
        block_ref[steps + extra] = len(entries)
        query_ref[steps + extra] = query_ref[0]
        first_ref[steps + extra] = first_ref[0]

    ones = jnp.ones((KB, 128), bf16)

    def weigh(step, weights_ref):
        start = pl.multiple_of(first_ref[step], KB)
        query = query_ref[step]
        for pair in range(pairs):
            scores = jnp.dot(
                twin_ref[query, pair],
                keys_ref[pair * 128 : (pair + 1) * 128, pl.ds(start, KB)],
                preferred_element_type=f32,
            )
            weights_ref[pair] = jnp.exp(scores).astype(bf16)

    def gather(step, weights_ref):
        start = pl.multiple_of(first_ref[step], KB)
        block = block_ref[step]
        for pair in range(pairs):
            side = jnp.concatenate(
                [values_ref[pl.ds(start, KB), pair * 128 : (pair + 1) * 128], ones], axis=1
            )
            total_ref[block, pair] += jnp.dot(weights_ref[pair], side, preferred_element_type=f32)

    weigh(0, even_ref)

    def visit(twice, carry):
        step = twice * 2
        weigh(step + 1, odd_ref)
        gather(step, even_ref)
        weigh(step + 2, even_ref)
        gather(step + 1, odd_ref)
        return carry

    lax.fori_loop(0, (steps + 1) // 2, visit, 0)

    for index in range(len(entries)):
        for pair in range(pairs):
            both = total_ref[index, pair, :, 0:128] / total_ref[index, pair, :, 128:256]
            out_refs[index][:, pair * 128 : (pair + 1) * 128] = jnp.where(
                left, both[0:QB], both[QB : 2 * QB]
            ).astype(bf16)


def attend_scratch(entries, heads_width):
    pairs = heads_width // 128
    return [
        pltpu.VMEM((entries + 1, pairs, 2 * QB, 256), f32),
        pltpu.VMEM((pairs, 2 * QB, KB), bf16),
        pltpu.VMEM((pairs, 2 * QB, KB), bf16),
        pltpu.SMEM((entries * NB + 2,), jnp.int32),
        pltpu.SMEM((entries * NB + 2,), jnp.int32),
        pltpu.SMEM((entries * NB + 2,), jnp.int32),
    ]


def output_kernel(parts, narrow_count, together, order_ref, *refs):
    attended_refs = refs[: parts * narrow_count]
    weight_ref, gate_ref, out_ref = refs[parts * narrow_count :]
    rows = out_ref.shape[1] // together
    totals = [None] * together
    for away in range(narrow_count):
        attended = jnp.concatenate(
            [attended_refs[chunk * narrow_count + away][...] for chunk in range(parts)], axis=0
        )
        for index in range(together):
            at = pl.multiple_of((index * narrow_count + (order_ref[0] ^ away)) * rows, 16)
            term = ntdot(attended, weight_ref[pl.ds(at, rows), :])
            totals[index] = term if away == 0 else totals[index] + term
    for index, total in enumerate(totals):
        columns = slice(index * rows, (index + 1) * rows)
        out_ref[:, columns] = (total * gate_ref[:, columns]).astype(bf16)


def partial_kernel(kept, sent, held_ref, *refs):
    total = kept + sent
    outs = (kept > 0) + (sent > 0)
    attended_refs = refs[:total]
    weight_refs = refs[total:-outs]
    rows = weight_refs[0].shape[0]
    for index, weight_ref in enumerate(weight_refs):

        @pl.when(held_ref[index] >= 0)
        def _(index=index, weight_ref=weight_ref):
            attended = jnp.concatenate([ref[...] for ref in attended_refs], axis=0)
            product = ntdot(attended, weight_ref[...])
            columns = pl.ds(pl.multiple_of(held_ref[index] * rows, 128), rows)
            if kept:
                refs[-outs][:, columns] = product[: kept * QB]
            if sent:
                refs[-1][:, columns] = product[kept * QB :].astype(bf16)


def final_kernel(own_ref, first_ref, second_ref, third_ref, gate_ref, out_ref):
    far = jnp.concatenate([second_ref[...], third_ref[...]], axis=0).astype(f32)
    total = own_ref[...] + first_ref[...].astype(f32) + far
    out_ref[...] = (total * gate_ref[...]).astype(bf16)


def flip(block, axis, bit):
    devices = range(lax.axis_size(axis))
    return lax.ppermute(block, axis, [(i, i ^ bit) for i in devices])


def cost(flops, moved):
    return pl.CostEstimate(flops=flops, bytes_accessed=moved, transcendentals=0)


def gathered_rows(own):
    count = lax.axis_size("wide")
    index = lax.axis_index("wide")
    length = count // 2
    blocks, held = [own], [index]
    blocks.append(lax.ppermute(own, "wide", [(i, i ^ 1) for i in range(count)]))
    held.append(index ^ 1)
    for sign in (1, -1):
        current = own
        for step in range(1, length):
            move = 2 * sign
            route = [
                (i, i + move)
                for i in range(count)
                if 0 <= i + move < count and 0 <= i - move * (step - 1) < count
            ]
            current = lax.ppermute(current, "wide", route)
            source = index - move * step
            valid = (source >= 0) & (source < count)
            blocks.append(current)
            held.append(jnp.where(valid, source, -1))
            swap = [(i, i ^ 1) for i in range(count) if 0 <= i - move * step < count]
            blocks.append(lax.ppermute(current, "wide", swap))
            held.append(jnp.where(valid, source ^ 1, -1))
    return blocks, jnp.stack(held).astype(jnp.int32)


def block(
    latents,
    targets,
    embed_weight,
    mod_shift,
    mod_scale,
    qkv_weight,
    out_weight,
    mod_gate,
    block_list,
    block_count,
):
    row_total, patch = latents.shape
    width = embed_weight.shape[1]
    wide_count = lax.axis_size("wide")
    narrow_count = lax.axis_size("narrow")
    wide_index = lax.axis_index("wide")
    narrow_index = lax.axis_index("narrow")
    tile_size = row_total * narrow_count
    depth, heads_width = qkv_weight.shape[1:]
    share = row_total // wide_count
    count = -(-SPAN * share // 16) * 16
    piece = 3 * heads_width // wide_count

    small = pltpu.CompilerParams(vmem_limit_bytes=SMALL_VMEM)
    chained = narrow_count == 4 and out_weight.shape[0] % 128 == 0 and row_total == 2 * QB
    if chained:
        blocks, held = gathered_rows(out_weight)
    else:
        out_all = lax.all_gather(out_weight, ("wide", "narrow"), axis=0, tiled=True)

    first = wide_index * depth
    extra = 16 + count + 16
    sliced = depth % 128 != 0 or piece % 16 != 0
    scale = mod_scale.reshape(1, width)
    shift = mod_shift.reshape(1, width)
    own = embed_weight
    if sliced:
        own, scale, shift = (
            lax.dynamic_slice_in_dim(array, first, depth, 1) for array in (own, scale, shift)
        )
        prep_shapes = (
            jax.ShapeDtypeStruct((3 * heads_width, patch), bf16),
            jax.ShapeDtypeStruct((wide_count, extra, patch), bf16),
        )
    else:
        prep_shapes = (jax.ShapeDtypeStruct((wide_count, piece + extra, patch), bf16),)
    smem = pl.BlockSpec(memory_space=pltpu.SMEM)
    prepare = pl.pallas_call(
        functools.partial(prep_kernel, wide_count, sliced),
        out_shape=prep_shapes,
        in_specs=[smem] + [whole_spec()] * 7,
        out_specs=tuple(whole_spec() for _ in prep_shapes),
        cost_estimate=cost(1 << 28, 4 << 20),
        name="prep",
    )
    prepared = prepare(
        first.astype(jnp.int32).reshape(1),
        embed_weight,
        own,
        scale,
        shift,
        qkv_weight,
        latents,
        targets.reshape(1, row_total),
    )
    payload = prepared[0]
    if sliced:
        payload = jnp.concatenate(
            [payload.reshape(wide_count, piece, patch), prepared[1]], axis=1
        )
    gram = pl.pallas_call(
        gram_kernel,
        out_shape=jax.ShapeDtypeStruct((3, patch, patch), bf16),
        in_specs=[whole_spec()],
        out_specs=whole_spec(),
        compiler_params=small,
        name="gram",
    )(embed_weight)
    arrived = lax.all_to_all(payload, "wide", split_axis=0, concat_axis=0, tiled=True)

    summed = jnp.sum(arrived[:, :piece].astype(f32), axis=0).astype(bf16)
    bias = jnp.sum(arrived[:, piece : piece + 16].astype(f32), axis=0)
    spread = jnp.broadcast_to(summed[None], (wide_count,) + summed.shape)
    near = arrived[:, piece + 16 : piece + 16 + SPAN * share]
    near = near.reshape(wide_count, SPAN, share, patch).transpose(1, 0, 2, 3)
    near = near.reshape(SPAN * row_total, patch)
    mine = arrived[:, piece + 16 + count, :share].reshape(-1)
    mine = jnp.pad(mine, (0, 16 * 128 - row_total)).reshape(16, 128)
    group = jnp.concatenate([near, mine], axis=0)[None]
    order = [0]
    bits = [1 << k for k in range(1, narrow_count.bit_length() - 1)] + [1]
    for bit in bits:
        other = flip(group, "narrow", bit)
        group = jnp.concatenate([group, other], axis=0)
        order = order + [index ^ bit for index in order]
    everything = lax.all_to_all(spread, "wide", split_axis=0, concat_axis=0, tiled=True)
    weight_all = everything.reshape(3 * heads_width, patch)

    order_ids = jnp.bitwise_xor(jnp.array(order, jnp.int32), narrow_index)
    starts = (block_list * KB - (wide_index - REACH) * tile_size).reshape(-1)
    parts = row_total // QB
    pairs = heads_width // 128
    keys, values, twin = pl.pallas_call(
        functools.partial(project_kernel, row_total, tile_size),
        out_shape=(
            pltpu.VMEM((heads_width, SPAN * tile_size), bf16),
            pltpu.VMEM((SPAN * tile_size, heads_width), bf16),
            pltpu.VMEM((tile_size // QB, pairs, 2 * QB, 128), bf16),
        ),
        in_specs=[smem] + [whole_spec()] * 4,
        out_specs=(whole_spec(),) * 3,
        scratch_shapes=[pltpu.VMEM((SPAN * tile_size, 256), bf16)],
        compiler_params=pltpu.CompilerParams(vmem_limit_bytes=PROJECT_VMEM),
        cost_estimate=cost(10 * SPAN * tile_size * patch * heads_width, 16 << 20),
        name="project",
    )(order_ids, group, weight_all, bias, gram)

    def attend(entries):
        return pl.pallas_call(
            functools.partial(attend_kernel, parts, entries),
            out_shape=(jax.ShapeDtypeStruct((QB, heads_width), bf16),) * len(entries),
            in_specs=[smem] * 3 + [whole_spec()] * 3,
            out_specs=(whole_spec(),) * len(entries),
            scratch_shapes=attend_scratch(len(entries), heads_width),
            compiler_params=pltpu.CompilerParams(vmem_limit_bytes=ATTEND_VMEM),
            cost_estimate=cost(4 * QB * len(entries) * NB * KB * heads_width, 16 << 20),
        )(order_ids, starts, block_count, keys, values, twin)

    if chained:
        gate = mod_gate.reshape(1, width)

        def multiply(attended, kept):
            sent = len(attended) - kept
            shapes = []
            if kept:
                shapes.append(jax.ShapeDtypeStruct((kept * QB, width), f32))
            if sent:
                shapes.append(jax.ShapeDtypeStruct((sent * QB, width), bf16))
            return pl.pallas_call(
                functools.partial(partial_kernel, kept, sent),
                out_shape=tuple(shapes),
                in_specs=[smem] + [whole_spec()] * (len(attended) + len(blocks)),
                out_specs=(whole_spec(),) * len(shapes),
                compiler_params=small,
                cost_estimate=cost(2 * len(attended) * QB * heads_width * width, 8 << 20),
            )(held, *attended, *blocks)

        far = []
        for part in range(parts):
            attended = attend(((2, part), (3, part)))
            keep, send = multiply(attended, 1)
            other = flip(send, "narrow", 1)
            joined = (keep + other.astype(f32)).astype(bf16)
            far.append(flip(joined, "narrow", 2))
        (send,) = multiply(attend(((1, 0), (1, 1))), 0)
        other = flip(send, "narrow", 1)
        (own,) = multiply(attend(((0, 0), (0, 1))), parts)
        return pl.pallas_call(
            final_kernel,
            out_shape=jax.ShapeDtypeStruct((row_total, width), bf16),
            in_specs=[whole_spec()] * 5,
            out_specs=whole_spec(),
            compiler_params=small,
            name="final",
        )(own, other, *far, gate)

    pieces = []
    for chunk in range(parts):
        mine = attend(tuple((away, chunk) for away in range(narrow_count)))
        pieces.append(mine[0])
        for away in range(1, narrow_count):
            pieces.append(flip(mine[away], "narrow", away))

    out_rows = out_weight.shape[0]
    gate = mod_gate.reshape(1, width)
    if out_rows % 128 == 0:
        together = 2 if wide_count % 2 == 0 else 1
        span = together * out_rows
        return pl.pallas_call(
            functools.partial(output_kernel, parts, narrow_count, together),
            grid=(wide_count // together,),
            out_shape=jax.ShapeDtypeStruct((row_total, width), bf16),
            in_specs=[smem]
            + [pl.BlockSpec((QB, heads_width), lambda i: (0, 0))] * (parts * narrow_count)
            + [
                pl.BlockSpec((narrow_count * span, heads_width), lambda i: (i, 0)),
                pl.BlockSpec((1, span), lambda i: (0, i)),
            ],
            out_specs=pl.BlockSpec((row_total, span), lambda i: (0, i)),
            compiler_params=pltpu.CompilerParams(vmem_limit_bytes=OUTPUT_VMEM),
            name="output",
        )(order_ids, *pieces, out_all, gate)
    weights = out_all.reshape(wide_count, narrow_count, out_rows, heads_width)
    product = 0.0
    for away in range(narrow_count):
        attended = jnp.concatenate(pieces[away::narrow_count], axis=0)
        weight = lax.dynamic_index_in_dim(weights, narrow_index ^ away, 1, False)
        product = product + jnp.einsum(
            "tk,wfk->twf", attended, weight, preferred_element_type=f32
        )
    return (gate * product.reshape(row_total, width)).astype(bf16)


def solution(mesh):
    in_specs = (
        P(("wide", "narrow"), None),
        P(("wide", "narrow")),
        P(),
        P(),
        P(),
        P(None, "wide", "narrow"),
        P("wide", "narrow"),
        P(),
        P("wide", None),
        P("wide"),
    )
    out_specs = P(("wide", "narrow"), None)
    return jax.shard_map(block, mesh=mesh, in_specs=in_specs, out_specs=out_specs, check_vma=False)
```

```python
import functools

import jax
import jax.numpy as jnp
from jax import lax
from jax.experimental import pallas as pl
from jax.experimental.pallas import tpu as pltpu
from jax.sharding import PartitionSpec as P


HEAD = 64
NB = 8
KB = 512
QB = 128
REACH = 2
SPAN = 2 * REACH + 1
EPSILON = 1e-06
PROJECT_VMEM = 19 << 20
ATTEND_VMEM = 11 << 20
OUTPUT_VMEM = 53 << 20
SMALL_VMEM = 11 << 20

f32 = jnp.float32
bf16 = jnp.bfloat16
NT = (((1,), (1,)), ((), ()))


def ntdot(a, b):
    return lax.dot_general(a, b, NT, preferred_element_type=f32)


def whole_spec():
    return pl.BlockSpec(memory_space=pltpu.VMEM)


def split3(value):
    high = value.astype(bf16)
    rest = value - high.astype(f32)
    mid = rest.astype(bf16)
    low = (rest - mid.astype(f32)).astype(bf16)
    return high, mid, low


def gram_kernel(embed_ref, gram_ref):
    embed = embed_ref[...].astype(f32)
    width = embed.shape[1]
    centred = embed - jnp.mean(embed, axis=1, keepdims=True)
    gram = lax.dot_general(
        centred, centred, NT, preferred_element_type=f32, precision=lax.Precision.HIGHEST
    ) * (1.0 / width)
    for index, term in enumerate(split3(gram)):
        gram_ref[index] = term


def prep_kernel(
    wide_count,
    sliced,
    at_ref,
    embed_ref,
    slice_ref,
    scale_ref,
    shift_ref,
    qkv_ref,
    latents_ref,
    targets_ref,
    *out_refs,
):
    depth, heads_width = qkv_ref.shape[1:]
    patch = embed_ref.shape[0]
    if sliced:
        own, scale, shift = slice_ref[...], scale_ref[...], shift_ref[...]
    else:
        columns = pl.ds(pl.multiple_of(at_ref[0], 128), depth)
        own, scale, shift = embed_ref[:, columns], scale_ref[:, columns], shift_ref[:, columns]
    piece = 3 * heads_width // wide_count
    row_mean = jnp.mean(embed_ref[...].astype(f32), axis=1, keepdims=True)
    factor = (own.astype(f32) - row_mean) * (1.0 + scale)
    stacked = jnp.concatenate([factor, jnp.broadcast_to(shift, (16, depth))], axis=0)
    high, mid, _ = split3(stacked)
    bias_rows = []
    for part in range(3):
        weights = qkv_ref[part]
        product = jnp.dot(high, weights, preferred_element_type=f32) + jnp.dot(
            mid, weights, preferred_element_type=f32
        )
        for chunk in range(heads_width // 128):
            bias_rows.append(product[patch : patch + 1, chunk * 128 : (chunk + 1) * 128])
        turned = product[0:patch].T
        if part < 2:
            grouped = turned.reshape(heads_width // HEAD, HEAD, patch)
            grouped = grouped - jnp.mean(grouped, axis=1, keepdims=True)
            turned = grouped.reshape(turned.shape)
        turned = turned.astype(bf16)
        top = part * heads_width
        if sliced:
            out_refs[0][top : top + heads_width, :] = turned
            continue
        for receiver in range(wide_count):
            low = max(receiver * piece, top)
            end = min((receiver + 1) * piece, top + heads_width)
            if low < end:
                base = receiver * piece
                out_refs[0][receiver, low - base : end - base, :] = turned[low - top : end - top]
    bias_rows.append(jnp.zeros((16 - len(bias_rows), 128), f32))
    bias = jnp.concatenate(bias_rows, axis=0).astype(bf16)
    row_total = latents_ref.shape[0]
    share = row_total // wide_count
    across = targets_ref[...]
    same = lax.broadcasted_iota(jnp.int32, (row_total, row_total), 0) == lax.broadcasted_iota(
        jnp.int32, (row_total, row_total), 1
    )
    down = jnp.sum(jnp.where(same, across.astype(f32), 0.0), axis=1, keepdims=True)
    across = across.astype(f32)
    slot_across = jnp.sum((down < across).astype(f32), axis=0, keepdims=True)
    slot_down = jnp.sum((across < down).astype(f32), axis=1, keepdims=True)
    local = (down.astype(jnp.int32) % row_total).astype(f32)
    count = -(-SPAN * share // 16) * 16
    latents = latents_ref[...]
    wanted = lax.broadcasted_iota(jnp.int32, (count, row_total), 0)
    spot_rows = -(-row_total // 128)
    lane = lax.broadcasted_iota(jnp.int32, (row_total, 128), 1)
    for receiver in range(wide_count):
        first = (receiver - REACH) * share
        chosen = (slot_across == (wanted + first).astype(f32)) & (wanted < SPAN * share)
        rows = jnp.dot(chosen.astype(bf16), latents, preferred_element_type=f32).astype(bf16)
        lines = []
        for line in range(spot_rows):
            place = lane + (line * 128 - at_ref[1])
            mine = (slot_down == (place + receiver * share).astype(f32)) & (
                (place >= 0) & (place < share)
            )
            lines.append(jnp.sum(jnp.where(mine, local, 0.0), axis=0, keepdims=True))
        lines.append(jnp.zeros((16 - spot_rows, 128), f32))
        spots = jnp.concatenate(lines, axis=0).astype(bf16)
        if sliced:
            out_refs[1][receiver, 0:16, :] = bias
            out_refs[1][receiver, 16 : 16 + count, :] = rows
            out_refs[1][receiver, 16 + count :, :] = spots
        else:
            out_refs[0][receiver, piece : piece + 16, :] = bias
            out_refs[0][receiver, piece + 16 : piece + 16 + count, :] = rows
            out_refs[0][receiver, piece + 16 + count :, :] = spots


def middle_kernel(piece, count, arrived_ref, spread_ref, near_ref, bias_ref):
    senders = arrived_ref.shape[0]
    row_total = (near_ref.shape[0] - 16) // SPAN
    share = row_total // senders
    total = arrived_ref[0, 0:piece].astype(f32)
    for sender in range(1, senders):
        total = total + arrived_ref[sender, 0:piece].astype(f32)
    total = total.astype(bf16)
    for receiver in range(senders):
        spread_ref[receiver] = total
    bias = arrived_ref[0, piece : piece + 16].astype(f32)
    spots = arrived_ref[0, piece + 16 + count :].astype(f32)
    for sender in range(1, senders):
        bias = bias + arrived_ref[sender, piece : piece + 16].astype(f32)
        spots = spots + arrived_ref[sender, piece + 16 + count :].astype(f32)
    bias_ref[...] = bias
    near_ref[SPAN * row_total :, :] = spots.astype(bf16)
    for tile in range(SPAN):
        for sender in range(senders):
            near_ref[pl.ds(tile * row_total + sender * share, share), :] = arrived_ref[
                sender, pl.ds(piece + 16 + tile * share, share), :
            ]


def project_kernel(
    row_total,
    tile_size,
    order_ref,
    weight_ref,
    bias_ref,
    gram_ref,
    *rest,
):
    patches_refs = rest[:-4]
    keys_ref, values_ref, twin_ref, both_ref = rest[-4:]
    heads_width = keys_ref.shape[0]
    local_heads = heads_width // HEAD
    pairs = heads_width // 128
    chunks = heads_width // 128

    def doubled(part):
        weight = weight_ref[part * heads_width : (part + 1) * heads_width, :]
        return jnp.concatenate([weight, weight], axis=1)

    def centred_bias(part):
        same = lax.broadcasted_iota(jnp.int32, (128, 128), 0) == lax.broadcasted_iota(
            jnp.int32, (128, 128), 1
        )
        pieces = []
        for chunk in range(chunks):
            row = bias_ref[part * chunks + chunk : part * chunks + chunk + 1, :]
            pieces.append(jnp.sum(jnp.where(same, row, 0.0), axis=1, keepdims=True))
        grouped = jnp.concatenate(pieces, axis=0).reshape(local_heads, HEAD, 1)
        grouped = grouped - jnp.mean(grouped, axis=1, keepdims=True)
        return grouped.reshape(heads_width, 1)

    def unit_heads(turned, bias):
        grouped = (turned + bias).reshape(local_heads, HEAD, turned.shape[1])
        square = jnp.mean(grouped * grouped, axis=1, keepdims=True)
        return (grouped * lax.rsqrt(square + EPSILON)).reshape(turned.shape)

    gram_top = jnp.concatenate([gram_ref[0], gram_ref[1]], axis=0)
    gram_low = gram_ref[2]

    for block, patches_ref in enumerate(patches_refs):
        place = order_ref[block] * row_total

        def scale(tile, carry, patches_ref=patches_ref, place=place):
            rows = patches_ref[pl.ds(pl.multiple_of(tile * row_total, row_total), row_total), :]
            wide_rows = rows.astype(f32)
            image = jnp.dot(
                jnp.concatenate([rows, rows], axis=1), gram_top, preferred_element_type=f32
            ) + jnp.dot(rows, gram_low, preferred_element_type=f32)
            variance = jnp.sum(image * wide_rows, axis=1, keepdims=True)
            scaled = wide_rows * lax.rsqrt(jnp.maximum(variance, 0.0) + EPSILON)
            high = scaled.astype(bf16)
            at = pl.multiple_of(tile * tile_size + place, row_total)
            both_ref[pl.ds(at, row_total), 0:128] = high
            both_ref[pl.ds(at, row_total), 128:256] = (scaled - high.astype(f32)).astype(bf16)
            return carry

        lax.fori_loop(0, SPAN, scale, 0, unroll=SPAN)

    key_bias = centred_bias(1)
    key_weight = doubled(1)
    value_weight = doubled(2).astype(f32).T.astype(bf16)
    value_bias = jnp.concatenate(
        [bias_ref[2 * chunks + chunk : 2 * chunks + chunk + 1, :] for chunk in range(chunks)], axis=1
    )

    def project(step, carry):
        at = pl.multiple_of(step * 256, 256)
        both = both_ref[pl.ds(at, 256), :]
        keys_ref[:, pl.ds(at, 256)] = unit_heads(ntdot(key_weight, both), key_bias).astype(bf16)
        values_ref[pl.ds(at, 256), :] = (
            jnp.dot(both, value_weight, preferred_element_type=f32) + value_bias
        ).astype(bf16)
        return carry

    lax.fori_loop(0, SPAN * tile_size // 256, project, 0, unroll=2)

    query_bias = centred_bias(0)
    query_weight = doubled(0)
    left = lax.broadcasted_iota(jnp.int32, (QB, 128), 1) < HEAD
    spot_rows = row_total // 128

    for block, patches_ref in enumerate(patches_refs):
        place = order_ref[block] * row_total
        spots = jnp.concatenate(
            [
                patches_ref[SPAN * row_total + row : SPAN * row_total + row + 1, :]
                for row in range(spot_rows)
            ],
            axis=1,
        )
        wanted = lax.broadcasted_iota(jnp.int32, (row_total, row_total), 0).astype(f32)
        chosen = (spots.astype(f32) == wanted).astype(bf16)
        both = both_ref[pl.ds(pl.multiple_of(REACH * tile_size + place, row_total), row_total), :]
        placed = jnp.dot(chosen, both, preferred_element_type=f32).astype(bf16)
        turned = unit_heads(ntdot(query_weight, placed), query_bias).astype(bf16).astype(f32) * 0.125
        rows = turned.T.astype(bf16)
        for part in range(row_total // QB):
            query = order_ref[block] * (row_total // QB) + part
            for pair in range(pairs):
                piece = rows[part * QB : (part + 1) * QB, pair * 128 : (pair + 1) * 128]
                twin_ref[query, pair, 0:QB, :] = jnp.where(left, piece, jnp.zeros_like(piece))
                twin_ref[query, pair, QB : 2 * QB, :] = jnp.where(left, jnp.zeros_like(piece), piece)


def attend_kernel(
    parts, entries, order_ref, starts_ref, counts_ref, keys_ref, values_ref, twin_ref, *rest
):
    out_refs = rest[:-6]
    total_ref, even_ref, odd_ref, block_ref, query_ref, first_ref = rest[-6:]
    pairs = twin_ref.shape[1]
    left = lax.broadcasted_iota(jnp.int32, (QB, 128), 1) < HEAD

    steps = jnp.int32(0)
    for index, (away, part) in enumerate(entries):
        total_ref[index] = jnp.zeros_like(total_ref[index])
        block = (order_ref[0] ^ away) * parts + part

        def note(slot, at, index=index, block=block):
            block_ref[at] = index
            query_ref[at] = block
            first_ref[at] = starts_ref[block * NB + slot]
            return at + 1

        steps = lax.fori_loop(0, counts_ref[block], note, steps)
    for extra in range(2):
        block_ref[steps + extra] = len(entries)
        query_ref[steps + extra] = query_ref[0]
        first_ref[steps + extra] = first_ref[0]

    ones = jnp.ones((KB, 128), bf16)

    def weigh(step, weights_ref):
        start = pl.multiple_of(first_ref[step], KB)
        query = query_ref[step]
        for pair in range(pairs):
            scores = jnp.dot(
                twin_ref[query, pair],
                keys_ref[pair * 128 : (pair + 1) * 128, pl.ds(start, KB)],
                preferred_element_type=f32,
            )
            weights_ref[pair] = jnp.exp(scores).astype(bf16)

    def gather(step, weights_ref):
        start = pl.multiple_of(first_ref[step], KB)
        block = block_ref[step]
        for pair in range(pairs):
            side = jnp.concatenate(
                [values_ref[pl.ds(start, KB), pair * 128 : (pair + 1) * 128], ones], axis=1
            )
            total_ref[block, pair] += jnp.dot(weights_ref[pair], side, preferred_element_type=f32)

    weigh(0, even_ref)

    def visit(twice, carry):
        step = twice * 2
        weigh(step + 1, odd_ref)
        gather(step, even_ref)
        weigh(step + 2, even_ref)
        gather(step + 1, odd_ref)
        return carry

    lax.fori_loop(0, (steps + 1) // 2, visit, 0)

    for index in range(len(entries)):
        for pair in range(pairs):
            both = total_ref[index, pair, :, 0:128] / total_ref[index, pair, :, 128:256]
            out_refs[index][:, pair * 128 : (pair + 1) * 128] = jnp.where(
                left, both[0:QB], both[QB : 2 * QB]
            ).astype(bf16)


def attend_scratch(entries, heads_width):
    pairs = heads_width // 128
    return [
        pltpu.VMEM((entries + 1, pairs, 2 * QB, 256), f32),
        pltpu.VMEM((pairs, 2 * QB, KB), bf16),
        pltpu.VMEM((pairs, 2 * QB, KB), bf16),
        pltpu.SMEM((entries * NB + 2,), jnp.int32),
        pltpu.SMEM((entries * NB + 2,), jnp.int32),
        pltpu.SMEM((entries * NB + 2,), jnp.int32),
    ]


def output_kernel(parts, narrow_count, together, order_ref, *refs):
    attended_refs = refs[: parts * narrow_count]
    weight_ref, gate_ref, out_ref = refs[parts * narrow_count :]
    rows = out_ref.shape[1] // together
    totals = [None] * together
    for away in range(narrow_count):
        attended = jnp.concatenate(
            [attended_refs[chunk * narrow_count + away][...] for chunk in range(parts)], axis=0
        )
        for index in range(together):
            at = pl.multiple_of((index * narrow_count + (order_ref[0] ^ away)) * rows, 16)
            term = ntdot(attended, weight_ref[pl.ds(at, rows), :])
            totals[index] = term if away == 0 else totals[index] + term
    for index, total in enumerate(totals):
        columns = slice(index * rows, (index + 1) * rows)
        out_ref[:, columns] = (total * gate_ref[:, columns]).astype(bf16)


def partial_kernel(kept, sent, held_ref, *refs):
    total = kept + sent
    outs = (kept > 0) + (sent > 0)
    attended_refs = refs[:total]
    weight_refs = refs[total:-outs]
    rows = weight_refs[0].shape[0]
    for index, weight_ref in enumerate(weight_refs):

        @pl.when(held_ref[index] >= 0)
        def _(index=index, weight_ref=weight_ref):
            attended = jnp.concatenate([ref[...] for ref in attended_refs], axis=0)
            product = ntdot(attended, weight_ref[...])
            columns = pl.ds(pl.multiple_of(held_ref[index] * rows, 128), rows)
            if kept:
                refs[-outs][:, columns] = product[: kept * QB]
            if sent:
                refs[-1][:, columns] = product[kept * QB :].astype(bf16)


def final_kernel(own_ref, first_ref, second_ref, third_ref, gate_ref, out_ref):
    far = jnp.concatenate([second_ref[...], third_ref[...]], axis=0).astype(f32)
    total = own_ref[...] + first_ref[...].astype(f32) + far
    out_ref[...] = (total * gate_ref[...]).astype(bf16)


def flip(block, axis, bit):
    devices = range(lax.axis_size(axis))
    return lax.ppermute(block, axis, [(i, i ^ bit) for i in devices])


def cost(flops, moved):
    return pl.CostEstimate(flops=flops, bytes_accessed=moved, transcendentals=0)


def gathered_rows(own):
    count = lax.axis_size("wide")
    index = lax.axis_index("wide")
    length = count // 2
    blocks, held = [own], [index]
    blocks.append(lax.ppermute(own, "wide", [(i, i ^ 1) for i in range(count)]))
    held.append(index ^ 1)
    for sign in (1, -1):
        current = own
        for step in range(1, length):
            move = 2 * sign
            route = [
                (i, i + move)
                for i in range(count)
                if 0 <= i + move < count and 0 <= i - move * (step - 1) < count
            ]
            current = lax.ppermute(current, "wide", route)
            source = index - move * step
            valid = (source >= 0) & (source < count)
            blocks.append(current)
            held.append(jnp.where(valid, source, -1))
            swap = [(i, i ^ 1) for i in range(count) if 0 <= i - move * step < count]
            blocks.append(lax.ppermute(current, "wide", swap))
            held.append(jnp.where(valid, source ^ 1, -1))
    return blocks, jnp.stack(held).astype(jnp.int32)


def block(
    latents,
    targets,
    embed_weight,
    mod_shift,
    mod_scale,
    qkv_weight,
    out_weight,
    mod_gate,
    block_list,
    block_count,
):
    row_total, patch = latents.shape
    width = embed_weight.shape[1]
    wide_count = lax.axis_size("wide")
    narrow_count = lax.axis_size("narrow")
    wide_index = lax.axis_index("wide")
    narrow_index = lax.axis_index("narrow")
    tile_size = row_total * narrow_count
    depth, heads_width = qkv_weight.shape[1:]
    share = row_total // wide_count
    count = -(-SPAN * share // 16) * 16
    piece = 3 * heads_width // wide_count

    small = pltpu.CompilerParams(vmem_limit_bytes=SMALL_VMEM)
    chained = narrow_count == 4 and out_weight.shape[0] % 128 == 0 and row_total == 2 * QB
    if chained:
        blocks, held = gathered_rows(out_weight)
    else:
        out_all = lax.all_gather(out_weight, ("wide", "narrow"), axis=0, tiled=True)

    first = wide_index * depth
    extra = 16 + count + 16
    sliced = depth % 128 != 0 or piece % 16 != 0
    scale = mod_scale.reshape(1, width)
    shift = mod_shift.reshape(1, width)
    own = embed_weight
    if sliced:
        own, scale, shift = (
            lax.dynamic_slice_in_dim(array, first, depth, 1) for array in (own, scale, shift)
        )
        prep_shapes = (
            jax.ShapeDtypeStruct((3 * heads_width, patch), bf16),
            jax.ShapeDtypeStruct((wide_count, extra, patch), bf16),
        )
    else:
        prep_shapes = (jax.ShapeDtypeStruct((wide_count, piece + extra, patch), bf16),)
    smem = pl.BlockSpec(memory_space=pltpu.SMEM)
    prepare = pl.pallas_call(
        functools.partial(prep_kernel, wide_count, sliced),
        out_shape=prep_shapes,
        in_specs=[smem] + [whole_spec()] * 7,
        out_specs=tuple(whole_spec() for _ in prep_shapes),
        cost_estimate=cost(1 << 28, 4 << 20),
        name="prep",
    )
    prepared = prepare(
        jnp.stack([first, wide_index * share]).astype(jnp.int32),
        embed_weight,
        own,
        scale,
        shift,
        qkv_weight,
        latents,
        targets.reshape(1, row_total),
    )
    payload = prepared[0]
    if sliced:
        payload = jnp.concatenate(
            [payload.reshape(wide_count, piece, patch), prepared[1]], axis=1
        )
    gram = pl.pallas_call(
        gram_kernel,
        out_shape=jax.ShapeDtypeStruct((3, patch, patch), bf16),
        in_specs=[whole_spec()],
        out_specs=whole_spec(),
        compiler_params=small,
        name="gram",
    )(embed_weight)
    arrived = lax.all_to_all(payload, "wide", split_axis=0, concat_axis=0, tiled=True)

    near_rows = SPAN * row_total + 16
    if share % 16 == 0 and piece % 16 == 0:
        spread, near, bias = pl.pallas_call(
            functools.partial(middle_kernel, piece, count),
            out_shape=(
                jax.ShapeDtypeStruct((wide_count, piece, patch), bf16),
                jax.ShapeDtypeStruct((near_rows, patch), bf16),
                jax.ShapeDtypeStruct((16, 128), f32),
            ),
            in_specs=[whole_spec()],
            out_specs=(whole_spec(),) * 3,
            compiler_params=small,
            name="middle",
        )(arrived)
    else:
        summed = jnp.sum(arrived[:, :piece].astype(f32), axis=0).astype(bf16)
        bias = jnp.sum(arrived[:, piece : piece + 16].astype(f32), axis=0)
        spread = jnp.broadcast_to(summed[None], (wide_count,) + summed.shape)
        near = arrived[:, piece + 16 : piece + 16 + SPAN * share]
        near = near.reshape(wide_count, SPAN, share, patch).transpose(1, 0, 2, 3)
        spots = jnp.sum(arrived[:, piece + 16 + count :].astype(f32), axis=0).astype(bf16)
        near = jnp.concatenate([near.reshape(SPAN * row_total, patch), spots], axis=0)
    group, order = [near], [0]
    bits = [1 << k for k in range(1, narrow_count.bit_length() - 1)] + [1]
    for bit in bits:
        group = group + [flip(rows, "narrow", bit) for rows in group]
        order = order + [index ^ bit for index in order]
    everything = lax.all_to_all(spread, "wide", split_axis=0, concat_axis=0, tiled=True)
    weight_all = everything.reshape(3 * heads_width, patch)

    order_ids = jnp.bitwise_xor(jnp.array(order, jnp.int32), narrow_index)
    starts = (block_list * KB - (wide_index - REACH) * tile_size).reshape(-1)
    parts = row_total // QB
    pairs = heads_width // 128
    keys, values, twin = pl.pallas_call(
        functools.partial(project_kernel, row_total, tile_size),
        out_shape=(
            pltpu.VMEM((heads_width, SPAN * tile_size), bf16),
            pltpu.VMEM((SPAN * tile_size, heads_width), bf16),
            pltpu.VMEM((tile_size // QB, pairs, 2 * QB, 128), bf16),
        ),
        in_specs=[smem] + [whole_spec()] * (3 + narrow_count),
        out_specs=(whole_spec(),) * 3,
        scratch_shapes=[pltpu.VMEM((SPAN * tile_size, 256), bf16)],
        compiler_params=pltpu.CompilerParams(vmem_limit_bytes=PROJECT_VMEM),
        cost_estimate=cost(10 * SPAN * tile_size * patch * heads_width, 16 << 20),
        name="project",
    )(order_ids, weight_all, bias, gram, *group)

    def attend(entries):
        return pl.pallas_call(
            functools.partial(attend_kernel, parts, entries),
            out_shape=(jax.ShapeDtypeStruct((QB, heads_width), bf16),) * len(entries),
            in_specs=[smem] * 3 + [whole_spec()] * 3,
            out_specs=(whole_spec(),) * len(entries),
            scratch_shapes=attend_scratch(len(entries), heads_width),
            compiler_params=pltpu.CompilerParams(vmem_limit_bytes=ATTEND_VMEM),
            cost_estimate=cost(4 * QB * len(entries) * NB * KB * heads_width, 16 << 20),
        )(order_ids, starts, block_count, keys, values, twin)

    if chained:
        gate = mod_gate.reshape(1, width)

        def multiply(attended, kept):
            sent = len(attended) - kept
            shapes = []
            if kept:
                shapes.append(jax.ShapeDtypeStruct((kept * QB, width), f32))
            if sent:
                shapes.append(jax.ShapeDtypeStruct((sent * QB, width), bf16))
            return pl.pallas_call(
                functools.partial(partial_kernel, kept, sent),
                out_shape=tuple(shapes),
                in_specs=[smem] + [whole_spec()] * (len(attended) + len(blocks)),
                out_specs=(whole_spec(),) * len(shapes),
                compiler_params=small,
                cost_estimate=cost(2 * len(attended) * QB * heads_width * width, 8 << 20),
            )(held, *attended, *blocks)

        far = []
        for part in range(parts):
            attended = attend(((2, part), (3, part)))
            keep, send = multiply(attended, 1)
            other = flip(send, "narrow", 1)
            joined = (keep + other.astype(f32)).astype(bf16)
            far.append(flip(joined, "narrow", 2))
        (send,) = multiply(attend(((1, 0), (1, 1))), 0)
        other = flip(send, "narrow", 1)
        (own,) = multiply(attend(((0, 0), (0, 1))), parts)
        return pl.pallas_call(
            final_kernel,
            out_shape=jax.ShapeDtypeStruct((row_total, width), bf16),
            in_specs=[whole_spec()] * 5,
            out_specs=whole_spec(),
            compiler_params=small,
            name="final",
        )(own, other, *far, gate)

    pieces = []
    for chunk in range(parts):
        mine = attend(tuple((away, chunk) for away in range(narrow_count)))
        pieces.append(mine[0])
        for away in range(1, narrow_count):
            pieces.append(flip(mine[away], "narrow", away))

    out_rows = out_weight.shape[0]
    gate = mod_gate.reshape(1, width)
    if out_rows % 128 == 0:
        together = 2 if wide_count % 2 == 0 else 1
        span = together * out_rows
        return pl.pallas_call(
            functools.partial(output_kernel, parts, narrow_count, together),
            grid=(wide_count // together,),
            out_shape=jax.ShapeDtypeStruct((row_total, width), bf16),
            in_specs=[smem]
            + [pl.BlockSpec((QB, heads_width), lambda i: (0, 0))] * (parts * narrow_count)
            + [
                pl.BlockSpec((narrow_count * span, heads_width), lambda i: (i, 0)),
                pl.BlockSpec((1, span), lambda i: (0, i)),
            ],
            out_specs=pl.BlockSpec((row_total, span), lambda i: (0, i)),
            compiler_params=pltpu.CompilerParams(vmem_limit_bytes=OUTPUT_VMEM),
            name="output",
        )(order_ids, *pieces, out_all, gate)
    weights = out_all.reshape(wide_count, narrow_count, out_rows, heads_width)
    product = 0.0
    for away in range(narrow_count):
        attended = jnp.concatenate(pieces[away::narrow_count], axis=0)
        weight = lax.dynamic_index_in_dim(weights, narrow_index ^ away, 1, False)
        product = product + jnp.einsum(
            "tk,wfk->twf", attended, weight, preferred_element_type=f32
        )
    return (gate * product.reshape(row_total, width)).astype(bf16)


def solution(mesh):
    in_specs = (
        P(("wide", "narrow"), None),
        P(("wide", "narrow")),
        P(),
        P(),
        P(),
        P(None, "wide", "narrow"),
        P("wide", "narrow"),
        P(),
        P("wide", None),
        P("wide"),
    )
    out_specs = P(("wide", "narrow"), None)
    return jax.shard_map(block, mesh=mesh, in_specs=in_specs, out_specs=out_specs, check_vma=False)
```

```python
import functools

import jax
import jax.numpy as jnp
from jax import lax
from jax.experimental import pallas as pl
from jax.experimental.pallas import tpu as pltpu
from jax.sharding import PartitionSpec as P


HEAD = 64
NB = 8
KB = 512
QB = 128
REACH = 2
SPAN = 2 * REACH + 1
EPSILON = 1e-06
PROJECT_VMEM = 19 << 20
ATTEND_VMEM = 11 << 20
OUTPUT_VMEM = 53 << 20
SMALL_VMEM = 11 << 20

f32 = jnp.float32
bf16 = jnp.bfloat16
NT = (((1,), (1,)), ((), ()))


def ntdot(a, b):
    return lax.dot_general(a, b, NT, preferred_element_type=f32)


def whole_spec():
    return pl.BlockSpec(memory_space=pltpu.VMEM)


def split3(value):
    high = value.astype(bf16)
    rest = value - high.astype(f32)
    mid = rest.astype(bf16)
    low = (rest - mid.astype(f32)).astype(bf16)
    return high, mid, low


def gram_kernel(embed_ref, gram_ref):
    embed = embed_ref[...].astype(f32)
    width = embed.shape[1]
    centred = embed - jnp.mean(embed, axis=1, keepdims=True)
    gram = lax.dot_general(
        centred, centred, NT, preferred_element_type=f32, precision=lax.Precision.HIGHEST
    ) * (1.0 / width)
    for index, term in enumerate(split3(gram)):
        gram_ref[index] = term


def prep_kernel(
    wide_count,
    sliced,
    at_ref,
    embed_ref,
    slice_ref,
    scale_ref,
    shift_ref,
    qkv_ref,
    latents_ref,
    targets_ref,
    *out_refs,
):
    depth, heads_width = qkv_ref.shape[1:]
    patch = embed_ref.shape[0]
    if sliced:
        own, scale, shift = slice_ref[...], scale_ref[...], shift_ref[...]
    else:
        columns = pl.ds(pl.multiple_of(at_ref[0], 128), depth)
        own, scale, shift = embed_ref[:, columns], scale_ref[:, columns], shift_ref[:, columns]
    piece = 3 * heads_width // wide_count
    row_mean = jnp.mean(embed_ref[...].astype(f32), axis=1, keepdims=True)
    factor = (own.astype(f32) - row_mean) * (1.0 + scale)
    stacked = jnp.concatenate([factor, jnp.broadcast_to(shift, (16, depth))], axis=0)
    high, mid, _ = split3(stacked)
    bias_rows = []
    for part in range(3):
        weights = qkv_ref[part]
        product = jnp.dot(high, weights, preferred_element_type=f32) + jnp.dot(
            mid, weights, preferred_element_type=f32
        )
        for chunk in range(heads_width // 128):
            bias_rows.append(product[patch : patch + 1, chunk * 128 : (chunk + 1) * 128])
        turned = product[0:patch].T
        if part < 2:
            grouped = turned.reshape(heads_width // HEAD, HEAD, patch)
            grouped = grouped - jnp.mean(grouped, axis=1, keepdims=True)
            turned = grouped.reshape(turned.shape)
        turned = turned.astype(bf16)
        top = part * heads_width
        if sliced:
            out_refs[0][top : top + heads_width, :] = turned
            continue
        for receiver in range(wide_count):
            low = max(receiver * piece, top)
            end = min((receiver + 1) * piece, top + heads_width)
            if low < end:
                base = receiver * piece
                out_refs[0][receiver, low - base : end - base, :] = turned[low - top : end - top]
    bias_rows.append(jnp.zeros((16 - len(bias_rows), 128), f32))
    bias = jnp.concatenate(bias_rows, axis=0).astype(bf16)
    row_total = latents_ref.shape[0]
    share = row_total // wide_count
    across = targets_ref[...]
    same = lax.broadcasted_iota(jnp.int32, (row_total, row_total), 0) == lax.broadcasted_iota(
        jnp.int32, (row_total, row_total), 1
    )
    down = jnp.sum(jnp.where(same, across.astype(f32), 0.0), axis=1, keepdims=True)
    across = across.astype(f32)
    slot_across = jnp.sum((down < across).astype(f32), axis=0, keepdims=True)
    slot_down = jnp.sum((across < down).astype(f32), axis=1, keepdims=True)
    local = (down.astype(jnp.int32) % row_total).astype(f32)
    count = -(-SPAN * share // 16) * 16
    latents = latents_ref[...]
    wanted = lax.broadcasted_iota(jnp.int32, (count, row_total), 0)
    spot_rows = -(-row_total // 128)
    lane = lax.broadcasted_iota(jnp.int32, (row_total, 128), 1)
    for receiver in range(wide_count):
        first = (receiver - REACH) * share
        chosen = (slot_across == (wanted + first).astype(f32)) & (wanted < SPAN * share)
        rows = jnp.dot(chosen.astype(bf16), latents, preferred_element_type=f32).astype(bf16)
        lines = []
        for line in range(spot_rows):
            place = lane + (line * 128 - at_ref[1])
            mine = (slot_down == (place + receiver * share).astype(f32)) & (
                (place >= 0) & (place < share)
            )
            lines.append(jnp.sum(jnp.where(mine, local, 0.0), axis=0, keepdims=True))
        lines.append(jnp.zeros((16 - spot_rows, 128), f32))
        spots = jnp.concatenate(lines, axis=0).astype(bf16)
        if sliced:
            out_refs[1][receiver, 0:16, :] = bias
            out_refs[1][receiver, 16 : 16 + count, :] = rows
            out_refs[1][receiver, 16 + count :, :] = spots
        else:
            out_refs[0][receiver, piece : piece + 16, :] = bias
            out_refs[0][receiver, piece + 16 : piece + 16 + count, :] = rows
            out_refs[0][receiver, piece + 16 + count :, :] = spots


def middle_kernel(piece, count, arrived_ref, spread_ref, near_ref, bias_ref):
    senders = arrived_ref.shape[0]
    row_total = (near_ref.shape[0] - 16) // SPAN
    share = row_total // senders
    total = arrived_ref[0, 0:piece].astype(f32)
    for sender in range(1, senders):
        total = total + arrived_ref[sender, 0:piece].astype(f32)
    total = total.astype(bf16)
    for receiver in range(senders):
        spread_ref[receiver] = total
    bias = arrived_ref[0, piece : piece + 16].astype(f32)
    spots = arrived_ref[0, piece + 16 + count :].astype(f32)
    for sender in range(1, senders):
        bias = bias + arrived_ref[sender, piece : piece + 16].astype(f32)
        spots = spots + arrived_ref[sender, piece + 16 + count :].astype(f32)
    bias_ref[...] = bias
    near_ref[SPAN * row_total :, :] = spots.astype(bf16)
    for tile in range(SPAN):
        for sender in range(senders):
            near_ref[pl.ds(tile * row_total + sender * share, share), :] = arrived_ref[
                sender, pl.ds(piece + 16 + tile * share, share), :
            ]


def project_kernel(
    row_total,
    tile_size,
    order_ref,
    weight_ref,
    bias_ref,
    gram_ref,
    *rest,
):
    patches_refs = rest[:-4]
    keys_ref, values_ref, twin_ref, both_ref = rest[-4:]
    heads_width = keys_ref.shape[0]
    local_heads = heads_width // HEAD
    pairs = heads_width // 128
    chunks = heads_width // 128

    def doubled(part):
        weight = weight_ref[part * heads_width : (part + 1) * heads_width, :]
        return jnp.concatenate([weight, weight], axis=1)

    def centred_bias(part):
        same = lax.broadcasted_iota(jnp.int32, (128, 128), 0) == lax.broadcasted_iota(
            jnp.int32, (128, 128), 1
        )
        pieces = []
        for chunk in range(chunks):
            row = bias_ref[part * chunks + chunk : part * chunks + chunk + 1, :]
            pieces.append(jnp.sum(jnp.where(same, row, 0.0), axis=1, keepdims=True))
        grouped = jnp.concatenate(pieces, axis=0).reshape(local_heads, HEAD, 1)
        grouped = grouped - jnp.mean(grouped, axis=1, keepdims=True)
        return grouped.reshape(heads_width, 1)

    def unit_heads(turned, bias):
        grouped = (turned + bias).reshape(local_heads, HEAD, turned.shape[1])
        square = jnp.mean(grouped * grouped, axis=1, keepdims=True)
        return (grouped * lax.rsqrt(square + EPSILON)).reshape(turned.shape)

    gram_top = jnp.concatenate([gram_ref[0], gram_ref[1]], axis=0)
    gram_low = gram_ref[2]

    for block, patches_ref in enumerate(patches_refs):
        place = order_ref[block] * row_total

        def scale(tile, carry, patches_ref=patches_ref, place=place):
            rows = patches_ref[pl.ds(pl.multiple_of(tile * row_total, row_total), row_total), :]
            wide_rows = rows.astype(f32)
            image = jnp.dot(
                jnp.concatenate([rows, rows], axis=1), gram_top, preferred_element_type=f32
            ) + jnp.dot(rows, gram_low, preferred_element_type=f32)
            variance = jnp.sum(image * wide_rows, axis=1, keepdims=True)
            scaled = wide_rows * lax.rsqrt(jnp.maximum(variance, 0.0) + EPSILON)
            high = scaled.astype(bf16)
            at = pl.multiple_of(tile * tile_size + place, row_total)
            both_ref[pl.ds(at, row_total), 0:128] = high
            both_ref[pl.ds(at, row_total), 128:256] = (scaled - high.astype(f32)).astype(bf16)
            return carry

        lax.fori_loop(0, SPAN, scale, 0, unroll=SPAN)

    key_bias = centred_bias(1)
    key_weight = doubled(1)
    value_weight = doubled(2).astype(f32).T.astype(bf16)
    value_bias = jnp.concatenate(
        [bias_ref[2 * chunks + chunk : 2 * chunks + chunk + 1, :] for chunk in range(chunks)], axis=1
    )

    def project(step, carry):
        at = pl.multiple_of(step * 256, 256)
        both = both_ref[pl.ds(at, 256), :]
        keys_ref[:, pl.ds(at, 256)] = unit_heads(ntdot(key_weight, both), key_bias).astype(bf16)
        values_ref[pl.ds(at, 256), :] = (
            jnp.dot(both, value_weight, preferred_element_type=f32) + value_bias
        ).astype(bf16)
        return carry

    lax.fori_loop(0, SPAN * tile_size // 256, project, 0, unroll=2)

    query_bias = centred_bias(0)
    query_weight = doubled(0)
    left = lax.broadcasted_iota(jnp.int32, (QB, 128), 1) < HEAD
    spot_rows = row_total // 128

    for block, patches_ref in enumerate(patches_refs):
        place = order_ref[block] * row_total
        spots = jnp.concatenate(
            [
                patches_ref[SPAN * row_total + row : SPAN * row_total + row + 1, :]
                for row in range(spot_rows)
            ],
            axis=1,
        )
        wanted = lax.broadcasted_iota(jnp.int32, (row_total, row_total), 0).astype(f32)
        chosen = (spots.astype(f32) == wanted).astype(bf16)
        both = both_ref[pl.ds(pl.multiple_of(REACH * tile_size + place, row_total), row_total), :]
        placed = jnp.dot(chosen, both, preferred_element_type=f32).astype(bf16)
        turned = unit_heads(ntdot(query_weight, placed), query_bias).astype(bf16).astype(f32) * 0.125
        rows = turned.T.astype(bf16)
        for part in range(row_total // QB):
            query = order_ref[block] * (row_total // QB) + part
            for pair in range(pairs):
                piece = rows[part * QB : (part + 1) * QB, pair * 128 : (pair + 1) * 128]
                twin_ref[query, pair, 0:QB, :] = jnp.where(left, piece, jnp.zeros_like(piece))
                twin_ref[query, pair, QB : 2 * QB, :] = jnp.where(left, jnp.zeros_like(piece), piece)


def attend_kernel(
    parts, entries, order_ref, starts_ref, counts_ref, keys_ref, values_ref, twin_ref, *rest
):
    out_refs = rest[:-6]
    total_ref, even_ref, odd_ref, block_ref, query_ref, first_ref = rest[-6:]
    pairs = twin_ref.shape[1]
    left = lax.broadcasted_iota(jnp.int32, (QB, 128), 1) < HEAD

    steps = jnp.int32(0)
    for index, (away, part) in enumerate(entries):
        total_ref[index] = jnp.zeros_like(total_ref[index])
        block = (order_ref[0] ^ away) * parts + part

        def note(slot, at, index=index, block=block):
            block_ref[at] = index
            query_ref[at] = block
            first_ref[at] = starts_ref[block * NB + slot]
            return at + 1

        steps = lax.fori_loop(0, counts_ref[block], note, steps)
    for extra in range(2):
        block_ref[steps + extra] = len(entries)
        query_ref[steps + extra] = query_ref[0]
        first_ref[steps + extra] = first_ref[0]

    ones = jnp.ones((KB, 128), bf16)

    def weigh(step, weights_ref):
        start = pl.multiple_of(first_ref[step], KB)
        query = query_ref[step]
        for pair in range(pairs):
            scores = jnp.dot(
                twin_ref[query, pair],
                keys_ref[pair * 128 : (pair + 1) * 128, pl.ds(start, KB)],
                preferred_element_type=f32,
            )
            weights_ref[pair] = jnp.exp(scores).astype(bf16)

    def gather(step, weights_ref):
        start = pl.multiple_of(first_ref[step], KB)
        block = block_ref[step]
        for pair in range(pairs):
            side = jnp.concatenate(
                [values_ref[pl.ds(start, KB), pair * 128 : (pair + 1) * 128], ones], axis=1
            )
            total_ref[block, pair] += jnp.dot(weights_ref[pair], side, preferred_element_type=f32)

    weigh(0, even_ref)

    def visit(twice, carry):
        step = twice * 2
        weigh(step + 1, odd_ref)
        gather(step, even_ref)
        weigh(step + 2, even_ref)
        gather(step + 1, odd_ref)
        return carry

    lax.fori_loop(0, (steps + 1) // 2, visit, 0)

    for index in range(len(entries)):
        for pair in range(pairs):
            both = total_ref[index, pair, :, 0:128] / total_ref[index, pair, :, 128:256]
            out_refs[index][:, pair * 128 : (pair + 1) * 128] = jnp.where(
                left, both[0:QB], both[QB : 2 * QB]
            ).astype(bf16)


def attend_scratch(entries, heads_width):
    pairs = heads_width // 128
    return [
        pltpu.VMEM((entries + 1, pairs, 2 * QB, 256), f32),
        pltpu.VMEM((pairs, 2 * QB, KB), bf16),
        pltpu.VMEM((pairs, 2 * QB, KB), bf16),
        pltpu.SMEM((entries * NB + 2,), jnp.int32),
        pltpu.SMEM((entries * NB + 2,), jnp.int32),
        pltpu.SMEM((entries * NB + 2,), jnp.int32),
    ]


def output_kernel(parts, narrow_count, together, order_ref, *refs):
    attended_refs = refs[: parts * narrow_count]
    weight_ref, gate_ref, out_ref = refs[parts * narrow_count :]
    rows = out_ref.shape[1] // together
    totals = [None] * together
    for away in range(narrow_count):
        attended = jnp.concatenate(
            [attended_refs[chunk * narrow_count + away][...] for chunk in range(parts)], axis=0
        )
        for index in range(together):
            at = pl.multiple_of((index * narrow_count + (order_ref[0] ^ away)) * rows, 16)
            term = ntdot(attended, weight_ref[pl.ds(at, rows), :])
            totals[index] = term if away == 0 else totals[index] + term
    for index, total in enumerate(totals):
        columns = slice(index * rows, (index + 1) * rows)
        out_ref[:, columns] = (total * gate_ref[:, columns]).astype(bf16)


def partial_kernel(kept, sent, held_ref, *refs):
    total = kept + sent
    outs = (kept > 0) + (sent > 0)
    attended_refs = refs[:total]
    weight_refs = refs[total:-outs]
    rows = weight_refs[0].shape[0]
    for index, weight_ref in enumerate(weight_refs):

        @pl.when(held_ref[index] >= 0)
        def _(index=index, weight_ref=weight_ref):
            attended = jnp.concatenate([ref[...] for ref in attended_refs], axis=0)
            product = ntdot(attended, weight_ref[...])
            columns = pl.ds(pl.multiple_of(held_ref[index] * rows, 128), rows)
            if kept:
                refs[-outs][:, columns] = product[: kept * QB]
            if sent:
                refs[-1][:, columns] = product[kept * QB :].astype(bf16)


def final_kernel(own_ref, first_ref, second_ref, third_ref, gate_ref, out_ref):
    far = jnp.concatenate([second_ref[...], third_ref[...]], axis=0).astype(f32)
    total = own_ref[...] + first_ref[...].astype(f32) + far
    out_ref[...] = (total * gate_ref[...]).astype(bf16)


def flip(block, axis, bit):
    devices = range(lax.axis_size(axis))
    return lax.ppermute(block, axis, [(i, i ^ bit) for i in devices])


def cost(flops, moved):
    return pl.CostEstimate(flops=flops, bytes_accessed=moved, transcendentals=0)


def gathered_rows(own):
    count = lax.axis_size("wide")
    index = lax.axis_index("wide")
    length = count // 2
    blocks, held = [own], [index]
    blocks.append(lax.ppermute(own, "wide", [(i, i ^ 1) for i in range(count)]))
    held.append(index ^ 1)
    for sign in (1, -1):
        current = own
        for step in range(1, length):
            move = 2 * sign
            route = [
                (i, i + move)
                for i in range(count)
                if 0 <= i + move < count and 0 <= i - move * (step - 1) < count
            ]
            current = lax.ppermute(current, "wide", route)
            source = index - move * step
            valid = (source >= 0) & (source < count)
            blocks.append(current)
            held.append(jnp.where(valid, source, -1))
            swap = [(i, i ^ 1) for i in range(count) if 0 <= i - move * step < count]
            blocks.append(lax.ppermute(current, "wide", swap))
            held.append(jnp.where(valid, source ^ 1, -1))
    return blocks, jnp.stack(held).astype(jnp.int32)


def block(
    latents,
    targets,
    embed_weight,
    mod_shift,
    mod_scale,
    qkv_weight,
    out_weight,
    mod_gate,
    block_list,
    block_count,
):
    row_total, patch = latents.shape
    width = embed_weight.shape[1]
    wide_count = lax.axis_size("wide")
    narrow_count = lax.axis_size("narrow")
    wide_index = lax.axis_index("wide")
    narrow_index = lax.axis_index("narrow")
    tile_size = row_total * narrow_count
    depth, heads_width = qkv_weight.shape[1:]
    share = row_total // wide_count
    count = -(-SPAN * share // 16) * 16
    piece = 3 * heads_width // wide_count

    small = pltpu.CompilerParams(vmem_limit_bytes=SMALL_VMEM)
    chained = narrow_count == 4 and out_weight.shape[0] % 128 == 0 and row_total == 2 * QB
    if chained:
        blocks, held = gathered_rows(out_weight)
    else:
        out_all = lax.all_gather(out_weight, ("wide", "narrow"), axis=0, tiled=True)

    first = wide_index * depth
    extra = 16 + count + 16
    sliced = depth % 128 != 0 or piece % 16 != 0
    scale = mod_scale.reshape(1, width)
    shift = mod_shift.reshape(1, width)
    own = embed_weight
    if sliced:
        own, scale, shift = (
            lax.dynamic_slice_in_dim(array, first, depth, 1) for array in (own, scale, shift)
        )
        prep_shapes = (
            jax.ShapeDtypeStruct((3 * heads_width, patch), bf16),
            jax.ShapeDtypeStruct((wide_count, extra, patch), bf16),
        )
    else:
        prep_shapes = (jax.ShapeDtypeStruct((wide_count, piece + extra, patch), bf16),)
    smem = pl.BlockSpec(memory_space=pltpu.SMEM)
    prepare = pl.pallas_call(
        functools.partial(prep_kernel, wide_count, sliced),
        out_shape=prep_shapes,
        in_specs=[smem] + [whole_spec()] * 7,
        out_specs=tuple(whole_spec() for _ in prep_shapes),
        cost_estimate=cost(1 << 28, 4 << 20),
        name="prep",
    )
    prepared = prepare(
        jnp.stack([first, wide_index * share]).astype(jnp.int32),
        embed_weight,
        own,
        scale,
        shift,
        qkv_weight,
        latents,
        targets.reshape(1, row_total),
    )
    payload = prepared[0]
    if sliced:
        payload = jnp.concatenate(
            [payload.reshape(wide_count, piece, patch), prepared[1]], axis=1
        )
    gram = pl.pallas_call(
        gram_kernel,
        out_shape=jax.ShapeDtypeStruct((3, patch, patch), bf16),
        in_specs=[whole_spec()],
        out_specs=whole_spec(),
        compiler_params=small,
        name="gram",
    )(embed_weight)
    arrived = lax.all_to_all(payload, "wide", split_axis=0, concat_axis=0, tiled=True)

    near_rows = SPAN * row_total + 16
    if share % 16 == 0 and piece % 16 == 0:
        spread, near, bias = pl.pallas_call(
            functools.partial(middle_kernel, piece, count),
            out_shape=(
                jax.ShapeDtypeStruct((wide_count, piece, patch), bf16),
                jax.ShapeDtypeStruct((near_rows, patch), bf16),
                jax.ShapeDtypeStruct((16, 128), f32),
            ),
            in_specs=[whole_spec()],
            out_specs=(whole_spec(),) * 3,
            name="middle",
        )(arrived)
    else:
        summed = jnp.sum(arrived[:, :piece].astype(f32), axis=0).astype(bf16)
        bias = jnp.sum(arrived[:, piece : piece + 16].astype(f32), axis=0)
        spread = jnp.broadcast_to(summed[None], (wide_count,) + summed.shape)
        near = arrived[:, piece + 16 : piece + 16 + SPAN * share]
        near = near.reshape(wide_count, SPAN, share, patch).transpose(1, 0, 2, 3)
        spots = jnp.sum(arrived[:, piece + 16 + count :].astype(f32), axis=0).astype(bf16)
        near = jnp.concatenate([near.reshape(SPAN * row_total, patch), spots], axis=0)
    group, order = [near], [0]
    bits = [1 << k for k in range(1, narrow_count.bit_length() - 1)] + [1]
    for bit in bits:
        others = []
        for rows in group:
            others.append(flip(rows, "narrow", bit))
        group = group + others
        order = order + [index ^ bit for index in order]
    everything = lax.all_to_all(spread, "wide", split_axis=0, concat_axis=0, tiled=True)
    weight_all = everything.reshape(3 * heads_width, patch)

    order_ids = jnp.bitwise_xor(jnp.array(order, jnp.int32), narrow_index)
    starts = (block_list * KB - (wide_index - REACH) * tile_size).reshape(-1)
    parts = row_total // QB
    pairs = heads_width // 128
    keys, values, twin = pl.pallas_call(
        functools.partial(project_kernel, row_total, tile_size),
        out_shape=(
            pltpu.VMEM((heads_width, SPAN * tile_size), bf16),
            pltpu.VMEM((SPAN * tile_size, heads_width), bf16),
            pltpu.VMEM((tile_size // QB, pairs, 2 * QB, 128), bf16),
        ),
        in_specs=[smem] + [whole_spec()] * (3 + narrow_count),
        out_specs=(whole_spec(),) * 3,
        scratch_shapes=[pltpu.VMEM((SPAN * tile_size, 256), bf16)],
        compiler_params=pltpu.CompilerParams(vmem_limit_bytes=PROJECT_VMEM),
        cost_estimate=cost(10 * SPAN * tile_size * patch * heads_width, 16 << 20),
        name="project",
    )(order_ids, weight_all, bias, gram, *group)

    def attend(entries):
        return pl.pallas_call(
            functools.partial(attend_kernel, parts, entries),
            out_shape=(jax.ShapeDtypeStruct((QB, heads_width), bf16),) * len(entries),
            in_specs=[smem] * 3 + [whole_spec()] * 3,
            out_specs=(whole_spec(),) * len(entries),
            scratch_shapes=attend_scratch(len(entries), heads_width),
            compiler_params=pltpu.CompilerParams(vmem_limit_bytes=ATTEND_VMEM),
            cost_estimate=cost(4 * QB * len(entries) * NB * KB * heads_width, 16 << 20),
        )(order_ids, starts, block_count, keys, values, twin)

    if chained:
        gate = mod_gate.reshape(1, width)

        def multiply(attended, kept):
            sent = len(attended) - kept
            shapes = []
            if kept:
                shapes.append(jax.ShapeDtypeStruct((kept * QB, width), f32))
            if sent:
                shapes.append(jax.ShapeDtypeStruct((sent * QB, width), bf16))
            return pl.pallas_call(
                functools.partial(partial_kernel, kept, sent),
                out_shape=tuple(shapes),
                in_specs=[smem] + [whole_spec()] * (len(attended) + len(blocks)),
                out_specs=(whole_spec(),) * len(shapes),
                compiler_params=small,
                cost_estimate=cost(2 * len(attended) * QB * heads_width * width, 8 << 20),
            )(held, *attended, *blocks)

        far = []
        for part in range(parts):
            attended = attend(((2, part), (3, part)))
            keep, send = multiply(attended, 1)
            other = flip(send, "narrow", 1)
            joined = (keep + other.astype(f32)).astype(bf16)
            far.append(flip(joined, "narrow", 2))
        (send,) = multiply(attend(((1, 0), (1, 1))), 0)
        other = flip(send, "narrow", 1)
        (own,) = multiply(attend(((0, 0), (0, 1))), parts)
        return pl.pallas_call(
            final_kernel,
            out_shape=jax.ShapeDtypeStruct((row_total, width), bf16),
            in_specs=[whole_spec()] * 5,
            out_specs=whole_spec(),
            compiler_params=small,
            name="final",
        )(own, other, *far, gate)

    pieces = []
    for chunk in range(parts):
        mine = attend(tuple((away, chunk) for away in range(narrow_count)))
        pieces.append(mine[0])
        for away in range(1, narrow_count):
            pieces.append(flip(mine[away], "narrow", away))

    out_rows = out_weight.shape[0]
    gate = mod_gate.reshape(1, width)
    if out_rows % 128 == 0:
        together = 2 if wide_count % 2 == 0 else 1
        span = together * out_rows
        return pl.pallas_call(
            functools.partial(output_kernel, parts, narrow_count, together),
            grid=(wide_count // together,),
            out_shape=jax.ShapeDtypeStruct((row_total, width), bf16),
            in_specs=[smem]
            + [pl.BlockSpec((QB, heads_width), lambda i: (0, 0))] * (parts * narrow_count)
            + [
                pl.BlockSpec((narrow_count * span, heads_width), lambda i: (i, 0)),
                pl.BlockSpec((1, span), lambda i: (0, i)),
            ],
            out_specs=pl.BlockSpec((row_total, span), lambda i: (0, i)),
            compiler_params=pltpu.CompilerParams(vmem_limit_bytes=OUTPUT_VMEM),
            name="output",
        )(order_ids, *pieces, out_all, gate)
    weights = out_all.reshape(wide_count, narrow_count, out_rows, heads_width)
    product = 0.0
    for away in range(narrow_count):
        attended = jnp.concatenate(pieces[away::narrow_count], axis=0)
        weight = lax.dynamic_index_in_dim(weights, narrow_index ^ away, 1, False)
        product = product + jnp.einsum(
            "tk,wfk->twf", attended, weight, preferred_element_type=f32
        )
    return (gate * product.reshape(row_total, width)).astype(bf16)


def solution(mesh):
    in_specs = (
        P(("wide", "narrow"), None),
        P(("wide", "narrow")),
        P(),
        P(),
        P(),
        P(None, "wide", "narrow"),
        P("wide", "narrow"),
        P(),
        P("wide", None),
        P("wide"),
    )
    out_specs = P(("wide", "narrow"), None)
    return jax.shard_map(block, mesh=mesh, in_specs=in_specs, out_specs=out_specs, check_vma=False)
```

```python
import functools

import jax
import jax.numpy as jnp
from jax import lax
from jax.experimental import pallas as pl
from jax.experimental.pallas import tpu as pltpu
from jax.sharding import PartitionSpec as P


HEAD = 64
NB = 8
KB = 512
QB = 128
REACH = 2
SPAN = 2 * REACH + 1
EPSILON = 1e-06
PROJECT_VMEM = 19 << 20
ATTEND_VMEM = 11 << 20
OUTPUT_VMEM = 53 << 20
SMALL_VMEM = 11 << 20

f32 = jnp.float32
bf16 = jnp.bfloat16
NT = (((1,), (1,)), ((), ()))


def ntdot(a, b):
    return lax.dot_general(a, b, NT, preferred_element_type=f32)


def whole_spec():
    return pl.BlockSpec(memory_space=pltpu.VMEM)


def split3(value):
    high = value.astype(bf16)
    rest = value - high.astype(f32)
    mid = rest.astype(bf16)
    low = (rest - mid.astype(f32)).astype(bf16)
    return high, mid, low


def gram_kernel(embed_ref, gram_ref):
    embed = embed_ref[...].astype(f32)
    width = embed.shape[1]
    centred = embed - jnp.mean(embed, axis=1, keepdims=True)
    gram = lax.dot_general(
        centred, centred, NT, preferred_element_type=f32, precision=lax.Precision.HIGHEST
    ) * (1.0 / width)
    for index, term in enumerate(split3(gram)):
        gram_ref[index] = term


def prep_kernel(
    wide_count,
    sliced,
    at_ref,
    embed_ref,
    slice_ref,
    scale_ref,
    shift_ref,
    qkv_ref,
    latents_ref,
    targets_ref,
    *out_refs,
):
    depth, heads_width = qkv_ref.shape[1:]
    patch = embed_ref.shape[0]
    if sliced:
        own, scale, shift = slice_ref[...], scale_ref[...], shift_ref[...]
    else:
        columns = pl.ds(pl.multiple_of(at_ref[0], 128), depth)
        own, scale, shift = embed_ref[:, columns], scale_ref[:, columns], shift_ref[:, columns]
    piece = 3 * heads_width // wide_count
    row_mean = jnp.mean(embed_ref[...].astype(f32), axis=1, keepdims=True)
    factor = (own.astype(f32) - row_mean) * (1.0 + scale)
    stacked = jnp.concatenate([factor, jnp.broadcast_to(shift, (16, depth))], axis=0)
    high, mid, _ = split3(stacked)
    bias_rows = []
    for part in range(3):
        weights = qkv_ref[part]
        product = jnp.dot(high, weights, preferred_element_type=f32) + jnp.dot(
            mid, weights, preferred_element_type=f32
        )
        for chunk in range(heads_width // 128):
            bias_rows.append(product[patch : patch + 1, chunk * 128 : (chunk + 1) * 128])
        turned = product[0:patch].T
        if part < 2:
            grouped = turned.reshape(heads_width // HEAD, HEAD, patch)
            grouped = grouped - jnp.mean(grouped, axis=1, keepdims=True)
            turned = grouped.reshape(turned.shape)
        turned = turned.astype(bf16)
        top = part * heads_width
        if sliced:
            out_refs[0][top : top + heads_width, :] = turned
            continue
        for receiver in range(wide_count):
            low = max(receiver * piece, top)
            end = min((receiver + 1) * piece, top + heads_width)
            if low < end:
                base = receiver * piece
                out_refs[0][receiver, low - base : end - base, :] = turned[low - top : end - top]
    bias_rows.append(jnp.zeros((16 - len(bias_rows), 128), f32))
    bias = jnp.concatenate(bias_rows, axis=0).astype(bf16)
    row_total = latents_ref.shape[0]
    share = row_total // wide_count
    across = targets_ref[...]
    same = lax.broadcasted_iota(jnp.int32, (row_total, row_total), 0) == lax.broadcasted_iota(
        jnp.int32, (row_total, row_total), 1
    )
    down = jnp.sum(jnp.where(same, across.astype(f32), 0.0), axis=1, keepdims=True)
    across = across.astype(f32)
    slot_across = jnp.sum((down < across).astype(f32), axis=0, keepdims=True)
    slot_down = jnp.sum((across < down).astype(f32), axis=1, keepdims=True)
    local = (down.astype(jnp.int32) % row_total).astype(f32)
    count = -(-SPAN * share // 16) * 16
    latents = latents_ref[...]
    wanted = lax.broadcasted_iota(jnp.int32, (count, row_total), 0)
    spot_rows = -(-row_total // 128)
    lane = lax.broadcasted_iota(jnp.int32, (row_total, 128), 1)
    for receiver in range(wide_count):
        first = (receiver - REACH) * share
        chosen = (slot_across == (wanted + first).astype(f32)) & (wanted < SPAN * share)
        rows = jnp.dot(chosen.astype(bf16), latents, preferred_element_type=f32).astype(bf16)
        lines = []
        for line in range(spot_rows):
            place = lane + (line * 128 - at_ref[1])
            mine = (slot_down == (place + receiver * share).astype(f32)) & (
                (place >= 0) & (place < share)
            )
            lines.append(jnp.sum(jnp.where(mine, local, 0.0), axis=0, keepdims=True))
        lines.append(jnp.zeros((16 - spot_rows, 128), f32))
        spots = jnp.concatenate(lines, axis=0).astype(bf16)
        if sliced:
            out_refs[1][receiver, 0:16, :] = bias
            out_refs[1][receiver, 16 : 16 + count, :] = rows
            out_refs[1][receiver, 16 + count :, :] = spots
        else:
            out_refs[0][receiver, piece : piece + 16, :] = bias
            out_refs[0][receiver, piece + 16 : piece + 16 + count, :] = rows
            out_refs[0][receiver, piece + 16 + count :, :] = spots


def middle_kernel(piece, count, arrived_ref, spread_ref, near_ref, bias_ref):
    senders = arrived_ref.shape[0]
    row_total = (near_ref.shape[0] - 16) // SPAN
    share = row_total // senders
    total = arrived_ref[0, 0:piece].astype(f32)
    for sender in range(1, senders):
        total = total + arrived_ref[sender, 0:piece].astype(f32)
    total = total.astype(bf16)
    for receiver in range(senders):
        spread_ref[receiver] = total
    bias = arrived_ref[0, piece : piece + 16].astype(f32)
    spots = arrived_ref[0, piece + 16 + count :].astype(f32)
    for sender in range(1, senders):
        bias = bias + arrived_ref[sender, piece : piece + 16].astype(f32)
        spots = spots + arrived_ref[sender, piece + 16 + count :].astype(f32)
    bias_ref[...] = bias
    near_ref[SPAN * row_total :, :] = spots.astype(bf16)
    for tile in range(SPAN):
        for sender in range(senders):
            near_ref[pl.ds(tile * row_total + sender * share, share), :] = arrived_ref[
                sender, pl.ds(piece + 16 + tile * share, share), :
            ]


def project_kernel(
    row_total,
    tile_size,
    order_ref,
    weight_ref,
    bias_ref,
    gram_ref,
    *rest,
):
    patches_refs = rest[:-4]
    keys_ref, values_ref, twin_ref, both_ref = rest[-4:]
    heads_width = keys_ref.shape[0]
    local_heads = heads_width // HEAD
    pairs = heads_width // 128
    chunks = heads_width // 128

    def doubled(part):
        weight = weight_ref[part * heads_width : (part + 1) * heads_width, :]
        return jnp.concatenate([weight, weight], axis=1)

    def centred_bias(part):
        same = lax.broadcasted_iota(jnp.int32, (128, 128), 0) == lax.broadcasted_iota(
            jnp.int32, (128, 128), 1
        )
        pieces = []
        for chunk in range(chunks):
            row = bias_ref[part * chunks + chunk : part * chunks + chunk + 1, :]
            pieces.append(jnp.sum(jnp.where(same, row, 0.0), axis=1, keepdims=True))
        grouped = jnp.concatenate(pieces, axis=0).reshape(local_heads, HEAD, 1)
        grouped = grouped - jnp.mean(grouped, axis=1, keepdims=True)
        return grouped.reshape(heads_width, 1)

    def unit_heads(turned, bias):
        grouped = (turned + bias).reshape(local_heads, HEAD, turned.shape[1])
        square = jnp.mean(grouped * grouped, axis=1, keepdims=True)
        return (grouped * lax.rsqrt(square + EPSILON)).reshape(turned.shape)

    gram_top = jnp.concatenate([gram_ref[0], gram_ref[1]], axis=0)
    gram_low = gram_ref[2]

    for block, patches_ref in enumerate(patches_refs):
        place = order_ref[block] * row_total

        def scale(tile, carry, patches_ref=patches_ref, place=place):
            rows = patches_ref[pl.ds(pl.multiple_of(tile * row_total, row_total), row_total), :]
            wide_rows = rows.astype(f32)
            image = jnp.dot(
                jnp.concatenate([rows, rows], axis=1), gram_top, preferred_element_type=f32
            ) + jnp.dot(rows, gram_low, preferred_element_type=f32)
            variance = jnp.sum(image * wide_rows, axis=1, keepdims=True)
            scaled = wide_rows * lax.rsqrt(jnp.maximum(variance, 0.0) + EPSILON)
            high = scaled.astype(bf16)
            at = pl.multiple_of(tile * tile_size + place, row_total)
            both_ref[pl.ds(at, row_total), 0:128] = high
            both_ref[pl.ds(at, row_total), 128:256] = (scaled - high.astype(f32)).astype(bf16)
            return carry

        lax.fori_loop(0, SPAN, scale, 0, unroll=SPAN)

    key_bias = centred_bias(1)
    key_weight = doubled(1)
    value_weight = doubled(2).astype(f32).T.astype(bf16)
    value_bias = jnp.concatenate(
        [bias_ref[2 * chunks + chunk : 2 * chunks + chunk + 1, :] for chunk in range(chunks)], axis=1
    )

    def project(step, carry):
        at = pl.multiple_of(step * 256, 256)
        both = both_ref[pl.ds(at, 256), :]
        keys_ref[:, pl.ds(at, 256)] = unit_heads(ntdot(key_weight, both), key_bias).astype(bf16)
        values_ref[pl.ds(at, 256), :] = (
            jnp.dot(both, value_weight, preferred_element_type=f32) + value_bias
        ).astype(bf16)
        return carry

    lax.fori_loop(0, SPAN * tile_size // 256, project, 0, unroll=2)

    query_bias = centred_bias(0)
    query_weight = doubled(0)
    left = lax.broadcasted_iota(jnp.int32, (QB, 128), 1) < HEAD
    spot_rows = row_total // 128

    for block, patches_ref in enumerate(patches_refs):
        place = order_ref[block] * row_total
        spots = jnp.concatenate(
            [
                patches_ref[SPAN * row_total + row : SPAN * row_total + row + 1, :]
                for row in range(spot_rows)
            ],
            axis=1,
        )
        wanted = lax.broadcasted_iota(jnp.int32, (row_total, row_total), 0).astype(f32)
        chosen = (spots.astype(f32) == wanted).astype(bf16)
        both = both_ref[pl.ds(pl.multiple_of(REACH * tile_size + place, row_total), row_total), :]
        placed = jnp.dot(chosen, both, preferred_element_type=f32).astype(bf16)
        turned = unit_heads(ntdot(query_weight, placed), query_bias).astype(bf16).astype(f32) * 0.125
        rows = turned.T.astype(bf16)
        for part in range(row_total // QB):
            query = order_ref[block] * (row_total // QB) + part
            for pair in range(pairs):
                piece = rows[part * QB : (part + 1) * QB, pair * 128 : (pair + 1) * 128]
                twin_ref[query, pair, 0:QB, :] = jnp.where(left, piece, jnp.zeros_like(piece))
                twin_ref[query, pair, QB : 2 * QB, :] = jnp.where(left, jnp.zeros_like(piece), piece)


def attend_kernel(
    parts, entries, order_ref, starts_ref, counts_ref, keys_ref, values_ref, twin_ref, *rest
):
    out_refs = rest[:-6]
    total_ref, even_ref, odd_ref, block_ref, query_ref, first_ref = rest[-6:]
    pairs = twin_ref.shape[1]
    left = lax.broadcasted_iota(jnp.int32, (QB, 128), 1) < HEAD

    steps = jnp.int32(0)
    for index, (away, part) in enumerate(entries):
        total_ref[index] = jnp.zeros_like(total_ref[index])
        block = (order_ref[0] ^ away) * parts + part

        def note(slot, at, index=index, block=block):
            block_ref[at] = index
            query_ref[at] = block
            first_ref[at] = starts_ref[block * NB + slot]
            return at + 1

        steps = lax.fori_loop(0, counts_ref[block], note, steps)
    for extra in range(2):
        block_ref[steps + extra] = len(entries)
        query_ref[steps + extra] = query_ref[0]
        first_ref[steps + extra] = first_ref[0]

    ones = jnp.ones((KB, 128), bf16)

    def weigh(step, weights_ref):
        start = pl.multiple_of(first_ref[step], KB)
        query = query_ref[step]
        for pair in range(pairs):
            scores = jnp.dot(
                twin_ref[query, pair],
                keys_ref[pair * 128 : (pair + 1) * 128, pl.ds(start, KB)],
                preferred_element_type=f32,
            )
            weights_ref[pair] = jnp.exp(scores).astype(bf16)

    def gather(step, weights_ref):
        start = pl.multiple_of(first_ref[step], KB)
        block = block_ref[step]
        for pair in range(pairs):
            side = jnp.concatenate(
                [values_ref[pl.ds(start, KB), pair * 128 : (pair + 1) * 128], ones], axis=1
            )
            total_ref[block, pair] += jnp.dot(weights_ref[pair], side, preferred_element_type=f32)

    weigh(0, even_ref)

    def visit(twice, carry):
        step = twice * 2
        weigh(step + 1, odd_ref)
        gather(step, even_ref)
        weigh(step + 2, even_ref)
        gather(step + 1, odd_ref)
        return carry

    lax.fori_loop(0, (steps + 1) // 2, visit, 0)

    for index in range(len(entries)):
        for pair in range(pairs):
            both = total_ref[index, pair, :, 0:128] / total_ref[index, pair, :, 128:256]
            out_refs[index][:, pair * 128 : (pair + 1) * 128] = jnp.where(
                left, both[0:QB], both[QB : 2 * QB]
            ).astype(bf16)


def attend_scratch(entries, heads_width):
    pairs = heads_width // 128
    return [
        pltpu.VMEM((entries + 1, pairs, 2 * QB, 256), f32),
        pltpu.VMEM((pairs, 2 * QB, KB), bf16),
        pltpu.VMEM((pairs, 2 * QB, KB), bf16),
        pltpu.SMEM((entries * NB + 2,), jnp.int32),
        pltpu.SMEM((entries * NB + 2,), jnp.int32),
        pltpu.SMEM((entries * NB + 2,), jnp.int32),
    ]


def output_kernel(parts, narrow_count, together, order_ref, *refs):
    attended_refs = refs[: parts * narrow_count]
    weight_ref, gate_ref, out_ref = refs[parts * narrow_count :]
    rows = out_ref.shape[1] // together
    totals = [None] * together
    for away in range(narrow_count):
        attended = jnp.concatenate(
            [attended_refs[chunk * narrow_count + away][...] for chunk in range(parts)], axis=0
        )
        for index in range(together):
            at = pl.multiple_of((index * narrow_count + (order_ref[0] ^ away)) * rows, 16)
            term = ntdot(attended, weight_ref[pl.ds(at, rows), :])
            totals[index] = term if away == 0 else totals[index] + term
    for index, total in enumerate(totals):
        columns = slice(index * rows, (index + 1) * rows)
        out_ref[:, columns] = (total * gate_ref[:, columns]).astype(bf16)


def partial_kernel(kept, sent, held_ref, *refs):
    total = kept + sent
    outs = (kept > 0) + (sent > 0)
    attended_refs = refs[:total]
    weight_refs = refs[total:-outs]
    rows = weight_refs[0].shape[0]
    for index, weight_ref in enumerate(weight_refs):

        @pl.when(held_ref[index] >= 0)
        def _(index=index, weight_ref=weight_ref):
            attended = jnp.concatenate([ref[...] for ref in attended_refs], axis=0)
            product = ntdot(attended, weight_ref[...])
            columns = pl.ds(pl.multiple_of(held_ref[index] * rows, 128), rows)
            if kept:
                refs[-outs][:, columns] = product[: kept * QB]
            if sent:
                refs[-1][:, columns] = product[kept * QB :].astype(bf16)


def final_kernel(own_ref, first_ref, second_ref, third_ref, gate_ref, out_ref):
    far = jnp.concatenate([second_ref[...], third_ref[...]], axis=0).astype(f32)
    total = own_ref[...] + first_ref[...].astype(f32) + far
    out_ref[...] = (total * gate_ref[...]).astype(bf16)


def flip(block, axis, bit):
    devices = range(lax.axis_size(axis))
    return lax.ppermute(block, axis, [(i, i ^ bit) for i in devices])


def cost(flops, moved):
    return pl.CostEstimate(flops=flops, bytes_accessed=moved, transcendentals=0)


def gathered_rows(own):
    count = lax.axis_size("wide")
    index = lax.axis_index("wide")
    length = count // 2
    blocks, held = [own], [index]

    def add(array, source, route):
        valid = (source >= 0) & (source < count)
        other = lax.ppermute(array, "wide", route)
        blocks.extend([array, other])
        held.extend([jnp.where(valid, source, -1), jnp.where(valid, source ^ 1, -1)])

    blocks.append(lax.ppermute(own, "wide", [(i, i ^ 1) for i in range(count)]))
    held.append(index ^ 1)

    def reached(step, move):
        return [i for i in range(count) if 0 <= i - move * step < count]

    def sent(step, move):
        return [(i - move, i) for i in reached(step, move)]

    forward, backward, single = own, own, None
    for step in range(1, length):
        apart = not set(reached(step, 2)) & set(reached(step, -2))
        if single is None:
            forward = lax.ppermute(forward, "wide", sent(step, 2))
            backward = lax.ppermute(backward, "wide", sent(step, -2))
        else:
            single = lax.ppermute(single, "wide", sent(step, 2) + sent(step, -2))
        if not apart:
            for array, move in ((forward, 2), (backward, -2)):
                swap = [(i, i ^ 1) for i in reached(step, move)]
                add(array, index - move * step, swap)
            continue
        ahead = index - 2 * step >= 0
        if single is None:
            single = jnp.where(ahead, forward, backward)
        source = jnp.where(ahead, index - 2 * step, index + 2 * step)
        swap = [(i, i ^ 1) for i in reached(step, 2) + reached(step, -2)]
        add(single, source, swap)
    return blocks, jnp.stack(held).astype(jnp.int32)


def block(
    latents,
    targets,
    embed_weight,
    mod_shift,
    mod_scale,
    qkv_weight,
    out_weight,
    mod_gate,
    block_list,
    block_count,
):
    row_total, patch = latents.shape
    width = embed_weight.shape[1]
    wide_count = lax.axis_size("wide")
    narrow_count = lax.axis_size("narrow")
    wide_index = lax.axis_index("wide")
    narrow_index = lax.axis_index("narrow")
    tile_size = row_total * narrow_count
    depth, heads_width = qkv_weight.shape[1:]
    share = row_total // wide_count
    count = -(-SPAN * share // 16) * 16
    piece = 3 * heads_width // wide_count

    small = pltpu.CompilerParams(vmem_limit_bytes=SMALL_VMEM)
    chained = narrow_count == 4 and out_weight.shape[0] % 128 == 0 and row_total == 2 * QB
    if chained:
        blocks, held = gathered_rows(out_weight)
    else:
        out_all = lax.all_gather(out_weight, ("wide", "narrow"), axis=0, tiled=True)

    first = wide_index * depth
    extra = 16 + count + 16
    sliced = depth % 128 != 0 or piece % 16 != 0
    scale = mod_scale.reshape(1, width)
    shift = mod_shift.reshape(1, width)
    own = embed_weight
    if sliced:
        own, scale, shift = (
            lax.dynamic_slice_in_dim(array, first, depth, 1) for array in (own, scale, shift)
        )
        prep_shapes = (
            jax.ShapeDtypeStruct((3 * heads_width, patch), bf16),
            jax.ShapeDtypeStruct((wide_count, extra, patch), bf16),
        )
    else:
        prep_shapes = (jax.ShapeDtypeStruct((wide_count, piece + extra, patch), bf16),)
    smem = pl.BlockSpec(memory_space=pltpu.SMEM)
    prepare = pl.pallas_call(
        functools.partial(prep_kernel, wide_count, sliced),
        out_shape=prep_shapes,
        in_specs=[smem] + [whole_spec()] * 7,
        out_specs=tuple(whole_spec() for _ in prep_shapes),
        cost_estimate=cost(1 << 28, 4 << 20),
        name="prep",
    )
    prepared = prepare(
        jnp.stack([first, wide_index * share]).astype(jnp.int32),
        embed_weight,
        own,
        scale,
        shift,
        qkv_weight,
        latents,
        targets.reshape(1, row_total),
    )
    payload = prepared[0]
    if sliced:
        payload = jnp.concatenate(
            [payload.reshape(wide_count, piece, patch), prepared[1]], axis=1
        )
    gram = pl.pallas_call(
        gram_kernel,
        out_shape=jax.ShapeDtypeStruct((3, patch, patch), bf16),
        in_specs=[whole_spec()],
        out_specs=whole_spec(),
        compiler_params=small,
        name="gram",
    )(embed_weight)
    arrived = lax.all_to_all(payload, "wide", split_axis=0, concat_axis=0, tiled=True)

    near_rows = SPAN * row_total + 16
    if share % 16 == 0 and piece % 16 == 0:
        spread, near, bias = pl.pallas_call(
            functools.partial(middle_kernel, piece, count),
            out_shape=(
                jax.ShapeDtypeStruct((wide_count, piece, patch), bf16),
                jax.ShapeDtypeStruct((near_rows, patch), bf16),
                jax.ShapeDtypeStruct((16, 128), f32),
            ),
            in_specs=[whole_spec()],
            out_specs=(whole_spec(),) * 3,
            name="middle",
        )(arrived)
    else:
        summed = jnp.sum(arrived[:, :piece].astype(f32), axis=0).astype(bf16)
        bias = jnp.sum(arrived[:, piece : piece + 16].astype(f32), axis=0)
        spread = jnp.broadcast_to(summed[None], (wide_count,) + summed.shape)
        near = arrived[:, piece + 16 : piece + 16 + SPAN * share]
        near = near.reshape(wide_count, SPAN, share, patch).transpose(1, 0, 2, 3)
        spots = jnp.sum(arrived[:, piece + 16 + count :].astype(f32), axis=0).astype(bf16)
        near = jnp.concatenate([near.reshape(SPAN * row_total, patch), spots], axis=0)
    group, order = [near], [0]
    bits = [1 << k for k in range(1, narrow_count.bit_length() - 1)] + [1]
    for bit in bits:
        others = []
        for rows in group:
            others.append(flip(rows, "narrow", bit))
        group = group + others
        order = order + [index ^ bit for index in order]
    everything = lax.all_to_all(spread, "wide", split_axis=0, concat_axis=0, tiled=True)
    weight_all = everything.reshape(3 * heads_width, patch)

    order_ids = jnp.bitwise_xor(jnp.array(order, jnp.int32), narrow_index)
    starts = (block_list * KB - (wide_index - REACH) * tile_size).reshape(-1)
    parts = row_total // QB
    pairs = heads_width // 128
    keys, values, twin = pl.pallas_call(
        functools.partial(project_kernel, row_total, tile_size),
        out_shape=(
            pltpu.VMEM((heads_width, SPAN * tile_size), bf16),
            pltpu.VMEM((SPAN * tile_size, heads_width), bf16),
            pltpu.VMEM((tile_size // QB, pairs, 2 * QB, 128), bf16),
        ),
        in_specs=[smem] + [whole_spec()] * (3 + narrow_count),
        out_specs=(whole_spec(),) * 3,
        scratch_shapes=[pltpu.VMEM((SPAN * tile_size, 256), bf16)],
        compiler_params=pltpu.CompilerParams(vmem_limit_bytes=PROJECT_VMEM),
        cost_estimate=cost(10 * SPAN * tile_size * patch * heads_width, 16 << 20),
        name="project",
    )(order_ids, weight_all, bias, gram, *group)

    def attend(entries):
        return pl.pallas_call(
            functools.partial(attend_kernel, parts, entries),
            out_shape=(jax.ShapeDtypeStruct((QB, heads_width), bf16),) * len(entries),
            in_specs=[smem] * 3 + [whole_spec()] * 3,
            out_specs=(whole_spec(),) * len(entries),
            scratch_shapes=attend_scratch(len(entries), heads_width),
            compiler_params=pltpu.CompilerParams(vmem_limit_bytes=ATTEND_VMEM),
            cost_estimate=cost(4 * QB * len(entries) * NB * KB * heads_width, 16 << 20),
        )(order_ids, starts, block_count, keys, values, twin)

    if chained:
        gate = mod_gate.reshape(1, width)

        def multiply(attended, kept):
            sent = len(attended) - kept
            shapes = []
            if kept:
                shapes.append(jax.ShapeDtypeStruct((kept * QB, width), f32))
            if sent:
                shapes.append(jax.ShapeDtypeStruct((sent * QB, width), bf16))
            return pl.pallas_call(
                functools.partial(partial_kernel, kept, sent),
                out_shape=tuple(shapes),
                in_specs=[smem] + [whole_spec()] * (len(attended) + len(blocks)),
                out_specs=(whole_spec(),) * len(shapes),
                compiler_params=small,
                cost_estimate=cost(2 * len(attended) * QB * heads_width * width, 8 << 20),
            )(held, *attended, *blocks)

        far = []
        for part in range(parts):
            attended = attend(((2, part), (3, part)))
            keep, send = multiply(attended, 1)
            other = flip(send, "narrow", 1)
            joined = (keep + other.astype(f32)).astype(bf16)
            far.append(flip(joined, "narrow", 2))
        (send,) = multiply(attend(((1, 0), (1, 1))), 0)
        other = flip(send, "narrow", 1)
        (own,) = multiply(attend(((0, 0), (0, 1))), parts)
        return pl.pallas_call(
            final_kernel,
            out_shape=jax.ShapeDtypeStruct((row_total, width), bf16),
            in_specs=[whole_spec()] * 5,
            out_specs=whole_spec(),
            compiler_params=small,
            name="final",
        )(own, other, *far, gate)

    pieces = []
    for chunk in range(parts):
        mine = attend(tuple((away, chunk) for away in range(narrow_count)))
        pieces.append(mine[0])
        for away in range(1, narrow_count):
            pieces.append(flip(mine[away], "narrow", away))

    out_rows = out_weight.shape[0]
    gate = mod_gate.reshape(1, width)
    if out_rows % 128 == 0:
        together = 2 if wide_count % 2 == 0 else 1
        span = together * out_rows
        return pl.pallas_call(
            functools.partial(output_kernel, parts, narrow_count, together),
            grid=(wide_count // together,),
            out_shape=jax.ShapeDtypeStruct((row_total, width), bf16),
            in_specs=[smem]
            + [pl.BlockSpec((QB, heads_width), lambda i: (0, 0))] * (parts * narrow_count)
            + [
                pl.BlockSpec((narrow_count * span, heads_width), lambda i: (i, 0)),
                pl.BlockSpec((1, span), lambda i: (0, i)),
            ],
            out_specs=pl.BlockSpec((row_total, span), lambda i: (0, i)),
            compiler_params=pltpu.CompilerParams(vmem_limit_bytes=OUTPUT_VMEM),
            name="output",
        )(order_ids, *pieces, out_all, gate)
    weights = out_all.reshape(wide_count, narrow_count, out_rows, heads_width)
    product = 0.0
    for away in range(narrow_count):
        attended = jnp.concatenate(pieces[away::narrow_count], axis=0)
        weight = lax.dynamic_index_in_dim(weights, narrow_index ^ away, 1, False)
        product = product + jnp.einsum(
            "tk,wfk->twf", attended, weight, preferred_element_type=f32
        )
    return (gate * product.reshape(row_total, width)).astype(bf16)


def solution(mesh):
    in_specs = (
        P(("wide", "narrow"), None),
        P(("wide", "narrow")),
        P(),
        P(),
        P(),
        P(None, "wide", "narrow"),
        P("wide", "narrow"),
        P(),
        P("wide", None),
        P("wide"),
    )
    out_specs = P(("wide", "narrow"), None)
    return jax.shard_map(block, mesh=mesh, in_specs=in_specs, out_specs=out_specs, check_vma=False)
```
